32 devices in a mesh: ctx: 16 (over z, x, core), tp: 2 (over y).
Axes of the slice: x: 2, y: 2, z: 4, core: 2. Of those that a mesh axis runs over, the one named last changes fastest.
Arguments:
- layer_input: bfloat16 [8192, 5376], P('ctx', 'tp'), may hold values from -60 to 60
- norm_weight: bfloat16 [5376], P('tp'), may hold values from 0.099609375 to 1.8984375
- document_index: int32 [8192], P('ctx'), may hold values from 0 to 3, never falling along the last dimension, each value on 1 to 4096 neighbouring positions
- stored_queries: bfloat16 [8192, 4096], P('ctx', 'tp'), may hold values from -6 to 6
- stored_keys: bfloat16 [8192, 2048], P('ctx', 'tp'), may hold values from -6 to 6
- stored_values: bfloat16 [8192, 2048], P('ctx', 'tp'), may hold values from -6 to 6
- output_weight: bfloat16 [4096, 5376], P(None, 'tp'), may hold values from -0.1500248 to 0.1500248
- projection_gradient: bfloat16 [8192, 5376], P('ctx', 'tp'), may hold values from -600 to 600
- adapter_down_maps: bfloat16 [5376, 24], P('tp'), may hold values from -0.078125 to 0.078125
Outputs:
- feature_q: float32 [8, 4096], P(None, 'tp')
- feature_k: float32 [8, 2048], P(None, 'tp')
- feature_v: float32 [8, 2048], P(None, 'tp')
The draws below stay inside these ranges and needn't reach their ends.
Inputs may be any that keep to these rules, and one draw needn't show every extreme that they name: `document_index`: document numbers never fall along the sequence; every document is one run of positions.
All inputs are finite; a program needn't handle non-finite values.
Results may differ from the reference program's by a relative error of at most 0.0095.
Values may be sent and summed in bfloat16 or wider, within the bound.
No kernel may reach another device: no remote copies, remote signals or barrier semaphores. Data moves between devices by JAX's collectives and lax.ppermute only.
A program may use at most 192 MiB of HBM per device.

```python
import math
import jax
import jax.numpy as jnp
import numpy as np
from jax import lax

MODEL_WIDTH = 5376
QUERY_HEADS = 32
KEY_VALUE_HEADS = 16
HEAD_SIZE = 128
LOOKBACK_SPAN = 1024
ADAPTER_RANK = 8
TOK_DEV = 512
SEQUENCE_TOKENS = 8192
DOCS = 4


def paired_states(key):
    base = jax.random.fold_in(key, 11)
    key_query, key_random_seeds = jax.random.split(base, 2)
    query_draw = jax.random.normal(key_query, (SEQUENCE_TOKENS, QUERY_HEADS * HEAD_SIZE), jnp.float32)
    key_sample = jax.random.normal(key_random_seeds, (SEQUENCE_TOKENS, KEY_VALUE_HEADS * HEAD_SIZE), jnp.float32)
    return (jnp.clip(query_draw, -6.0, 6.0), jnp.clip(key_sample, -6.0, 6.0))


def draw_stored_queries(key, part):
    return paired_states(key)[0].astype(jnp.bfloat16)


def draw_stored_keys(key, part):
    return paired_states(key)[1].astype(jnp.bfloat16)


def draw_layer_input(key, part):
    key_main, key_cols = jax.random.split(jax.random.fold_in(key, 31), 2)
    col_scale = jnp.exp(jax.random.uniform(key_cols, (1, MODEL_WIDTH), jnp.float32, 0.0, math.log(10.0)))
    values = jax.random.normal(key_main, (SEQUENCE_TOKENS, MODEL_WIDTH), jnp.float32)
    return (jnp.clip(values, -6.0, 6.0) * col_scale).astype(jnp.bfloat16)


def draw_projection_gradient(key, part):
    key_main, key_rows, key_cols = jax.random.split(jax.random.fold_in(key, 23), 3)
    along = jnp.arange(SEQUENCE_TOKENS, dtype=jnp.float32) / max(SEQUENCE_TOKENS - 1, 1)
    row_scale = jnp.exp(jax.random.uniform(key_rows, (SEQUENCE_TOKENS, 1), jnp.float32, 0.0, math.log(10.0)))
    col_scale = jnp.exp(jax.random.uniform(key_cols, (1, MODEL_WIDTH), jnp.float32, 0.0, math.log(10.0)))
    rising = jnp.exp(math.log(3.0) * along)[:, None]
    values = jax.random.normal(key_main, (SEQUENCE_TOKENS, MODEL_WIDTH), jnp.float32)
    return (jnp.clip(values, -6.0, 6.0) * rising * row_scale * col_scale / 10.0).astype(jnp.bfloat16)


def draw_output_weight(key, part):
    key_main = jax.random.fold_in(key, 41)
    along = jnp.arange(QUERY_HEADS * HEAD_SIZE, dtype=jnp.float32) / (QUERY_HEADS * HEAD_SIZE - 1) - 0.5
    rising = jnp.exp(math.log(3.0) * along)[:, None]
    values = jax.random.normal(key_main, (QUERY_HEADS * HEAD_SIZE, MODEL_WIDTH), jnp.float32)
    return (jnp.clip(values, -6.0, 6.0) * rising * float(MODEL_WIDTH) ** (-0.5)).astype(jnp.bfloat16)


def levels(own_key, extent, cuts, low, top_value):
    loudness, own = 1.0, jax.random.fold_in(own_key, 6)
    for axis_at, shards_of in cuts:
        draws = jnp.exp(jax.random.uniform(jax.random.fold_in(own, axis_at), (shards_of,), jnp.float32, low / len(cuts), top_value / len(cuts)))
        loudness = loudness * jnp.repeat(draws, extent[axis_at] // shards_of).reshape([-1 if axis == axis_at else 1 for axis in range(len(extent))])
    return loudness


def profile(number_of, total, reach, lean):
    weights = [(1 << 20) // math.isqrt(standing ** lean) + 1 for standing in range(2, number_of + 1)]
    surplus, given = total - reach - (number_of - 1), [1] * (number_of - 1)
    while surplus > 0:
        movable = [i for i in range(number_of - 1) if given[i] < reach]
        pool, remaining = sum([weights[i] for i in movable]), surplus
        for i in movable:
            extra = min(reach - given[i], max(1, remaining * weights[i] // pool), surplus)
            given[i] = given[i] + extra
            surplus = surplus - extra
    return np.array([reach] + given)


def uneven_parts(own_key, amount, total, bound, skew):
    if amount == 2:
        one = jax.random.randint(own_key, (), max(1, total - bound), min(bound, total - 1) + 1)
        return jnp.stack([one, total - one])
    sizes = jnp.asarray(profile(amount, total, bound, skew), jnp.int32)
    pairs = (amount - 1) // 2
    source_of, receiver = sizes[1:1 + 2 * pairs:2], sizes[2:2 + 2 * pairs:2]
    slack = jnp.minimum(source_of - 1, bound - receiver)
    moved = jax.random.randint(jax.random.fold_in(own_key, 1), (pairs,), 0, 1 << 20) % (slack + 1)
    sizes = sizes.at[1:1 + 2 * pairs:2].set(source_of - moved).at[2:2 + 2 * pairs:2].set(receiver + moved)
    return sizes[jax.random.permutation(jax.random.fold_in(own_key, 2), amount)]


def scatter_about(own_key, shape, spread, bound, cuts=(), kind=jnp.bfloat16):
    drawn = spread * jax.random.normal(own_key, shape, jnp.float32)
    if cuts:
        drawn = drawn * levels(own_key, shape, cuts, -0.22, 0.18)
    return jnp.clip(drawn, -bound, bound).astype(kind)


def setup_inputs(seed: int = 0) -> dict:
    splits = jax.random.split(jax.random.key(seed), 10)
    return {
        "layer_input": draw_layer_input(jax.random.fold_in(splits[9], 71), 0),
        "norm_weight": jnp.clip(1.0 + 0.18 * jax.random.normal(splits[1], (MODEL_WIDTH,), jnp.float32), 0.099609375, 1.8984375).astype(jnp.bfloat16),
        "document_index": jnp.searchsorted(jnp.cumsum(uneven_parts(splits[2], DOCS, SEQUENCE_TOKENS, SEQUENCE_TOKENS // 2, 2)), jnp.arange(SEQUENCE_TOKENS), side="right").astype(jnp.int32),
        "stored_queries": draw_stored_queries(jax.random.fold_in(splits[9], 71), 0),
        "stored_keys": draw_stored_keys(jax.random.fold_in(splits[9], 71), 0),
        "stored_values": scatter_about(splits[5], (SEQUENCE_TOKENS, KEY_VALUE_HEADS * HEAD_SIZE), 1.0, 6.0, ((0, 16), (1, 2))),
        "output_weight": draw_output_weight(jax.random.fold_in(splits[9], 71), 0),
        "projection_gradient": draw_projection_gradient(jax.random.fold_in(splits[9], 71), 0),
        "adapter_down_maps": scatter_about(splits[8], (MODEL_WIDTH, 3 * ADAPTER_RANK), MODEL_WIDTH ** -0.5, 0.078125, ((0, 2),)),
    }


def attend_block(query_block, key_block, value_block, gradient_block, allowed, softmax_scale):
    query_wide = query_block.astype(jnp.float32)
    key_wide = key_block.astype(jnp.float32)
    value_wide = value_block.astype(jnp.float32)
    grad_wide = gradient_block.astype(jnp.float32)
    scores = jnp.einsum('sgrd,kgd->grsk', query_wide, key_wide) * softmax_scale
    scores = jnp.where(allowed[None, None], scores, -1e+30)
    highest = lax.optimization_barrier(jnp.max(scores, axis=-1, keepdims=True))
    expons = jnp.exp(scores - highest)
    probs = expons / lax.optimization_barrier(jnp.sum(expons, axis=-1, keepdims=True))
    probs_low = probs.astype(jnp.bfloat16).astype(jnp.float32)
    attended = jnp.einsum('grsk,kgd->sgrd', probs_low, value_wide)
    delta = jnp.einsum('sgrd,sgrd->grs', grad_wide, attended)
    grad_probs = jnp.einsum('sgrd,kgd->grsk', grad_wide, value_wide)
    grad_scores = (probs * (grad_probs - delta[..., None]) * softmax_scale).astype(jnp.bfloat16).astype(jnp.float32)
    query_gradient = jnp.einsum('grsk,kgd->sgrd', grad_scores, key_wide)
    key_gradient = jnp.einsum('grsk,sgrd->kgd', grad_scores, query_wide)
    value_gradient = jnp.einsum('grsk,sgrd->kgd', probs_low, grad_wide)
    return (query_gradient, key_gradient, value_gradient)

def reference(layer_input, norm_weight, document_index, stored_queries, stored_keys, stored_values, output_weight, projection_gradient, adapter_down_maps):
    hidden_wide = layer_input.astype(jnp.float32)
    normalized_input = (hidden_wide * lax.rsqrt(lax.optimization_barrier(jnp.mean(hidden_wide * hidden_wide, axis=-1, keepdims=True)) + 1e-06) * norm_weight.astype(jnp.float32)).astype(jnp.bfloat16)
    reduced_rank = jnp.dot(normalized_input, adapter_down_maps, preferred_element_type=jnp.float32).astype(jnp.bfloat16)
    output_gradient = jnp.dot(projection_gradient, output_weight.T, preferred_element_type=jnp.float32).astype(jnp.bfloat16)
    overall_rows = stored_queries.shape[0]
    query_groups = QUERY_HEADS // KEY_VALUE_HEADS
    rows_per_block = TOK_DEV
    window_rows = rows_per_block + LOOKBACK_SPAN
    key_padded = jnp.concatenate([jnp.zeros((LOOKBACK_SPAN, KEY_VALUE_HEADS * HEAD_SIZE), stored_keys.dtype), stored_keys], 0)
    value_padded = jnp.concatenate([jnp.zeros((LOOKBACK_SPAN, KEY_VALUE_HEADS * HEAD_SIZE), stored_values.dtype), stored_values], 0)
    id_pad = jnp.concatenate([jnp.full((LOOKBACK_SPAN,), -1, jnp.int32), document_index.astype(jnp.int32)], 0)
    softmax_scale = float(MODEL_WIDTH // QUERY_HEADS) ** (-0.5)

    def one_block(carry, block_index):
        key_gradient_total, value_gradient_total = carry
        start_offset = (block_index * rows_per_block).astype(jnp.int32)
        query_block = lax.dynamic_slice_in_dim(stored_queries, start_offset, rows_per_block, 0).reshape(rows_per_block, KEY_VALUE_HEADS, query_groups, HEAD_SIZE)
        gradient_block = lax.dynamic_slice_in_dim(output_gradient, start_offset, rows_per_block, 0).reshape(rows_per_block, KEY_VALUE_HEADS, query_groups, HEAD_SIZE)
        key_block = lax.dynamic_slice_in_dim(key_padded, start_offset, window_rows, 0).reshape(window_rows, KEY_VALUE_HEADS, HEAD_SIZE)
        value_block = lax.dynamic_slice_in_dim(value_padded, start_offset, window_rows, 0).reshape(window_rows, KEY_VALUE_HEADS, HEAD_SIZE)
        query_ids = lax.dynamic_slice_in_dim(document_index.astype(jnp.int32), start_offset, rows_per_block, 0)
        key_ids = lax.dynamic_slice_in_dim(id_pad, start_offset, window_rows, 0)
        query_pos = start_offset + jnp.arange(rows_per_block, dtype=jnp.int32)
        key_pos = start_offset - LOOKBACK_SPAN + jnp.arange(window_rows, dtype=jnp.int32)
        spacing = query_pos[:, None] - key_pos[None, :]
        allowed = (spacing >= 0) & (spacing < LOOKBACK_SPAN) & (query_ids[:, None] == key_ids[None, :])
        query_gradient, key_gradient, value_gradient = attend_block(query_block, key_block, value_block, gradient_block, allowed, softmax_scale)
        key_previous = lax.dynamic_slice_in_dim(key_gradient_total, start_offset, window_rows, 0)
        key_gradient_total = lax.dynamic_update_slice_in_dim(key_gradient_total, key_previous + key_gradient.reshape(window_rows, KEY_VALUE_HEADS * HEAD_SIZE), start_offset, 0)
        value_previous = lax.dynamic_slice_in_dim(value_gradient_total, start_offset, window_rows, 0)
        value_gradient_total = lax.dynamic_update_slice_in_dim(value_gradient_total, value_previous + value_gradient.reshape(window_rows, KEY_VALUE_HEADS * HEAD_SIZE), start_offset, 0)
        return ((key_gradient_total, value_gradient_total), query_gradient.reshape(rows_per_block, QUERY_HEADS * HEAD_SIZE).astype(jnp.bfloat16))
    blank_block = jnp.zeros((overall_rows + LOOKBACK_SPAN, KEY_VALUE_HEADS * HEAD_SIZE), jnp.float32)
    (key_gradient_total, value_gradient_total), query_grads = lax.scan(one_block, (blank_block, blank_block), jnp.arange(overall_rows // rows_per_block, dtype=jnp.int32))
    query_gradient = query_grads.reshape(overall_rows, QUERY_HEADS * HEAD_SIZE)
    key_gradient = key_gradient_total[LOOKBACK_SPAN:].astype(jnp.bfloat16)
    value_gradient = value_gradient_total[LOOKBACK_SPAN:].astype(jnp.bfloat16)
    adapter_query = jnp.dot(reduced_rank[:, 0:ADAPTER_RANK].T, query_gradient, preferred_element_type=jnp.float32)
    adapter_key = jnp.dot(reduced_rank[:, ADAPTER_RANK:2 * ADAPTER_RANK].T, key_gradient, preferred_element_type=jnp.float32)
    adapter_value = jnp.dot(reduced_rank[:, 2 * ADAPTER_RANK:3 * ADAPTER_RANK].T, value_gradient, preferred_element_type=jnp.float32)
    grand_total = jnp.sum(adapter_query * adapter_query) + jnp.sum(adapter_key * adapter_key) + jnp.sum(adapter_value * adapter_value)
    scale_factor = jnp.sqrt(float(ADAPTER_RANK * (QUERY_HEADS + 2 * KEY_VALUE_HEADS) * HEAD_SIZE) / (grand_total + 1e-06))
    return (adapter_query * scale_factor, adapter_key * scale_factor, adapter_value * scale_factor)
```

```python
import functools

import jax
import jax.numpy as jnp
from jax import lax
from jax.experimental import pallas as pl
from jax.experimental.pallas import tpu as pltpu
from jax.sharding import PartitionSpec as P

MODEL_WIDTH = 5376
QUERY_HEADS = 32
KEY_VALUE_HEADS = 16
HEAD_SIZE = 128
LOOKBACK_SPAN = 1024
ADAPTER_RANK = 8
LOG2E = 1.4426950408889634
SCALE = float(MODEL_WIDTH // QUERY_HEADS) ** (-0.5)
LANES = 128
COL_K, COL_V, COL_ONE, COL_DOC, COL_Q = 0, ADAPTER_RANK, 2 * ADAPTER_RANK, 17, 3 * ADAPTER_RANK

NT = (((1,), (1,)), ((), ()))
NN = (((1,), (0,)), ((), ()))
TN = (((0,), (0,)), ((), ()))


def dotf(left, right, dims):
    return lax.dot_general(left, right, dims, preferred_element_type=jnp.float32)


def shifted(value, axis, steps):
    count = lax.axis_size(axis)
    first, last = (max(0, -steps), min(count, count - steps))
    return lax.ppermute(value, axis, [(source, source + steps) for source in range(first, last)])


def xor_sum(value, axis):
    count = lax.axis_size(axis)
    step = 1
    while step < count:
        value = value + lax.ppermute(value, axis, [(at, at ^ step) for at in range(count)])
        step *= 2
    return value


def project_body(offset_ref, gradient_ref, weight_ref, out_ref):
    out_ref[...] = dotf(gradient_ref[...], weight_ref[...], NT).astype(out_ref.dtype)


def project(gradient, weight, first_block, blocks, width, dtype):
    rows, depth = gradient.shape
    return pl.pallas_call(
        project_body,
        grid_spec=pltpu.PrefetchScalarGridSpec(
            num_scalar_prefetch=1,
            grid=(blocks,),
            in_specs=[
                pl.BlockSpec((rows, depth), lambda i, off: (0, 0)),
                pl.BlockSpec((width, depth), lambda i, off: (off[0] + i, 0)),
            ],
            out_specs=pl.BlockSpec((rows, width), lambda i, off: (0, i)),
        ),
        out_shape=jax.ShapeDtypeStruct((rows, blocks * width), dtype),
        cost_estimate=pl.CostEstimate(
            flops=2 * rows * depth * width * blocks,
            bytes_accessed=2 * (rows * depth + width * blocks * depth + rows * width * blocks),
            transcendentals=0,
        ),
        compiler_params=pltpu.CompilerParams(vmem_limit_bytes=40 << 20),
    )(first_block, gradient, weight)


def attend_body(
    q_ref, own_ref, recv_ref, k0, k1, k2, v0, v1, v2, x0, x1, x2, st_ref, out_ref, s_scr, e_scr, lq_scr
):
    rows = q_ref.shape[0]
    tile = s_scr.shape[1] // 2
    width = 256 if rows % 256 == 0 else rows
    step = s_scr.shape[2]
    factor = SCALE * LOG2E

    @pl.when(pl.program_id(0) == 0)
    def _():
        lq_scr[...] = x2[...].astype(jnp.float32).T.astype(jnp.bfloat16)

    def window(refs, at):
        block, inside = at // rows, at % rows
        return refs[block][inside : inside + width, :]

    sum_q = sum_k = sum_v = None
    for t in range(rows // tile):
        r0 = t * tile
        q = jnp.concatenate([q_ref[r0 : r0 + tile, 0:LANES], q_ref[r0 : r0 + tile, LANES:]], 0)
        do = (own_ref[r0 : r0 + tile, :] + recv_ref[r0 : r0 + tile, :].astype(jnp.float32)).astype(jnp.bfloat16)
        do = jnp.concatenate([do[:, 0:LANES], do[:, LANES:]], 0)
        st = st_ref[r0 : r0 + tile, :]
        st = jnp.concatenate([st, st], 0)
        tiles = step // width
        top = None
        for j in range(tiles):
            at = r0 + j * width
            s = dotf(q, window((k0, k1, k2), at), NT)
            pos = lax.broadcasted_iota(jnp.int32, s.shape, 1) + at
            ok = pos >= st
            if at + width > LOOKBACK_SPAN + r0:
                row = lax.broadcasted_iota(jnp.int32, s.shape, 0)
                row = jnp.where(row >= tile, row - tile, row)
                ok = ok & (pos <= row + (LOOKBACK_SPAN + r0))
            s = jnp.where(ok, s, -1e30)
            s_scr[t % s_scr.shape[0], :, j * width : (j + 1) * width] = s
            peak = jnp.max(s, axis=1, keepdims=True)
            top = peak if top is None else jnp.maximum(top, peak)
        acc = None
        for j in range(tiles):
            at = r0 + j * width
            cols = slice(j * width, (j + 1) * width)
            e = jnp.exp2((s_scr[t % s_scr.shape[0], :, cols] - top) * factor).astype(jnp.bfloat16)
            e_scr[t % e_scr.shape[0], :, cols] = e
            rhs = jnp.concatenate([window((v0, v1, v2), at), window((x0, x1, x2), at)], 1)
            part = dotf(e, rhs, NN)
            acc = part if acc is None else acc + part
        inverse = 1.0 / acc[:, LANES + COL_ONE : LANES + COL_ONE + 1]
        delta = jnp.sum(do.astype(jnp.float32) * acc[:, :LANES], axis=1, keepdims=True) * inverse
        uv = (acc[:, LANES:] * inverse).astype(jnp.bfloat16)
        acc = None
        for j in range(tiles):
            at = r0 + j * width
            cols = slice(j * width, (j + 1) * width)
            dp = dotf(do, window((v0, v1, v2), at), NT)
            e = e_scr[t % e_scr.shape[0], :, cols].astype(jnp.float32)
            ds = (e * (dp - delta)).astype(jnp.bfloat16)
            rhs = jnp.concatenate([window((k0, k1, k2), at), window((x0, x1, x2), at)], 1)
            part = dotf(ds, rhs, NN)
            acc = part if acc is None else acc + part
        fin = (acc * (inverse * SCALE)).astype(jnp.bfloat16)
        dq = jnp.concatenate([fin[:tile, :LANES], fin[tile:, :LANES]], 1)
        part_q = dotf(lq_scr[2 * ADAPTER_RANK : 4 * ADAPTER_RANK, r0 : r0 + tile], dq, NN)
        part_k = dotf(fin[:, LANES:], q, TN)
        part_v = dotf(uv, do, TN)
        sum_q = part_q if sum_q is None else sum_q + part_q
        sum_k = part_k if sum_k is None else sum_k + part_k
        sum_v = part_v if sum_v is None else sum_v + part_v
    out_ref[:, 0 : 2 * LANES] = sum_q[ADAPTER_RANK:]
    out_ref[:, 2 * LANES : 3 * LANES] = sum_k[COL_K : COL_K + ADAPTER_RANK]
    out_ref[:, 3 * LANES : 4 * LANES] = sum_v[COL_V : COL_V + ADAPTER_RANK]


def attend(queries, own, recv, packs, tables, starts, groups, first_group):
    rows = queries.shape[0]
    tile = 256 if rows % 256 == 0 else rows
    keys = LOOKBACK_SPAN + tile
    col = lambda width, fn: pl.BlockSpec((rows, width), fn)
    pushes = rows * groups * 2 * keys // 256 * 4
    return pl.pallas_call(
        attend_body,
        grid=(groups,),
        in_specs=[
            col(2 * LANES, lambda g: (0, g + first_group)),
            col(2 * LANES, lambda g: (0, g)),
            col(2 * LANES, lambda g: (0, g)),
        ]
        + [col(LANES, lambda g: (0, g))] * 3
        + [col(LANES, lambda g: (0, groups + g))] * 3
        + [col(LANES, lambda g: (0, 0))] * 3
        + [col(1, lambda g: (0, 0))],
        out_specs=pl.BlockSpec((ADAPTER_RANK, 4 * LANES), lambda g: (0, g)),
        out_shape=jax.ShapeDtypeStruct((ADAPTER_RANK, 4 * LANES * groups), jnp.float32),
        scratch_shapes=[
            pltpu.VMEM((1, 2 * tile, keys), jnp.float32),
            pltpu.VMEM((1, 2 * tile, keys), jnp.bfloat16),
            pltpu.VMEM((LANES, rows), jnp.bfloat16),
        ],
        cost_estimate=pl.CostEstimate(
            flops=pushes * 256 * 256 * 2,
            bytes_accessed=groups * rows * LANES * 30,
            transcendentals=rows * groups * 2 * keys,
        ),
        compiler_params=pltpu.CompilerParams(vmem_limit_bytes=56 << 20),
    )(queries, own, recv, *packs, *packs, *tables, starts)


def finish_body(sum_ref, total_ref, q_ref, k_ref, v_ref):
    scale = jnp.sqrt(
        float(ADAPTER_RANK * (QUERY_HEADS + 2 * KEY_VALUE_HEADS) * HEAD_SIZE) / (total_ref[0:1, 0:1] + 1e-06)
    )
    for g in range(k_ref.shape[1] // LANES):
        at = 4 * LANES * g
        q_ref[:, 2 * LANES * g : 2 * LANES * (g + 1)] = sum_ref[:, at : at + 2 * LANES] * scale
        k_ref[:, LANES * g : LANES * (g + 1)] = sum_ref[:, at + 2 * LANES : at + 3 * LANES] * scale
        v_ref[:, LANES * g : LANES * (g + 1)] = sum_ref[:, at + 3 * LANES : at + 4 * LANES] * scale


def per_device(
    layer_input,
    norm_weight,
    document_index,
    stored_queries,
    stored_keys,
    stored_values,
    output_weight,
    projection_gradient,
    adapter_down_maps,
):
    rows = stored_queries.shape[0]
    heads_width = stored_queries.shape[1]
    groups = stored_keys.shape[1] // HEAD_SIZE
    tp = lax.axis_size("tp")
    tp_at = lax.axis_index("tp")
    ctx_at = lax.axis_index("ctx")
    chunks = 2 if groups % 2 == 0 else 1
    per = groups // chunks
    wide = per * HEAD_SIZE

    second = (ctx_at % 2) == 1
    packs = []
    for c in range(chunks):
        own = jnp.concatenate(
            [stored_keys[:, c * wide : (c + 1) * wide], stored_values[:, c * wide : (c + 1) * wide]], 1
        )
        packs.append([own, shifted(own, "ctx", 2)])

    hidden = layer_input.astype(jnp.float32)
    squares = jnp.sum(hidden * hidden, axis=-1, keepdims=True)
    weighted = (hidden * norm_weight.astype(jnp.float32)[None, :]).astype(jnp.bfloat16)
    reduced = jnp.dot(weighted, adapter_down_maps, preferred_element_type=jnp.float32)
    joined = xor_sum(jnp.concatenate([reduced, squares], 1), "tp")
    inverse = lax.rsqrt(joined[:, 3 * ADAPTER_RANK :] / float(MODEL_WIDTH) + 1e-06)
    low = (joined[:, : 3 * ADAPTER_RANK] * inverse).astype(jnp.bfloat16)
    table = jnp.concatenate(
        [
            low[:, ADAPTER_RANK:],
            jnp.ones((rows, 1), jnp.bfloat16),
            document_index.astype(jnp.bfloat16)[:, None],
            jnp.zeros((rows, 6), jnp.bfloat16),
            low[:, :ADAPTER_RANK],
            jnp.zeros((rows, LANES - 4 * ADAPTER_RANK), jnp.bfloat16),
        ],
        1,
    )
    tables = [shifted(table, "ctx", 2), shifted(table, "ctx", 1), table]

    before = jnp.concatenate([tables[0][:, COL_DOC], tables[1][:, COL_DOC]], 0).astype(jnp.int32)
    ids = jnp.concatenate([before, document_index], 0)
    doc_start = jnp.sum((ids[None, :] < document_index[:, None]).astype(jnp.int32), axis=1)
    starts = jnp.maximum(doc_start, 1 + jnp.arange(rows, dtype=jnp.int32))
    starts = jnp.maximum(starts, LOOKBACK_SPAN - ctx_at * rows)[:, None]

    width = 256
    half = heads_width // width
    per_blocks = half // chunks
    owns, recvs = [], []
    for c in range(chunks):
        got = []
        for d in range(1, tp):
            peer = (tp_at + d) % tp
            first = (peer * half + c * per_blocks).astype(jnp.int32).reshape(1)
            part = project(projection_gradient, output_weight, first, per_blocks, width, jnp.bfloat16)
            got.append(lax.ppermute(part, "tp", [(at, (at + d) % tp) for at in range(tp)]))
        recvs.append(got)
    for c in range(chunks):
        first = (tp_at * half + c * per_blocks).astype(jnp.int32).reshape(1)
        owns.append(project(projection_gradient, output_weight, first, per_blocks, width, jnp.float32))

    pieces = []
    for c in range(chunks):
        own, far = packs[c]
        near = lax.ppermute(
            jnp.where(second, far, own), "ctx", [(at, at ^ 1) for at in range(lax.axis_size("ctx"))]
        )
        base = owns[c]
        for extra in recvs[c][:-1]:
            base = base + extra.astype(jnp.float32)
        pieces.append(
            attend(stored_queries, base, recvs[c][-1], (far, near, own), tables, starts, per, c * per)
        )
    summed = xor_sum(jnp.concatenate(pieces, 1), "ctx")
    total = xor_sum(jnp.sum(summed * summed).reshape(1, 1), "tp")
    sizes = (heads_width, groups * HEAD_SIZE, groups * HEAD_SIZE)
    return pl.pallas_call(
        finish_body,
        out_shape=[jax.ShapeDtypeStruct((ADAPTER_RANK, size), jnp.float32) for size in sizes],
    )(summed, total)


def solution(mesh):
    placed = (
        P("ctx", "tp"),
        P("tp"),
        P("ctx"),
        P("ctx", "tp"),
        P("ctx", "tp"),
        P("ctx", "tp"),
        P(None, "tp"),
        P("ctx", "tp"),
        P("tp", None),
    )
    return jax.shard_map(
        per_device,
        mesh=mesh,
        in_specs=placed,
        out_specs=(P(None, "tp"), P(None, "tp"), P(None, "tp")),
        check_vma=False,
    )
```

```python
import functools

import jax
import jax.numpy as jnp
from jax import lax
from jax.experimental import pallas as pl
from jax.experimental.pallas import tpu as pltpu
from jax.sharding import PartitionSpec as P

MODEL_WIDTH = 5376
QUERY_HEADS = 32
KEY_VALUE_HEADS = 16
HEAD_SIZE = 128
LOOKBACK_SPAN = 1024
ADAPTER_RANK = 8
LOG2E = 1.4426950408889634
SCALE = float(MODEL_WIDTH // QUERY_HEADS) ** (-0.5)
LANES = 128
ROW_K, ROW_V, ROW_ONE, ROW_DOC, ROW_Q = 0, ADAPTER_RANK, 2 * ADAPTER_RANK, 2 * ADAPTER_RANK + 1, 3 * ADAPTER_RANK
TABLE = 4 * ADAPTER_RANK

NT = (((1,), (1,)), ((), ()))
NN = (((1,), (0,)), ((), ()))
TN = (((0,), (0,)), ((), ()))


def dotf(left, right, dims):
    return lax.dot_general(left, right, dims, preferred_element_type=jnp.float32)


def shifted(value, axis, steps):
    count = lax.axis_size(axis)
    first, last = (max(0, -steps), min(count, count - steps))
    return lax.ppermute(value, axis, [(source, source + steps) for source in range(first, last)])


def xor_move(value, axis, step):
    return lax.ppermute(value, axis, [(at, at ^ step) for at in range(lax.axis_size(axis))])


def project_body(offset_ref, gradient_ref, weight_ref, out_ref):
    out_ref[...] = dotf(gradient_ref[...], weight_ref[...], NT).astype(out_ref.dtype)


def project(gradient, weight, first_block, blocks, width):
    rows, depth = gradient.shape
    return pl.pallas_call(
        project_body,
        grid_spec=pltpu.PrefetchScalarGridSpec(
            num_scalar_prefetch=1,
            grid=(blocks,),
            in_specs=[
                pl.BlockSpec((rows, depth), lambda i, off: (0, 0)),
                pl.BlockSpec((width, depth), lambda i, off: (off[0] + i, 0)),
            ],
            out_specs=pl.BlockSpec((rows, width), lambda i, off: (0, i)),
        ),
        out_shape=jax.ShapeDtypeStruct((rows, blocks * width), jnp.bfloat16),
        cost_estimate=pl.CostEstimate(
            flops=2 * rows * depth * width * blocks,
            bytes_accessed=2 * (rows * depth + width * blocks * depth + rows * width * blocks),
            transcendentals=0,
        ),
        compiler_params=pltpu.CompilerParams(vmem_limit_bytes=40 << 20),
    )(first_block, gradient, weight)


def open_body(chunks, offset_ref, gradient_ref, weight_ref, x_ref, norm_ref, down_ref, k_ref, v_ref, out_ref, low_ref, *packs):
    step = pl.program_id(0)
    out_ref[...] = dotf(gradient_ref[...], weight_ref[...], NT).astype(out_ref.dtype)
    hidden = x_ref[...].astype(jnp.float32)
    weighted = (hidden * norm_ref[...].astype(jnp.float32)).astype(jnp.bfloat16)
    low_ref[0 : 3 * ADAPTER_RANK, :] = dotf(down_ref[...], weighted, NT)
    ones = jnp.ones((ADAPTER_RANK, hidden.shape[1]), jnp.bfloat16)
    low_ref[3 * ADAPTER_RANK :, :] = dotf(ones, (hidden * hidden).astype(jnp.bfloat16), NT)
    wide = k_ref.shape[1]
    each = pl.num_programs(0) // chunks
    for c, pack_ref in enumerate(packs):

        @pl.when(step // each == c)
        def _(pack_ref=pack_ref):
            pack_ref[:, :wide] = k_ref[...]
            pack_ref[:, wide:] = v_ref[...]


def open_call(gradient, weight, first_block, blocks, width, x, norm, down, keys, values, chunks):
    rows, depth = gradient.shape
    slab = rows // blocks
    wide = keys.shape[1] // blocks
    each = blocks // chunks
    pack_specs = [
        pl.BlockSpec((rows, 2 * wide), lambda i, off, c=c: (0, jnp.clip(i - c * each, 0, each - 1)))
        for c in range(chunks)
    ]
    pack_shape = jax.ShapeDtypeStruct((rows, 2 * wide * each), keys.dtype)
    return pl.pallas_call(
        functools.partial(open_body, chunks),
        grid_spec=pltpu.PrefetchScalarGridSpec(
            num_scalar_prefetch=1,
            grid=(blocks,),
            in_specs=[
                pl.BlockSpec((rows, depth), lambda i, off: (0, 0)),
                pl.BlockSpec((width, depth), lambda i, off: (off[0] + i, 0)),
                pl.BlockSpec((slab, depth), lambda i, off: (i, 0)),
                pl.BlockSpec((1, depth), lambda i, off: (0, 0)),
                pl.BlockSpec((3 * ADAPTER_RANK, depth), lambda i, off: (0, 0)),
                pl.BlockSpec((rows, wide), lambda i, off: (0, i)),
                pl.BlockSpec((rows, wide), lambda i, off: (0, i)),
            ],
            out_specs=[
                pl.BlockSpec((rows, width), lambda i, off: (0, i)),
                pl.BlockSpec((TABLE, slab), lambda i, off: (0, i)),
            ]
            + pack_specs,
        ),
        out_shape=[
            jax.ShapeDtypeStruct((rows, blocks * width), jnp.bfloat16),
            jax.ShapeDtypeStruct((TABLE, rows), jnp.float32),
        ]
        + [pack_shape] * chunks,
        cost_estimate=pl.CostEstimate(
            flops=2 * rows * depth * width * blocks,
            bytes_accessed=2 * (2 * rows * depth + width * blocks * depth + rows * width * blocks),
            transcendentals=0,
        ),
        compiler_params=pltpu.CompilerParams(vmem_limit_bytes=40 << 20),
    )(first_block, gradient, weight, x, norm, down, keys, values)


def table_body(mine_ref, theirs_ref, doc_ref, out_ref):
    joined = mine_ref[...] + theirs_ref[...]
    inverse = lax.rsqrt(joined[3 * ADAPTER_RANK : 3 * ADAPTER_RANK + 1] / float(MODEL_WIDTH) + 1e-06)
    low = joined * inverse
    rank = ADAPTER_RANK
    row = lax.broadcasted_iota(jnp.int32, (rank, low.shape[1]), 0)
    extra = jnp.where(row == 0, 1.0, jnp.where(row == 1, doc_ref[...].astype(jnp.float32), 0.0))
    out_ref[...] = jnp.concatenate([low[rank : 3 * rank], extra, low[:rank]], 0).astype(out_ref.dtype)


def prep_body(first_ref, t2_ref, t1_ref, t0_ref, ext_ref, st_ref):
    rows = t0_ref.shape[1]
    tables = [ref[...].astype(jnp.float32) for ref in (t2_ref, t1_ref, t0_ref)]
    blank = jnp.zeros((LANES - TABLE, rows), jnp.float32)
    for at, table in enumerate(tables):
        turned = jnp.concatenate([table, blank], 0).T
        ext_ref[at * rows : (at + 1) * rows, :] = turned.astype(ext_ref.dtype)
    ids = [table[ROW_DOC : ROW_DOC + 1] for table in tables]
    column = turned[:, ROW_DOC : ROW_DOC + 1]
    leading = column[0:1]
    before = sum(jnp.sum((one < leading).astype(jnp.float32), axis=1, keepdims=True) for one in ids[:2])
    inside = jnp.sum((ids[2] < column).astype(jnp.float32), axis=1, keepdims=True)
    begin = jnp.where(column > leading, inside + float(2 * rows), before).astype(jnp.int32)
    begin = jnp.broadcast_to(begin, st_ref.shape)
    band = lax.broadcasted_iota(jnp.int32, st_ref.shape, 0) + (2 * rows + 1 - LOOKBACK_SPAN)
    st_ref[...] = jnp.maximum(jnp.maximum(begin, band), first_ref[0])


def attend_body(
    steps, step_units, base, offset_ref, q_ref, pg_ref, w_ref, recv_ref, k0, k1, k2, v0, v1, v2, ext_ref, lq_ref, st_ref, *rest
):
    if base:
        before_ref, out_ref, s_scr, e_scr, ve, ke, do_scr = rest
    else:
        out_ref, s_scr, e_scr, ve, ke, do_scr = rest
    rows = pg_ref.shape[0]
    tile = s_scr.shape[1] // 2
    keys = s_scr.shape[2]
    width = tile
    factor = SCALE * LOG2E
    parts = rows // tile
    units = [(g, t) for g in range(step_units) for t in range(parts)]
    state = [{} for _ in units]
    columns = range(keys // width)
    step = pl.program_id(0)
    if base:

        @pl.when(step == 0)
        def _():
            out_ref[:, :base] = before_ref[...]

    def prepare(i):
        g, t = units[i]
        if t == 0:
            own = dotf(pg_ref[...], w_ref[2 * LANES * g : 2 * LANES * (g + 1), :], NT)
            got = recv_ref[:, 2 * LANES * g : 2 * LANES * (g + 1)].astype(jnp.float32)
            do_scr[g % 2] = (own + got).astype(jnp.bfloat16)
            for b, (k_ref, v_ref) in enumerate(((k0, v0), (k1, v1), (k2, v2))):
                span = slice(b * rows, (b + 1) * rows)
                ke[g % 2, span, :LANES] = k_ref[:, g * LANES : (g + 1) * LANES]
                ve[g % 2, span, :LANES] = v_ref[:, g * LANES : (g + 1) * LANES]
                ke[g % 2, span, LANES:] = ext_ref[span, :]
                ve[g % 2, span, LANES:] = ext_ref[span, :]
        s = state[i]
        r0 = t * tile
        c0 = 2 * LANES * g
        s["q"] = jnp.concatenate(
            [q_ref[r0 : r0 + tile, c0 : c0 + LANES], q_ref[r0 : r0 + tile, c0 + LANES : c0 + 2 * LANES]], 0
        )
        start = st_ref[r0 : r0 + tile, :]
        s["start"] = jnp.concatenate([start, start], 0)
        s["peak"] = None

    def score(i, j):
        g, t = units[i]
        s = state[i]
        at = t * tile + j * width
        raw = dotf(s["q"], ke[g % 2, at : at + width, :LANES], NT)
        for h in range(width // LANES):
            value = raw[:, h * LANES : (h + 1) * LANES]
            pos = lax.broadcasted_iota(jnp.int32, value.shape, 1) + (at + h * LANES)
            ok = pos >= s["start"]
            if j == len(columns) - 1:
                row = lax.broadcasted_iota(jnp.int32, value.shape, 0)
                row = jnp.where(row >= tile, row - tile, row)
                ok = ok & (pos <= row + (2 * rows + t * tile))
            value = jnp.where(ok, value, -1e30)
            s_scr[i % 2, :, j * width + h * LANES : j * width + (h + 1) * LANES] = value
            s["peak"] = value if s["peak"] is None else jnp.maximum(s["peak"], value)

    def weigh(i, j):
        g, t = units[i]
        s = state[i]
        at = t * tile + j * width
        cols = slice(j * width, (j + 1) * width)
        e = jnp.exp2((s_scr[i % 2, :, cols] - s["top"]) * factor).astype(jnp.bfloat16)
        e_scr[i % 2, :, cols] = e
        part = dotf(e, ve[g % 2, at : at + width, :], NN)
        s["acc"] = part if j == 0 else s["acc"] + part

    def weighed(i):
        g, t = units[i]
        s = state[i]
        acc = s["acc"]
        do = do_scr[g % 2, t * tile : (t + 1) * tile, :]
        s["do"] = jnp.concatenate([do[:, :LANES], do[:, LANES:]], 0)
        s["inverse"] = 1.0 / acc[:, LANES + ROW_ONE : LANES + ROW_ONE + 1]
        s["delta"] = (
            jnp.sum(s["do"].astype(jnp.float32) * acc[:, :LANES], axis=1, keepdims=True) * s["inverse"]
        )
        s["uv"] = (acc[:, LANES:] * s["inverse"]).astype(jnp.bfloat16)

    def back(i, j):
        g, t = units[i]
        s = state[i]
        at = t * tile + j * width
        dp = dotf(s["do"], ve[g % 2, at : at + width, :LANES], NT)
        e = e_scr[i % 2, :, j * width : (j + 1) * width].astype(jnp.float32)
        ds = (e * (dp - s["delta"])).astype(jnp.bfloat16)
        part = dotf(ds, ke[g % 2, at : at + width, :], NN)
        s["back"] = part if j == 0 else s["back"] + part

    def backed(i):
        g, t = units[i]
        s = state[i]
        fin = (s["back"] * (s["inverse"] * SCALE)).astype(jnp.bfloat16)
        dq = jnp.concatenate([fin[:tile, :LANES], fin[tile:, :LANES]], 1)
        low_q = lq_ref[2 * ADAPTER_RANK :, t * tile : (t + 1) * tile]
        out = (dotf(low_q, dq, NN), dotf(fin[:, LANES:], s["q"], TN), dotf(s["uv"], s["do"], TN))
        if t > 0:
            out = tuple(a + b for a, b in zip(out, state[i - 1]["out"]))
            state[i - 1].clear()
        s["out"] = out
        if t == parts - 1:
            for unit_step in range(steps):

                @pl.when(step == unit_step)
                def _():
                    at = base + 4 * LANES * (unit_step * step_units + g)
                    out_ref[:, at : at + 2 * LANES] = out[0][ADAPTER_RANK:]
                    out_ref[:, at + 2 * LANES : at + 3 * LANES] = out[1][ROW_K : ROW_K + ADAPTER_RANK]
                    out_ref[:, at + 3 * LANES : at + 4 * LANES] = out[2][ROW_V : ROW_V + ADAPTER_RANK]

    prepare(0)
    for j in columns:
        score(0, j)
    for i in range(len(units) + 1):
        if i < len(units):
            state[i]["top"] = jnp.max(state[i]["peak"], axis=1, keepdims=True)
        if i + 1 < len(units):
            prepare(i + 1)
        for j in columns:
            if i < len(units):
                weigh(i, j)
            if i + 1 < len(units):
                score(i + 1, j)
            if i > 0:
                back(i - 1, j)
        if i < len(units):
            weighed(i)
        if i > 0:
            backed(i - 1)


def attend(queries, gradient, weight, recv, packs, ext, table, starts, first, steps, units, before):
    rows, depth = gradient.shape
    tile = rows // 2
    keys = LOOKBACK_SPAN + tile
    base = 0 if before is None else before.shape[1]
    groups = steps * units
    col = lambda width, fn: pl.BlockSpec((rows, width), fn)
    total = base + 4 * LANES * groups
    wide = units * LANES
    operands = [queries, gradient, weight, recv, *packs, *packs, ext, table, starts]
    in_specs = (
        [
            col(2 * wide, lambda g, off: (0, g + off[1])),
            col(depth, lambda g, off: (0, 0)),
            pl.BlockSpec((2 * wide, depth), lambda g, off: (g + off[0], 0)),
            col(2 * wide, lambda g, off: (0, g)),
        ]
        + [col(wide, lambda g, off: (0, 2 * g))] * 3
        + [col(wide, lambda g, off: (0, 2 * g + 1))] * 3
        + [
            pl.BlockSpec((3 * rows, LANES), lambda g, off: (0, 0)),
            pl.BlockSpec((TABLE, rows), lambda g, off: (0, 0)),
            pl.BlockSpec((rows, LANES), lambda g, off: (0, 0)),
        ]
    )
    if base:
        operands.append(before)
        in_specs.append(pl.BlockSpec((ADAPTER_RANK, base), lambda g, off: (0, 0)))
    pushes = rows * groups * 2 * keys // 256 * 4
    return pl.pallas_call(
        functools.partial(attend_body, steps, units, base),
        grid_spec=pltpu.PrefetchScalarGridSpec(
            num_scalar_prefetch=1,
            grid=(steps,),
            in_specs=in_specs,
            out_specs=pl.BlockSpec((ADAPTER_RANK, total), lambda g, off: (0, 0)),
            scratch_shapes=[
                pltpu.VMEM((2, 2 * tile, keys), jnp.float32),
                pltpu.VMEM((2, 2 * tile, keys), jnp.bfloat16),
                pltpu.VMEM((2, 3 * rows, 2 * LANES), jnp.bfloat16),
                pltpu.VMEM((2, 3 * rows, 2 * LANES), jnp.bfloat16),
                pltpu.VMEM((2, rows, 2 * LANES), jnp.bfloat16),
            ],
        ),
        out_shape=jax.ShapeDtypeStruct((ADAPTER_RANK, total), jnp.float32),
        cost_estimate=pl.CostEstimate(
            flops=pushes * 256 * 256 * 2 + 2 * rows * depth * 2 * LANES * groups,
            bytes_accessed=groups * rows * LANES * 20 + 4 * LANES * groups * depth,
            transcendentals=rows * groups * 2 * keys,
        ),
        compiler_params=pltpu.CompilerParams(vmem_limit_bytes=56 << 20),
    )(first, *operands)


def finish_body(*refs):
    q_ref, k_ref, v_ref = refs[-3:]
    mine = refs[0][...].astype(jnp.float32) + refs[1][...].astype(jnp.float32)
    total = jnp.sum(mine * mine, keepdims=True)
    if len(refs) == 7:
        theirs = refs[2][...].astype(jnp.float32) + refs[3][...].astype(jnp.float32)
        total = total + jnp.sum(theirs * theirs, keepdims=True)
    else:
        total = refs[2][0:1, 0:1]
    count = float(ADAPTER_RANK * (QUERY_HEADS + 2 * KEY_VALUE_HEADS) * HEAD_SIZE)
    mine = mine * jnp.sqrt(count / (total + 1e-06))
    for g in range(k_ref.shape[1] // LANES):
        at = 4 * LANES * g
        q_ref[:, 2 * LANES * g : 2 * LANES * (g + 1)] = mine[:, at : at + 2 * LANES]
        k_ref[:, LANES * g : LANES * (g + 1)] = mine[:, at + 2 * LANES : at + 3 * LANES]
        v_ref[:, LANES * g : LANES * (g + 1)] = mine[:, at + 3 * LANES : at + 4 * LANES]


def per_device(
    layer_input,
    norm_weight,
    document_index,
    stored_queries,
    stored_keys,
    stored_values,
    output_weight,
    projection_gradient,
    adapter_down_maps,
):
    rows = stored_queries.shape[0]
    heads_width = stored_queries.shape[1]
    groups = stored_keys.shape[1] // HEAD_SIZE
    tp, ctx = lax.axis_size("tp"), lax.axis_size("ctx")
    tp_at, ctx_at = lax.axis_index("tp"), lax.axis_index("ctx")
    chunks = 2 if groups % 4 == 0 else 1
    units = chunks
    steps = groups // (chunks * units)
    width = 2 * LANES
    half = heads_width // width
    per = half // chunks
    as_scalars = lambda *values: jnp.stack([jnp.asarray(v, jnp.int32) for v in values])

    received = []
    for c in range(chunks):
        got = []
        for d in range(1, tp):
            first = as_scalars(((tp_at + d) % tp) * half + c * per)
            if c == 0 and d == 1:
                part, low, *packs = open_call(
                    projection_gradient,
                    output_weight,
                    first,
                    per,
                    width,
                    layer_input,
                    norm_weight[None, :],
                    adapter_down_maps.T,
                    stored_keys,
                    stored_values,
                    chunks,
                )
            else:
                part = project(projection_gradient, output_weight, first, per, width)
            got.append(lax.ppermute(part, "tp", [(at, (at + d) % tp) for at in range(tp)]))
        total = got[0]
        if len(got) > 1:
            total = sum(one.astype(jnp.float32) for one in got)
        received.append(total)

    move = 1
    while 2 * move < tp:
        low = low + xor_move(low, "tp", move)
        move *= 2
    table = pl.pallas_call(table_body, out_shape=jax.ShapeDtypeStruct((TABLE, rows), jnp.bfloat16))(
        low, xor_move(low, "tp", move), document_index[None, :]
    )
    ext, starts = pl.pallas_call(
        prep_body,
        grid_spec=pltpu.PrefetchScalarGridSpec(
            num_scalar_prefetch=1,
            grid=(1,),
            in_specs=[pl.BlockSpec((TABLE, rows), lambda i, off: (0, 0))] * 3,
            out_specs=[
                pl.BlockSpec((3 * rows, LANES), lambda i, off: (0, 0)),
                pl.BlockSpec((rows, LANES), lambda i, off: (0, 0)),
            ],
        ),
        out_shape=[
            jax.ShapeDtypeStruct((3 * rows, LANES), jnp.bfloat16),
            jax.ShapeDtypeStruct((rows, LANES), jnp.int32),
        ],
    )(as_scalars(2 * rows - ctx_at * rows), shifted(table, "ctx", 2), shifted(table, "ctx", 1), table)

    second = (ctx_at % 2) == 1
    sums = None
    for c in range(chunks):
        own = packs[c]
        far = shifted(own, "ctx", 2)
        near = xor_move(jnp.where(second, far, own), "ctx", 1)
        first = as_scalars((tp_at * half + c * per) // units, c * steps)
        sums = attend(
            stored_queries,
            projection_gradient,
            output_weight,
            received[c],
            (far, near, own),
            ext,
            table,
            starts,
            first,
            steps,
            units,
            sums,
        )

    order = [1] + [1 << at for at in range(2, ctx.bit_length() - 1)]
    sums = sums.astype(jnp.bfloat16)
    for move in order:
        sums = (sums.astype(jnp.float32) + xor_move(sums, "ctx", move).astype(jnp.float32)).astype(jnp.bfloat16)
    last = [sums, xor_move(sums, "ctx", 2)]
    if tp == 2:
        both = [(at, at ^ 5) for at in range(2 * ctx)]
        last = last + [xor_move(sums, "tp", 1), lax.ppermute(sums, ("ctx", "tp"), both)]
    else:
        squared = jnp.sum(jnp.square(last[0].astype(jnp.float32) + last[1].astype(jnp.float32))).reshape(1, 1)
        move = 1
        while move < tp:
            squared = squared + xor_move(squared, "tp", move)
            move *= 2
        last.append(squared)
    sizes = (heads_width, groups * HEAD_SIZE, groups * HEAD_SIZE)
    return pl.pallas_call(
        finish_body,
        out_shape=[jax.ShapeDtypeStruct((ADAPTER_RANK, size), jnp.float32) for size in sizes],
    )(*last)


def solution(mesh):
    placed = (
        P("ctx", "tp"),
        P("tp"),
        P("ctx"),
        P("ctx", "tp"),
        P("ctx", "tp"),
        P("ctx", "tp"),
        P(None, "tp"),
        P("ctx", "tp"),
        P("tp", None),
    )
    return jax.shard_map(
        per_device,
        mesh=mesh,
        in_specs=placed,
        out_specs=(P(None, "tp"), P(None, "tp"), P(None, "tp")),
        check_vma=False,
    )
```

```python
import functools

import jax
import jax.numpy as jnp
from jax import lax
from jax.experimental import pallas as pl
from jax.experimental.pallas import tpu as pltpu
from jax.sharding import PartitionSpec as P


MODEL_WIDTH = 5376
QUERY_HEADS = 32
KEY_VALUE_HEADS = 16
HEAD_SIZE = 128
LOOKBACK_SPAN = 1024
ADAPTER_RANK = 8
LOG2E = 1.4426950408889634
SCALE = float(MODEL_WIDTH // QUERY_HEADS) ** (-0.5)
LANES = 128
GRANT = 62 << 20
ROW_K, ROW_V, ROW_ONE, ROW_DOC = 0, ADAPTER_RANK, 2 * ADAPTER_RANK, 2 * ADAPTER_RANK + 1
TABLE = 4 * ADAPTER_RANK

NT = (((1,), (1,)), ((), ()))
NN = (((1,), (0,)), ((), ()))
TN = (((0,), (0,)), ((), ()))


def dotf(left, right, dims):
    return lax.dot_general(left, right, dims, preferred_element_type=jnp.float32)


def shifted(value, axis, steps):
    count = lax.axis_size(axis)
    first, last = (max(0, -steps), min(count, count - steps))
    return lax.ppermute(value, axis, [(source, source + steps) for source in range(first, last)])


def xor_move(value, axis, step):
    return lax.ppermute(value, axis, [(at, at ^ step) for at in range(lax.axis_size(axis))])


def project_body(offset_ref, gradient_ref, weight_ref, out_ref):
    out_ref[...] = dotf(gradient_ref[...], weight_ref[...], NT).astype(out_ref.dtype)


def project(gradient, weight, first_block, blocks, width):
    rows, depth = gradient.shape
    return pl.pallas_call(
        project_body,
        grid_spec=pltpu.PrefetchScalarGridSpec(
            num_scalar_prefetch=1,
            grid=(blocks,),
            in_specs=[
                pl.BlockSpec((rows, depth), lambda i, off: (0, 0)),
                pl.BlockSpec((width, depth), lambda i, off: (off[0] + i, 0)),
            ],
            out_specs=pl.BlockSpec((rows, width), lambda i, off: (0, i)),
        ),
        out_shape=jax.ShapeDtypeStruct((rows, blocks * width), jnp.bfloat16),
        cost_estimate=pl.CostEstimate(
            flops=2 * rows * depth * width * blocks,
            bytes_accessed=2 * (rows * depth + width * blocks * depth + rows * width * blocks),
            transcendentals=0,
        ),
        compiler_params=pltpu.CompilerParams(vmem_limit_bytes=GRANT),
    )(first_block, gradient, weight)


def open_body(chunks, offset_ref, gradient_ref, weight_ref, x_ref, down_ref, k_ref, v_ref, out_ref, low_ref, *packs):
    step = pl.program_id(0)
    out_ref[...] = dotf(gradient_ref[...], weight_ref[...], NT).astype(out_ref.dtype)
    low_ref[0 : 3 * ADAPTER_RANK, :] = dotf(down_ref[...], x_ref[...], NT)
    hidden = x_ref[...].astype(jnp.float32)
    ones = jnp.ones((ADAPTER_RANK, hidden.shape[1]), jnp.bfloat16)
    low_ref[3 * ADAPTER_RANK :, :] = dotf(ones, (hidden * hidden).astype(jnp.bfloat16), NT)
    wide = k_ref.shape[1]
    each = pl.num_programs(0) // chunks
    for c, pack_ref in enumerate(packs):

        @pl.when(step // each == c)
        def _(pack_ref=pack_ref):
            pack_ref[:, :wide] = k_ref[...]
            pack_ref[:, wide:] = v_ref[...]


def open_call(gradient, weight, first_block, blocks, width, x, down, keys, values, chunks):
    rows, depth = gradient.shape
    slab = rows // blocks
    wide = keys.shape[1] // blocks
    each = blocks // chunks
    pack_specs = [
        pl.BlockSpec((rows, 2 * wide), lambda i, off, c=c: (0, jnp.clip(i - c * each, 0, each - 1)))
        for c in range(chunks)
    ]
    pack_shape = jax.ShapeDtypeStruct((rows, 2 * wide * each), keys.dtype)
    return pl.pallas_call(
        functools.partial(open_body, chunks),
        grid_spec=pltpu.PrefetchScalarGridSpec(
            num_scalar_prefetch=1,
            grid=(blocks,),
            in_specs=[
                pl.BlockSpec((rows, depth), lambda i, off: (0, 0)),
                pl.BlockSpec((width, depth), lambda i, off: (off[0] + i, 0)),
                pl.BlockSpec((slab, depth), lambda i, off: (i, 0)),
                pl.BlockSpec((3 * ADAPTER_RANK, depth), lambda i, off: (0, 0)),
                pl.BlockSpec((rows, wide), lambda i, off: (0, i)),
                pl.BlockSpec((rows, wide), lambda i, off: (0, i)),
            ],
            out_specs=[
                pl.BlockSpec((rows, width), lambda i, off: (0, i)),
                pl.BlockSpec((TABLE, slab), lambda i, off: (0, i)),
            ]
            + pack_specs,
        ),
        out_shape=[
            jax.ShapeDtypeStruct((rows, blocks * width), jnp.bfloat16),
            jax.ShapeDtypeStruct((TABLE, rows), jnp.float32),
        ]
        + [pack_shape] * chunks,
        cost_estimate=pl.CostEstimate(
            flops=2 * rows * depth * width * blocks,
            bytes_accessed=2 * (2 * rows * depth + width * blocks * depth + rows * width * blocks),
            transcendentals=0,
        ),
        compiler_params=pltpu.CompilerParams(vmem_limit_bytes=GRANT),
    )(first_block, gradient, weight, x, down, keys, values)


def table_body(mine_ref, theirs_ref, doc_ref, out_ref):
    joined = mine_ref[...] + theirs_ref[...]
    inverse = lax.rsqrt(joined[3 * ADAPTER_RANK : 3 * ADAPTER_RANK + 1] / float(MODEL_WIDTH) + 1e-06)
    low = joined * inverse
    rank = ADAPTER_RANK
    row = lax.broadcasted_iota(jnp.int32, (rank, low.shape[1]), 0)
    extra = jnp.where(row == 0, 1.0, jnp.where(row == 1, doc_ref[...].astype(jnp.float32), 0.0))
    out_ref[...] = jnp.concatenate([low[rank : 3 * rank], extra, low[:rank]], 0).astype(out_ref.dtype)


def prep_body(first_ref, t2_ref, t1_ref, t0_ref, ext_ref, st_ref):
    rows = t0_ref.shape[1]
    tables = [ref[...].astype(jnp.float32) for ref in (t2_ref, t1_ref, t0_ref)]
    blank = jnp.zeros((LANES - TABLE, rows), jnp.float32)
    for at, table in enumerate(tables):
        turned = jnp.concatenate([table, blank], 0).T
        ext_ref[at * rows : (at + 1) * rows, :] = turned.astype(ext_ref.dtype)
    ids = [table[ROW_DOC : ROW_DOC + 1] for table in tables]
    column = turned[:, ROW_DOC : ROW_DOC + 1]
    leading = column[0:1]
    before = sum(jnp.sum((one < leading).astype(jnp.float32), axis=1, keepdims=True) for one in ids[:2])
    inside = jnp.sum((ids[2] < column).astype(jnp.float32), axis=1, keepdims=True)
    begin = jnp.where(column > leading, inside + float(2 * rows), before).astype(jnp.int32)
    begin = jnp.broadcast_to(begin, st_ref.shape)
    band = lax.broadcasted_iota(jnp.int32, st_ref.shape, 0) + (2 * rows + 1 - LOOKBACK_SPAN)
    st_ref[...] = jnp.maximum(jnp.maximum(begin, band), first_ref[0])


def attend_body(
    steps, step_units, base, offset_ref, q_ref, pg_ref, w_ref, recv_ref, k0, k1, k2, v0, v1, v2, ext_ref, lq_ref, st_ref, *rest
):
    if base:
        before_ref, out_ref, s_scr, e_scr, ve, ke, do_scr = rest
    else:
        out_ref, s_scr, e_scr, ve, ke, do_scr = rest
    rows = pg_ref.shape[0]
    tile = s_scr.shape[1] // 2
    keys = s_scr.shape[2]
    width = tile
    factor = SCALE * LOG2E
    parts = rows // tile
    units = [(g, t) for g in range(step_units) for t in range(parts)]
    state = [{} for _ in units]
    columns = range(keys // width)
    step = pl.program_id(0)
    if base:

        @pl.when(step == 0)
        def _():
            out_ref[:, :base] = before_ref[...]

    def prepare(i):
        g, t = units[i]
        if t == 0:
            own = dotf(pg_ref[...], w_ref[2 * LANES * g : 2 * LANES * (g + 1), :], NT)
            got = recv_ref[:, 2 * LANES * g : 2 * LANES * (g + 1)].astype(jnp.float32)
            do_scr[g % 2] = (own + got).astype(jnp.bfloat16)
            for b, (k_ref, v_ref) in enumerate(((k0, v0), (k1, v1), (k2, v2))):
                span = slice(b * rows, (b + 1) * rows)
                ke[g % 2, span, :LANES] = k_ref[:, g * LANES : (g + 1) * LANES]
                ve[g % 2, span, :LANES] = v_ref[:, g * LANES : (g + 1) * LANES]
                ke[g % 2, span, LANES:] = ext_ref[span, :]
                ve[g % 2, span, LANES:] = ext_ref[span, :]
        s = state[i]
        r0 = t * tile
        c0 = 2 * LANES * g
        s["q"] = jnp.concatenate(
            [q_ref[r0 : r0 + tile, c0 : c0 + LANES], q_ref[r0 : r0 + tile, c0 + LANES : c0 + 2 * LANES]], 0
        )
        start = st_ref[r0 : r0 + tile, :]
        s["start"] = jnp.concatenate([start, start], 0)
        s["peak"] = None

    def score(i, j):
        g, t = units[i]
        s = state[i]
        at = t * tile + j * width
        raw = dotf(s["q"], ke[g % 2, at : at + width, :LANES], NT)
        for h in range(width // LANES):
            value = raw[:, h * LANES : (h + 1) * LANES]
            pos = lax.broadcasted_iota(jnp.int32, value.shape, 1) + (at + h * LANES)
            ok = pos >= s["start"]
            if j == len(columns) - 1:
                row = lax.broadcasted_iota(jnp.int32, value.shape, 0)
                row = jnp.where(row >= tile, row - tile, row)
                ok = ok & (pos <= row + (2 * rows + t * tile))
            value = jnp.where(ok, value, -1e30)
            s_scr[i % 2, :, j * width + h * LANES : j * width + (h + 1) * LANES] = value
            s["peak"] = value if s["peak"] is None else jnp.maximum(s["peak"], value)

    def weigh(i, j):
        g, t = units[i]
        s = state[i]
        at = t * tile + j * width
        cols = slice(j * width, (j + 1) * width)
        e = jnp.exp2((s_scr[i % 2, :, cols] - s["top"]) * factor).astype(jnp.bfloat16)
        e_scr[i % 2, :, cols] = e
        part = dotf(e, ve[g % 2, at : at + width, :], NN)
        s["acc"] = part if j == 0 else s["acc"] + part

    def weighed(i):
        g, t = units[i]
        s = state[i]
        acc = s["acc"]
        do = do_scr[g % 2, t * tile : (t + 1) * tile, :]
        s["do"] = jnp.concatenate([do[:, :LANES], do[:, LANES:]], 0)
        s["inverse"] = 1.0 / acc[:, LANES + ROW_ONE : LANES + ROW_ONE + 1]
        s["delta"] = (
            jnp.sum(s["do"].astype(jnp.float32) * acc[:, :LANES], axis=1, keepdims=True) * s["inverse"]
        )
        s["uv"] = (acc[:, LANES:] * s["inverse"]).astype(jnp.bfloat16)

    def back(i, j):
        g, t = units[i]
        s = state[i]
        at = t * tile + j * width
        dp = dotf(s["do"], ve[g % 2, at : at + width, :LANES], NT)
        e = e_scr[i % 2, :, j * width : (j + 1) * width].astype(jnp.float32)
        ds = (e * (dp - s["delta"])).astype(jnp.bfloat16)
        part = dotf(ds, ke[g % 2, at : at + width, :], NN)
        s["back"] = part if j == 0 else s["back"] + part

    def backed(i):
        g, t = units[i]
        s = state[i]
        fin = (s["back"] * (s["inverse"] * SCALE)).astype(jnp.bfloat16)
        dq = jnp.concatenate([fin[:tile, :LANES], fin[tile:, :LANES]], 1)
        low_q = lq_ref[2 * ADAPTER_RANK :, t * tile : (t + 1) * tile]
        out = (dotf(low_q, dq, NN), dotf(fin[:, LANES:], s["q"], TN), dotf(s["uv"], s["do"], TN))
        if t > 0:
            out = tuple(a + b for a, b in zip(out, state[i - 1]["out"]))
            state[i - 1].clear()
        s["out"] = out
        if t == parts - 1:
            for unit_step in range(steps):

                @pl.when(step == unit_step)
                def _():
                    at = base + 4 * LANES * (unit_step * step_units + g)
                    out_ref[:, at : at + 2 * LANES] = out[0][ADAPTER_RANK:].astype(out_ref.dtype)
                    out_ref[:, at + 2 * LANES : at + 3 * LANES] = out[1][ROW_K : ROW_K + ADAPTER_RANK].astype(out_ref.dtype)
                    out_ref[:, at + 3 * LANES : at + 4 * LANES] = out[2][ROW_V : ROW_V + ADAPTER_RANK].astype(out_ref.dtype)

    prepare(0)
    for j in columns:
        score(0, j)
    for i in range(len(units) + 1):
        if i < len(units):
            state[i]["top"] = jnp.max(state[i]["peak"], axis=1, keepdims=True)
        if i + 1 < len(units):
            prepare(i + 1)
        for j in columns:
            if i < len(units):
                weigh(i, j)
            if i + 1 < len(units):
                score(i + 1, j)
            if i > 0:
                back(i - 1, j)
        if i < len(units):
            weighed(i)
        if i > 0:
            backed(i - 1)


def attend(queries, gradient, weight, recv, packs, ext, table, starts, first, skip, steps, units, before):
    rows, depth = gradient.shape
    tile = rows // 2
    keys = LOOKBACK_SPAN + tile
    base = 0 if before is None else before.shape[1]
    groups = steps * units
    col = lambda width, fn: pl.BlockSpec((rows, width), fn)
    total = base + 4 * LANES * groups
    wide = units * LANES
    operands = [queries, gradient, weight, recv, *packs, *packs, ext, table, starts]
    in_specs = (
        [
            col(2 * wide, lambda g, off: (0, g + skip)),
            col(depth, lambda g, off: (0, 0)),
            pl.BlockSpec((2 * wide, depth), lambda g, off: (g + off[0], 0)),
            col(2 * wide, lambda g, off: (0, g)),
        ]
        + [col(wide, lambda g, off: (0, 2 * g))] * 3
        + [col(wide, lambda g, off: (0, 2 * g + 1))] * 3
        + [
            pl.BlockSpec((3 * rows, LANES), lambda g, off: (0, 0)),
            pl.BlockSpec((TABLE, rows), lambda g, off: (0, 0)),
            pl.BlockSpec((rows, LANES), lambda g, off: (0, 0)),
        ]
    )
    if base:
        operands.append(before)
        in_specs.append(pl.BlockSpec((ADAPTER_RANK, base), lambda g, off: (0, 0)))
    pushes = rows * groups * 2 * keys // 256 * 4
    return pl.pallas_call(
        functools.partial(attend_body, steps, units, base),
        grid_spec=pltpu.PrefetchScalarGridSpec(
            num_scalar_prefetch=1,
            grid=(steps,),
            in_specs=in_specs,
            out_specs=pl.BlockSpec((ADAPTER_RANK, total), lambda g, off: (0, 0)),
            scratch_shapes=[
                pltpu.VMEM((2, 2 * tile, keys), jnp.float32),
                pltpu.VMEM((2, 2 * tile, keys), jnp.bfloat16),
                pltpu.VMEM((2, 3 * rows, 2 * LANES), jnp.bfloat16),
                pltpu.VMEM((2, 3 * rows, 2 * LANES), jnp.bfloat16),
                pltpu.VMEM((2, rows, 2 * LANES), jnp.bfloat16),
            ],
        ),
        out_shape=jax.ShapeDtypeStruct((ADAPTER_RANK, total), jnp.bfloat16),
        cost_estimate=pl.CostEstimate(
            flops=pushes * 256 * 256 * 2 + 2 * rows * depth * 2 * LANES * groups,
            bytes_accessed=groups * rows * LANES * 20 + 4 * LANES * groups * depth,
            transcendentals=rows * groups * 2 * keys,
        ),
        compiler_params=pltpu.CompilerParams(vmem_limit_bytes=GRANT),
    )(first, *operands)


def finish_body(*refs):
    q_ref, k_ref, v_ref = refs[-3:]
    mine = refs[0][...].astype(jnp.float32) + refs[1][...].astype(jnp.float32)
    total = jnp.sum(mine * mine, keepdims=True)
    if len(refs) == 7:
        theirs = refs[2][...].astype(jnp.float32) + refs[3][...].astype(jnp.float32)
        total = total + jnp.sum(theirs * theirs, keepdims=True)
    else:
        total = refs[2][0:1, 0:1]
    count = float(ADAPTER_RANK * (QUERY_HEADS + 2 * KEY_VALUE_HEADS) * HEAD_SIZE)
    mine = mine * jnp.sqrt(count / (total + 1e-06))
    for g in range(k_ref.shape[1] // LANES):
        at = 4 * LANES * g
        q_ref[:, 2 * LANES * g : 2 * LANES * (g + 1)] = mine[:, at : at + 2 * LANES]
        k_ref[:, LANES * g : LANES * (g + 1)] = mine[:, at + 2 * LANES : at + 3 * LANES]
        v_ref[:, LANES * g : LANES * (g + 1)] = mine[:, at + 3 * LANES : at + 4 * LANES]


def local(
    layer_input,
    norm_weight,
    document_index,
    stored_queries,
    stored_keys,
    stored_values,
    output_weight,
    projection_gradient,
    adapter_down_maps,
):
    rows = stored_queries.shape[0]
    heads_width = stored_queries.shape[1]
    groups = stored_keys.shape[1] // HEAD_SIZE
    tp, ctx = lax.axis_size("tp"), lax.axis_size("ctx")
    tp_at, ctx_at = lax.axis_index("tp"), lax.axis_index("ctx")
    chunks = 2 if groups % 4 == 0 else 1
    units = chunks
    steps = groups // (chunks * units)
    width = 2 * LANES
    half = heads_width // width
    per = half // chunks
    scalar = lambda value: jnp.asarray(value, jnp.int32).reshape(1)
    gain = norm_weight.astype(jnp.float32)[None, :]
    down = (adapter_down_maps.T.astype(jnp.float32) * gain).astype(jnp.bfloat16)

    received = []
    for c in range(chunks):
        got = []
        for d in range(1, tp):
            first = scalar(((tp_at + d) % tp) * half + c * per)
            if c == 0 and d == 1:
                part, low, *packs = open_call(
                    projection_gradient,
                    output_weight,
                    first,
                    per,
                    width,
                    layer_input,
                    down,
                    stored_keys,
                    stored_values,
                    chunks,
                )
            else:
                part = project(projection_gradient, output_weight, first, per, width)
            got.append(lax.ppermute(part, "tp", [(at, (at + d) % tp) for at in range(tp)]))
        total = got[0]
        if len(got) > 1:
            total = sum(one.astype(jnp.float32) for one in got)
        received.append(total)

    move = 1
    while 2 * move < tp:
        low = low + xor_move(low, "tp", move)
        move *= 2
    other = xor_move(low, "tp", move)
    table = pl.pallas_call(table_body, out_shape=jax.ShapeDtypeStruct((TABLE, rows), jnp.bfloat16))(
        low, other, document_index[None, :]
    )
    table2 = shifted(table, "ctx", 2)
    table1 = shifted(table, "ctx", 1)
    prepare = pl.pallas_call(
        prep_body,
        grid_spec=pltpu.PrefetchScalarGridSpec(
            num_scalar_prefetch=1,
            grid=(1,),
            in_specs=[pl.BlockSpec((TABLE, rows), lambda i, off: (0, 0))] * 3,
            out_specs=[
                pl.BlockSpec((3 * rows, LANES), lambda i, off: (0, 0)),
                pl.BlockSpec((rows, LANES), lambda i, off: (0, 0)),
            ],
        ),
        out_shape=[
            jax.ShapeDtypeStruct((3 * rows, LANES), jnp.bfloat16),
            jax.ShapeDtypeStruct((rows, LANES), jnp.int32),
        ],
    )
    ext, starts = prepare(scalar(2 * rows - ctx_at * rows), table2, table1, table)

    second = (ctx_at % 2) == 1
    sums = None
    for c in range(chunks):
        own = packs[c]
        far = shifted(own, "ctx", 2)
        near = xor_move(jnp.where(second, far, own), "ctx", 1)
        first = scalar((tp_at * half + c * per) // units)
        sums = attend(
            stored_queries,
            projection_gradient,
            output_weight,
            received[c],
            (far, near, own),
            ext,
            table,
            starts,
            first,
            c * steps,
            steps,
            units,
            sums,
        )

    order = [1] + [1 << at for at in range(2, ctx.bit_length() - 1)]
    for move in order:
        sums = (sums.astype(jnp.float32) + xor_move(sums, "ctx", move).astype(jnp.float32)).astype(jnp.bfloat16)
    last = [sums, xor_move(sums, "ctx", 2)]
    if tp == 2:
        both = [(at, at ^ 5) for at in range(2 * ctx)]
        last = last + [xor_move(sums, "tp", 1), lax.ppermute(sums, ("ctx", "tp"), both)]
    else:
        squared = jnp.sum(jnp.square(last[0].astype(jnp.float32) + last[1].astype(jnp.float32))).reshape(1, 1)
        move = 1
        while move < tp:
            squared = squared + xor_move(squared, "tp", move)
            move *= 2
        last.append(squared)
    sizes = (heads_width, groups * HEAD_SIZE, groups * HEAD_SIZE)
    return pl.pallas_call(
        finish_body,
        out_shape=[jax.ShapeDtypeStruct((ADAPTER_RANK, size), jnp.float32) for size in sizes],
    )(*last)


def solution(mesh):
    placed = (
        P("ctx", "tp"),
        P("tp"),
        P("ctx"),
        P("ctx", "tp"),
        P("ctx", "tp"),
        P("ctx", "tp"),
        P(None, "tp"),
        P("ctx", "tp"),
        P("tp", None),
    )
    return jax.shard_map(
        local,
        mesh=mesh,
        in_specs=placed,
        out_specs=(P(None, "tp"), P(None, "tp"), P(None, "tp")),
        check_vma=False,
    )
```

```python
import functools

import jax
import jax.numpy as jnp
from jax import lax
from jax.experimental import pallas as pl
from jax.experimental.pallas import tpu as pltpu
from jax.sharding import PartitionSpec as P


MODEL_WIDTH = 5376
QUERY_HEADS = 32
KEY_VALUE_HEADS = 16
HEAD_SIZE = 128
LOOKBACK_SPAN = 1024
ADAPTER_RANK = 8
LOG2E = 1.4426950408889634
SCALE = float(MODEL_WIDTH // QUERY_HEADS) ** (-0.5)
LANES = 128
GRANT = 62 << 20
ROW_K, ROW_V, ROW_ONE, ROW_DOC = 0, ADAPTER_RANK, 2 * ADAPTER_RANK, 2 * ADAPTER_RANK + 1
TABLE = 4 * ADAPTER_RANK

NT = (((1,), (1,)), ((), ()))
NN = (((1,), (0,)), ((), ()))
TN = (((0,), (0,)), ((), ()))


def dotf(left, right, dims):
    return lax.dot_general(left, right, dims, preferred_element_type=jnp.float32)


def shifted(value, axis, steps):
    count = lax.axis_size(axis)
    first, last = (max(0, -steps), min(count, count - steps))
    return lax.ppermute(value, axis, [(source, source + steps) for source in range(first, last)])


def xor_move(value, axis, step):
    return lax.ppermute(value, axis, [(at, at ^ step) for at in range(lax.axis_size(axis))])


def project_body(offset_ref, gradient_ref, weight_ref, out_ref):
    out_ref[...] = dotf(gradient_ref[...], weight_ref[...], NT).astype(out_ref.dtype)


def project(gradient, weight, first_block, blocks, width):
    rows, depth = gradient.shape
    return pl.pallas_call(
        project_body,
        grid_spec=pltpu.PrefetchScalarGridSpec(
            num_scalar_prefetch=1,
            grid=(blocks,),
            in_specs=[
                pl.BlockSpec((rows, depth), lambda i, off: (0, 0)),
                pl.BlockSpec((width, depth), lambda i, off: (off[0] + i, 0)),
            ],
            out_specs=pl.BlockSpec((rows, width), lambda i, off: (0, i)),
        ),
        out_shape=jax.ShapeDtypeStruct((rows, blocks * width), jnp.bfloat16),
        cost_estimate=pl.CostEstimate(
            flops=2 * rows * depth * width * blocks,
            bytes_accessed=2 * (rows * depth + width * blocks * depth + rows * width * blocks),
            transcendentals=0,
        ),
        compiler_params=pltpu.CompilerParams(vmem_limit_bytes=GRANT),
    )(first_block, gradient, weight)


def open_body(each, offset_ref, gradient_ref, weight_ref, x_ref, norm_ref, down_ref, *rest):
    k_ref, v_ref, out_ref, low_ref, *packs, down_scr = rest
    step = pl.program_id(0)
    out_ref[...] = dotf(gradient_ref[...], weight_ref[...], NT).astype(out_ref.dtype)

    @pl.when(step == 0)
    def _():
        gain = norm_ref[...].astype(jnp.float32).reshape(1, -1)
        down_scr[...] = (down_ref[...].astype(jnp.float32) * gain).astype(jnp.bfloat16)

    low_ref[0 : 3 * ADAPTER_RANK, :] = dotf(down_scr[...], x_ref[...], NT)
    hidden = x_ref[...].astype(jnp.float32)
    ones = jnp.ones((ADAPTER_RANK, hidden.shape[1]), jnp.bfloat16)
    low_ref[3 * ADAPTER_RANK :, :] = dotf(ones, (hidden * hidden).astype(jnp.bfloat16), NT)
    wide = k_ref.shape[1]
    for c, pack_ref in enumerate(packs):

        @pl.when(step // each == c)
        def _(pack_ref=pack_ref):
            pack_ref[:, :wide] = k_ref[...]
            pack_ref[:, wide:] = v_ref[...]


def pack_body(k_ref, v_ref, out_ref):
    wide = k_ref.shape[1]
    out_ref[:, :wide] = k_ref[...]
    out_ref[:, wide:] = v_ref[...]


def pack_call(keys, values, wide, blocks):
    rows = keys.shape[0]
    return pl.pallas_call(
        pack_body,
        grid=(blocks,),
        in_specs=[pl.BlockSpec((rows, wide), lambda i: (0, i))] * 2,
        out_specs=pl.BlockSpec((rows, 2 * wide), lambda i: (0, i)),
        out_shape=jax.ShapeDtypeStruct((rows, 2 * wide * blocks), keys.dtype),
        compiler_params=pltpu.CompilerParams(vmem_limit_bytes=GRANT),
    )(keys, values)


def open_call(gradient, weight, first_block, blocks, width, x, norm, down, keys, values, chunks):
    rows, depth = gradient.shape
    slab = rows // blocks
    wide = keys.shape[1] // blocks
    each = blocks // chunks
    skip = each
    extra = chunks - 1
    pack_specs = [pl.BlockSpec((rows, 2 * wide), lambda i, off: (0, jnp.minimum(i, each - 1)))] * extra
    pack_shape = jax.ShapeDtypeStruct((rows, 2 * wide * each), keys.dtype)
    return pl.pallas_call(
        functools.partial(open_body, each),
        grid_spec=pltpu.PrefetchScalarGridSpec(
            num_scalar_prefetch=1,
            grid=(blocks,),
            in_specs=[
                pl.BlockSpec((rows, depth), lambda i, off: (0, 0)),
                pl.BlockSpec((width, depth), lambda i, off: (off[0] + i, 0)),
                pl.BlockSpec((slab, depth), lambda i, off: (i, 0)),
                pl.BlockSpec((depth,), lambda i, off: (0,)),
                pl.BlockSpec((3 * ADAPTER_RANK, depth), lambda i, off: (0, 0)),
                pl.BlockSpec((rows, wide), lambda i, off: (0, jnp.minimum(i + skip, blocks - 1))),
                pl.BlockSpec((rows, wide), lambda i, off: (0, jnp.minimum(i + skip, blocks - 1))),
            ],
            out_specs=[
                pl.BlockSpec((rows, width), lambda i, off: (0, i)),
                pl.BlockSpec((TABLE, slab), lambda i, off: (0, i)),
            ]
            + pack_specs,
            scratch_shapes=[pltpu.VMEM((3 * ADAPTER_RANK, depth), jnp.bfloat16)],
        ),
        out_shape=[
            jax.ShapeDtypeStruct((rows, blocks * width), jnp.bfloat16),
            jax.ShapeDtypeStruct((TABLE, rows), jnp.float32),
        ]
        + [pack_shape] * extra,
        cost_estimate=pl.CostEstimate(
            flops=2 * rows * depth * width * blocks,
            bytes_accessed=2 * (2 * rows * depth + width * blocks * depth + rows * width * blocks),
            transcendentals=0,
        ),
        compiler_params=pltpu.CompilerParams(vmem_limit_bytes=GRANT),
    )(first_block, gradient, weight, x, norm, down, keys, values)


def table_body(mine_ref, theirs_ref, doc_ref, out_ref):
    joined = mine_ref[...] + theirs_ref[...]
    inverse = lax.rsqrt(joined[3 * ADAPTER_RANK : 3 * ADAPTER_RANK + 1] / float(MODEL_WIDTH) + 1e-06)
    low = joined * inverse
    rank = ADAPTER_RANK
    row = lax.broadcasted_iota(jnp.int32, (rank, low.shape[1]), 0)
    extra = jnp.where(row == 0, 1.0, jnp.where(row == 1, doc_ref[...].astype(jnp.float32), 0.0))
    out_ref[...] = jnp.concatenate([low[rank : 3 * rank], extra, low[:rank]], 0).astype(out_ref.dtype)


def prep_body(first_ref, t2_ref, t1_ref, t0_ref, ext_ref, st_ref):
    rows = t0_ref.shape[1]
    tables = [ref[...].astype(jnp.float32) for ref in (t2_ref, t1_ref, t0_ref)]
    blank = jnp.zeros((LANES - TABLE, rows), jnp.float32)
    for at, table in enumerate(tables):
        turned = jnp.concatenate([table, blank], 0).T
        ext_ref[at * rows : (at + 1) * rows, :] = turned.astype(ext_ref.dtype)
    ids = [table[ROW_DOC : ROW_DOC + 1] for table in tables]
    column = turned[:, ROW_DOC : ROW_DOC + 1]
    leading = column[0:1]
    before = sum(jnp.sum((one < leading).astype(jnp.float32), axis=1, keepdims=True) for one in ids[:2])
    inside = jnp.sum((ids[2] < column).astype(jnp.float32), axis=1, keepdims=True)
    begin = jnp.where(column > leading, inside + float(2 * rows), before).astype(jnp.int32)
    begin = jnp.broadcast_to(begin, st_ref.shape)
    band = lax.broadcasted_iota(jnp.int32, st_ref.shape, 0) + (2 * rows + 1 - LOOKBACK_SPAN)
    st_ref[...] = jnp.maximum(jnp.maximum(begin, band), first_ref[0])


def attend_body(
    steps, step_units, base, offset_ref, second_ref, q_ref, pg_ref, w_ref, recv_ref, k0, ka, kb, k2, v0, va, vb, v2, ext_ref, lq_ref, st_ref, *rest
):
    if base:
        before_ref, out_ref, s_scr, e_scr, ve, ke, do_scr = rest
    else:
        out_ref, s_scr, e_scr, ve, ke, do_scr = rest
    rows = pg_ref.shape[0]
    tile = s_scr.shape[1] // 2
    keys = s_scr.shape[2]
    width = tile
    factor = SCALE * LOG2E
    parts = rows // tile
    units = [(g, t) for g in range(step_units) for t in range(parts)]
    state = [{} for _ in units]
    columns = range(keys // width)
    step = pl.program_id(0)
    if base:

        @pl.when(step == 0)
        def _():
            out_ref[:, :base] = before_ref[...]

    def prepare(i):
        g, t = units[i]
        if t == 0:
            own = dotf(pg_ref[...], w_ref[2 * LANES * g : 2 * LANES * (g + 1), :], NT)
            got = recv_ref[:, 2 * LANES * g : 2 * LANES * (g + 1)].astype(jnp.float32)
            do_scr[g % 2] = (own + got).astype(jnp.bfloat16)
            for b, pair in enumerate((((k0, v0),), ((ka, va), (kb, vb)), ((k2, v2),))):
                span = slice(b * rows, (b + 1) * rows)
                cols = slice(g * LANES, (g + 1) * LANES)
                key, value = pair[0][0][:, cols], pair[0][1][:, cols]
                if len(pair) > 1:
                    key = jnp.where(second_ref[0] == 1, pair[1][0][:, cols], key)
                    value = jnp.where(second_ref[0] == 1, pair[1][1][:, cols], value)
                ke[g % 2, span, :LANES] = key
                ve[g % 2, span, :LANES] = value
                ke[g % 2, span, LANES:] = ext_ref[span, :]
                ve[g % 2, span, LANES:] = ext_ref[span, :]
        s = state[i]
        r0 = t * tile
        c0 = 2 * LANES * g
        s["q"] = jnp.concatenate(
            [q_ref[r0 : r0 + tile, c0 : c0 + LANES], q_ref[r0 : r0 + tile, c0 + LANES : c0 + 2 * LANES]], 0
        )
        start = st_ref[r0 : r0 + tile, :]
        s["start"] = jnp.concatenate([start, start], 0)
        s["peak"] = None

    def score(i, j):
        g, t = units[i]
        s = state[i]
        at = t * tile + j * width
        raw = dotf(s["q"], ke[g % 2, at : at + width, :LANES], NT)
        for h in range(width // LANES):
            value = raw[:, h * LANES : (h + 1) * LANES]
            pos = lax.broadcasted_iota(jnp.int32, value.shape, 1) + (at + h * LANES)
            ok = pos >= s["start"]
            if j == len(columns) - 1:
                row = lax.broadcasted_iota(jnp.int32, value.shape, 0)
                row = jnp.where(row >= tile, row - tile, row)
                ok = ok & (pos <= row + (2 * rows + t * tile))
            value = jnp.where(ok, value, -1e30)
            s_scr[i % 2, :, j * width + h * LANES : j * width + (h + 1) * LANES] = value
            s["peak"] = value if s["peak"] is None else jnp.maximum(s["peak"], value)

    def weigh(i, j):
        g, t = units[i]
        s = state[i]
        at = t * tile + j * width
        cols = slice(j * width, (j + 1) * width)
        e = jnp.exp2((s_scr[i % 2, :, cols] - s["top"]) * factor).astype(jnp.bfloat16)
        e_scr[i % 2, :, cols] = e
        part = dotf(e, ve[g % 2, at : at + width, :], NN)
        s["acc"] = part if j == 0 else s["acc"] + part

    def weighed(i):
        g, t = units[i]
        s = state[i]
        acc = s["acc"]
        do = do_scr[g % 2, t * tile : (t + 1) * tile, :]
        s["do"] = jnp.concatenate([do[:, :LANES], do[:, LANES:]], 0)
        s["inverse"] = 1.0 / acc[:, LANES + ROW_ONE : LANES + ROW_ONE + 1]
        s["delta"] = (
            jnp.sum(s["do"].astype(jnp.float32) * acc[:, :LANES], axis=1, keepdims=True) * s["inverse"]
        )
        s["uv"] = (acc[:, LANES:] * s["inverse"]).astype(jnp.bfloat16)

    def back(i, j):
        g, t = units[i]
        s = state[i]
        at = t * tile + j * width
        dp = dotf(s["do"], ve[g % 2, at : at + width, :LANES], NT)
        e = e_scr[i % 2, :, j * width : (j + 1) * width].astype(jnp.float32)
        ds = (e * (dp - s["delta"])).astype(jnp.bfloat16)
        part = dotf(ds, ke[g % 2, at : at + width, :], NN)
        s["back"] = part if j == 0 else s["back"] + part

    def backed(i):
        g, t = units[i]
        s = state[i]
        fin = (s["back"] * (s["inverse"] * SCALE)).astype(jnp.bfloat16)
        dq = jnp.concatenate([fin[:tile, :LANES], fin[tile:, :LANES]], 1)
        low_q = lq_ref[2 * ADAPTER_RANK :, t * tile : (t + 1) * tile]
        out = (dotf(low_q, dq, NN), dotf(fin[:, LANES:], s["q"], TN), dotf(s["uv"], s["do"], TN))
        if t > 0:
            out = tuple(a + b for a, b in zip(out, state[i - 1]["out"]))
            state[i - 1].clear()
        s["out"] = out
        if t == parts - 1:
            for unit_step in range(steps):

                @pl.when(step == unit_step)
                def _():
                    at = base + 4 * LANES * (unit_step * step_units + g)
                    out_ref[:, at : at + 2 * LANES] = out[0][ADAPTER_RANK:].astype(out_ref.dtype)
                    out_ref[:, at + 2 * LANES : at + 3 * LANES] = out[1][ROW_K : ROW_K + ADAPTER_RANK].astype(out_ref.dtype)
                    out_ref[:, at + 3 * LANES : at + 4 * LANES] = out[2][ROW_V : ROW_V + ADAPTER_RANK].astype(out_ref.dtype)

    prepare(0)
    for j in columns:
        score(0, j)
    for i in range(len(units) + 1):
        if i < len(units):
            state[i]["top"] = jnp.max(state[i]["peak"], axis=1, keepdims=True)
        if i + 1 < len(units):
            prepare(i + 1)
        for j in columns:
            if i < len(units):
                weigh(i, j)
            if i + 1 < len(units):
                score(i + 1, j)
            if i > 0:
                back(i - 1, j)
        if i < len(units):
            weighed(i)
        if i > 0:
            backed(i - 1)


def attend(queries, gradient, weight, recv, packs, ext, table, starts, first, second, skip, steps, units, before):
    rows, depth = gradient.shape
    tile = rows // 2
    keys = LOOKBACK_SPAN + tile
    base = 0 if before is None else before.shape[1]
    groups = steps * units
    col = lambda width, fn: pl.BlockSpec((rows, width), fn)
    total = base + 4 * LANES * groups
    wide = units * LANES
    operands = [queries, gradient, weight, recv, *packs, *packs, ext, table, starts]
    in_specs = (
        [
            col(2 * wide, lambda g, off, sec: (0, g + skip)),
            col(depth, lambda g, off, sec: (0, 0)),
            pl.BlockSpec((2 * wide, depth), lambda g, off, sec: (g + off[0], 0)),
            col(2 * wide, lambda g, off, sec: (0, g)),
        ]
        + [col(wide, lambda g, off, sec: (0, 2 * g))] * 4
        + [col(wide, lambda g, off, sec: (0, 2 * g + 1))] * 4
        + [
            pl.BlockSpec((3 * rows, LANES), lambda g, off, sec: (0, 0)),
            pl.BlockSpec((TABLE, rows), lambda g, off, sec: (0, 0)),
            pl.BlockSpec((rows, LANES), lambda g, off, sec: (0, 0)),
        ]
    )
    if base:
        operands.append(before)
        in_specs.append(pl.BlockSpec((ADAPTER_RANK, base), lambda g, off, sec: (0, 0)))
    pushes = rows * groups * 2 * keys // 256 * 4
    return pl.pallas_call(
        functools.partial(attend_body, steps, units, base),
        grid_spec=pltpu.PrefetchScalarGridSpec(
            num_scalar_prefetch=2,
            grid=(steps,),
            in_specs=in_specs,
            out_specs=pl.BlockSpec((ADAPTER_RANK, total), lambda g, off, sec: (0, 0)),
            scratch_shapes=[
                pltpu.VMEM((2, 2 * tile, keys), jnp.float32),
                pltpu.VMEM((2, 2 * tile, keys), jnp.bfloat16),
                pltpu.VMEM((2, 3 * rows, 2 * LANES), jnp.bfloat16),
                pltpu.VMEM((2, 3 * rows, 2 * LANES), jnp.bfloat16),
                pltpu.VMEM((2, rows, 2 * LANES), jnp.bfloat16),
            ],
        ),
        out_shape=jax.ShapeDtypeStruct((ADAPTER_RANK, total), jnp.bfloat16),
        cost_estimate=pl.CostEstimate(
            flops=pushes * 256 * 256 * 2 + 2 * rows * depth * 2 * LANES * groups,
            bytes_accessed=groups * rows * LANES * 20 + 4 * LANES * groups * depth,
            transcendentals=rows * groups * 2 * keys,
        ),
        compiler_params=pltpu.CompilerParams(vmem_limit_bytes=40 << 20),
    )(first, second, *operands)


def finish_body(*refs):
    q_ref, k_ref, v_ref = refs[-3:]
    mine = refs[0][...].astype(jnp.float32) + refs[1][...].astype(jnp.float32)
    total = jnp.sum(mine * mine, keepdims=True)
    if len(refs) == 7:
        theirs = refs[2][...].astype(jnp.float32) + refs[3][...].astype(jnp.float32)
        total = total + jnp.sum(theirs * theirs, keepdims=True)
    else:
        total = refs[2][0:1, 0:1]
    count = float(ADAPTER_RANK * (QUERY_HEADS + 2 * KEY_VALUE_HEADS) * HEAD_SIZE)
    mine = mine * jnp.sqrt(count / (total + 1e-06))
    for g in range(k_ref.shape[1] // LANES):
        at = 4 * LANES * g
        q_ref[:, 2 * LANES * g : 2 * LANES * (g + 1)] = mine[:, at : at + 2 * LANES]
        k_ref[:, LANES * g : LANES * (g + 1)] = mine[:, at + 2 * LANES : at + 3 * LANES]
        v_ref[:, LANES * g : LANES * (g + 1)] = mine[:, at + 3 * LANES : at + 4 * LANES]


def local(
    layer_input,
    norm_weight,
    document_index,
    stored_queries,
    stored_keys,
    stored_values,
    output_weight,
    projection_gradient,
    adapter_down_maps,
):
    rows = stored_queries.shape[0]
    heads_width = stored_queries.shape[1]
    groups = stored_keys.shape[1] // HEAD_SIZE
    tp, ctx = lax.axis_size("tp"), lax.axis_size("ctx")
    tp_at, ctx_at = lax.axis_index("tp"), lax.axis_index("ctx")
    chunks = 2 if groups % 4 == 0 else 1
    units = chunks
    steps = groups // (chunks * units)
    width = 2 * LANES
    half = heads_width // width
    per = half // chunks
    scalar = lambda value: jnp.asarray(value, jnp.int32).reshape(1)

    pair = [(at, at + 1) for at in range(0, ctx, 2)]
    packs = [pack_call(stored_keys, stored_values, units * LANES, steps)]
    fars, befores = [], []
    fars.append(shifted(packs[0], "ctx", 2))
    befores.append(lax.ppermute(packs[0], "ctx", pair))

    received = []
    for c in range(chunks):
        got = []
        for d in range(1, tp):
            first = scalar(((tp_at + d) % tp) * half + c * per)
            if c == 0 and d == 1:
                part, low, *more = open_call(
                    projection_gradient,
                    output_weight,
                    first,
                    per,
                    width,
                    layer_input,
                    norm_weight,
                    adapter_down_maps.T,
                    stored_keys,
                    stored_values,
                    chunks,
                )
            else:
                part = project(projection_gradient, output_weight, first, per, width)
            got.append(lax.ppermute(part, "tp", [(at, (at + d) % tp) for at in range(tp)]))
        total = got[0]
        if len(got) > 1:
            total = sum(one.astype(jnp.float32) for one in got)
        received.append(total)

    move = 1
    while 2 * move < tp:
        low = low + xor_move(low, "tp", move)
        move *= 2
    other = xor_move(low, "tp", move)
    table = pl.pallas_call(table_body, out_shape=jax.ShapeDtypeStruct((TABLE, rows), jnp.bfloat16))(
        low, other, document_index[None, :]
    )
    table2 = shifted(table, "ctx", 2)
    table1 = shifted(table, "ctx", 1)
    prepare = pl.pallas_call(
        prep_body,
        grid_spec=pltpu.PrefetchScalarGridSpec(
            num_scalar_prefetch=1,
            grid=(1,),
            in_specs=[pl.BlockSpec((TABLE, rows), lambda i, off: (0, 0))] * 3,
            out_specs=[
                pl.BlockSpec((3 * rows, LANES), lambda i, off: (0, 0)),
                pl.BlockSpec((rows, LANES), lambda i, off: (0, 0)),
            ],
        ),
        out_shape=[
            jax.ShapeDtypeStruct((3 * rows, LANES), jnp.bfloat16),
            jax.ShapeDtypeStruct((rows, LANES), jnp.int32),
        ],
    )
    ext, starts = prepare(scalar(2 * rows - ctx_at * rows), table2, table1, table)

    second = scalar(ctx_at % 2)
    sums = None
    for c in range(chunks):
        if c > 0:
            packs.append(more[c - 1])
            fars.append(shifted(packs[c], "ctx", 2))
            befores.append(lax.ppermute(packs[c], "ctx", pair))
        back = lax.ppermute(fars[c], "ctx", [(b, a) for a, b in pair])
        first = scalar((tp_at * half + c * per) // units)
        sums = attend(
            stored_queries,
            projection_gradient,
            output_weight,
            received[c],
            (fars[c], back, befores[c], packs[c]),
            ext,
            table,
            starts,
            first,
            second,
            c * steps,
            steps,
            units,
            sums,
        )

    order = [1] + [1 << at for at in range(2, ctx.bit_length() - 1)]
    for move in order:
        sums = (sums.astype(jnp.float32) + xor_move(sums, "ctx", move).astype(jnp.float32)).astype(jnp.bfloat16)
    last = [sums, xor_move(sums, "ctx", 2)]
    if tp == 2:
        both = [(at, at ^ 5) for at in range(2 * ctx)]
        last = last + [xor_move(sums, "tp", 1), lax.ppermute(sums, ("ctx", "tp"), both)]
    else:
        squared = jnp.sum(jnp.square(last[0].astype(jnp.float32) + last[1].astype(jnp.float32))).reshape(1, 1)
        move = 1
        while move < tp:
            squared = squared + xor_move(squared, "tp", move)
            move *= 2
        last.append(squared)
    sizes = (heads_width, groups * HEAD_SIZE, groups * HEAD_SIZE)
    return pl.pallas_call(
        finish_body,
        out_shape=[jax.ShapeDtypeStruct((ADAPTER_RANK, size), jnp.float32) for size in sizes],
    )(*last)


def solution(mesh):
    placed = (
        P("ctx", "tp"),
        P("tp"),
        P("ctx"),
        P("ctx", "tp"),
        P("ctx", "tp"),
        P("ctx", "tp"),
        P(None, "tp"),
        P("ctx", "tp"),
        P("tp", None),
    )
    return jax.shard_map(
        local,
        mesh=mesh,
        in_specs=placed,
        out_specs=(P(None, "tp"), P(None, "tp"), P(None, "tp")),
        check_vma=False,
    )
```

```python
import functools

import jax
import jax.numpy as jnp
from jax import lax
from jax.experimental import pallas as pl
from jax.experimental.pallas import tpu as pltpu
from jax.sharding import PartitionSpec as P


MODEL_WIDTH = 5376
QUERY_HEADS = 32
KEY_VALUE_HEADS = 16
HEAD_SIZE = 128
LOOKBACK_SPAN = 1024
ADAPTER_RANK = 8
LOG2E = 1.4426950408889634
SCALE = float(MODEL_WIDTH // QUERY_HEADS) ** (-0.5)
LANES = 128
GRANT = 62 << 20
SMALL = pltpu.CompilerParams(vmem_limit_bytes=8 << 20)
ROW_K, ROW_V, ROW_ONE, ROW_DOC = 0, ADAPTER_RANK, 2 * ADAPTER_RANK, 2 * ADAPTER_RANK + 1
TABLE = 4 * ADAPTER_RANK

NT = (((1,), (1,)), ((), ()))
NN = (((1,), (0,)), ((), ()))
TN = (((0,), (0,)), ((), ()))


def dotf(left, right, dims):
    return lax.dot_general(left, right, dims, preferred_element_type=jnp.float32)


def shifted(value, axis, steps):
    count = lax.axis_size(axis)
    first, last = (max(0, -steps), min(count, count - steps))
    return lax.ppermute(value, axis, [(source, source + steps) for source in range(first, last)])


def xor_move(value, axis, step):
    return lax.ppermute(value, axis, [(at, at ^ step) for at in range(lax.axis_size(axis))])


def project_body(offset_ref, gradient_ref, weight_ref, out_ref):
    out_ref[...] = dotf(gradient_ref[...], weight_ref[...], NT).astype(out_ref.dtype)


def project(gradient, weight, first_block, blocks, width):
    rows, depth = gradient.shape
    return pl.pallas_call(
        project_body,
        grid_spec=pltpu.PrefetchScalarGridSpec(
            num_scalar_prefetch=1,
            grid=(blocks,),
            in_specs=[
                pl.BlockSpec((rows, depth), lambda i, off: (0, 0)),
                pl.BlockSpec((width, depth), lambda i, off: (off[0] + i, 0)),
            ],
            out_specs=pl.BlockSpec((rows, width), lambda i, off: (0, i)),
        ),
        out_shape=jax.ShapeDtypeStruct((rows, blocks * width), jnp.bfloat16),
        cost_estimate=pl.CostEstimate(
            flops=2 * rows * depth * width * blocks,
            bytes_accessed=2 * (rows * depth + width * blocks * depth + rows * width * blocks),
            transcendentals=0,
        ),
        compiler_params=pltpu.CompilerParams(vmem_limit_bytes=GRANT),
    )(first_block, gradient, weight)


def open_body(each, offset_ref, gradient_ref, weight_ref, x_ref, norm_ref, down_ref, *rest):
    k_ref, v_ref, out_ref, low_ref, *packs = rest
    step = pl.program_id(0)
    out_ref[...] = dotf(gradient_ref[...], weight_ref[...], NT).astype(out_ref.dtype)
    hidden = x_ref[...].astype(jnp.float32)
    weighted = (hidden * norm_ref[...].astype(jnp.float32)).astype(jnp.bfloat16)
    low_ref[0 : 3 * ADAPTER_RANK, :] = dotf(down_ref[...], weighted, NT)
    ones = jnp.ones((ADAPTER_RANK, hidden.shape[1]), jnp.bfloat16)
    low_ref[3 * ADAPTER_RANK :, :] = dotf(ones, (hidden * hidden).astype(jnp.bfloat16), NT)
    wide = k_ref.shape[1]
    for c, pack_ref in enumerate(packs):

        @pl.when(step // each == c)
        def _(pack_ref=pack_ref):
            pack_ref[:, :wide] = k_ref[...]
            pack_ref[:, wide:] = v_ref[...]


def pack_body(k_ref, v_ref, out_ref):
    wide = k_ref.shape[1]
    out_ref[:, :wide] = k_ref[...]
    out_ref[:, wide:] = v_ref[...]


def pack_call(keys, values, wide, blocks):
    rows = keys.shape[0]
    return pl.pallas_call(
        pack_body,
        grid=(blocks,),
        in_specs=[pl.BlockSpec((rows, wide), lambda i: (0, i))] * 2,
        out_specs=pl.BlockSpec((rows, 2 * wide), lambda i: (0, i)),
        out_shape=jax.ShapeDtypeStruct((rows, 2 * wide * blocks), keys.dtype),
        compiler_params=pltpu.CompilerParams(vmem_limit_bytes=GRANT),
    )(keys, values)


def open_call(gradient, weight, first_block, blocks, width, x, norm, down, keys, values, chunks):
    rows, depth = gradient.shape
    slab = rows // blocks
    wide = keys.shape[1] // blocks
    each = blocks // chunks
    skip = each
    extra = chunks - 1
    pack_specs = [pl.BlockSpec((rows, 2 * wide), lambda i, off: (0, jnp.minimum(i, each - 1)))] * extra
    pack_shape = jax.ShapeDtypeStruct((rows, 2 * wide * each), keys.dtype)
    return pl.pallas_call(
        functools.partial(open_body, each),
        grid_spec=pltpu.PrefetchScalarGridSpec(
            num_scalar_prefetch=1,
            grid=(blocks,),
            in_specs=[
                pl.BlockSpec((rows, depth), lambda i, off: (0, 0)),
                pl.BlockSpec((width, depth), lambda i, off: (off[0] + i, 0)),
                pl.BlockSpec((slab, depth), lambda i, off: (i, 0)),
                pl.BlockSpec((1, depth), lambda i, off: (0, 0)),
                pl.BlockSpec((3 * ADAPTER_RANK, depth), lambda i, off: (0, 0)),
                pl.BlockSpec((rows, wide), lambda i, off: (0, jnp.minimum(i + skip, blocks - 1))),
                pl.BlockSpec((rows, wide), lambda i, off: (0, jnp.minimum(i + skip, blocks - 1))),
            ],
            out_specs=[
                pl.BlockSpec((rows, width), lambda i, off: (0, i)),
                pl.BlockSpec((TABLE, slab), lambda i, off: (0, i)),
            ]
            + pack_specs,
        ),
        out_shape=[
            jax.ShapeDtypeStruct((rows, blocks * width), jnp.bfloat16),
            jax.ShapeDtypeStruct((TABLE, rows), jnp.float32),
        ]
        + [pack_shape] * extra,
        cost_estimate=pl.CostEstimate(
            flops=2 * rows * depth * width * blocks,
            bytes_accessed=2 * (2 * rows * depth + width * blocks * depth + rows * width * blocks),
            transcendentals=0,
        ),
        compiler_params=pltpu.CompilerParams(vmem_limit_bytes=GRANT),
    )(first_block, gradient, weight, x, norm, down, keys, values)


def table_body(mine_ref, theirs_ref, doc_ref, out_ref):
    joined = mine_ref[...] + theirs_ref[...]
    inverse = lax.rsqrt(joined[3 * ADAPTER_RANK : 3 * ADAPTER_RANK + 1] / float(MODEL_WIDTH) + 1e-06)
    low = joined * inverse
    rank = ADAPTER_RANK
    row = lax.broadcasted_iota(jnp.int32, (rank, low.shape[1]), 0)
    extra = jnp.where(row == 0, 1.0, jnp.where(row == 1, doc_ref[...].astype(jnp.float32), 0.0))
    out_ref[...] = jnp.concatenate([low[rank : 3 * rank], extra, low[:rank]], 0).astype(out_ref.dtype)


def prep_body(first_ref, t2_ref, t1_ref, t0_ref, ext_ref, st_ref):
    rows = t0_ref.shape[1]
    tables = [ref[...].astype(jnp.float32) for ref in (t2_ref, t1_ref, t0_ref)]
    blank = jnp.zeros((LANES - TABLE, rows), jnp.float32)
    for at, table in enumerate(tables):
        turned = jnp.concatenate([table, blank], 0).T
        ext_ref[at * rows : (at + 1) * rows, :] = turned.astype(ext_ref.dtype)
    ids = [table[ROW_DOC : ROW_DOC + 1] for table in tables]
    column = turned[:, ROW_DOC : ROW_DOC + 1]
    leading = column[0:1]
    before = sum(jnp.sum((one < leading).astype(jnp.float32), axis=1, keepdims=True) for one in ids[:2])
    inside = jnp.sum((ids[2] < column).astype(jnp.float32), axis=1, keepdims=True)
    begin = jnp.where(column > leading, inside + float(2 * rows), before).astype(jnp.int32)
    begin = jnp.broadcast_to(begin, st_ref.shape)
    band = lax.broadcasted_iota(jnp.int32, st_ref.shape, 0) + (2 * rows + 1 - LOOKBACK_SPAN)
    st_ref[...] = jnp.maximum(jnp.maximum(begin, band), first_ref[0])


def attend_body(
    steps, step_units, base, offset_ref, q_ref, pg_hbm, w_hbm, recv_ref, k0, k1, k2, v0, v1, v2, ext_ref, lq_ref, st_ref, *rest
):
    if base:
        before_ref, out_ref, *scratch = rest
    else:
        out_ref, *scratch = rest
    s_scr, e_scr, ve, ke, do_scr, pg_scr, w_scr, sems = scratch
    rows = pg_scr.shape[0]
    tile = s_scr.shape[1] // 2
    keys = s_scr.shape[2]
    width = tile
    factor = SCALE * LOG2E
    parts = rows // tile
    units = [(g, t) for g in range(step_units) for t in range(parts)]
    state = [{} for _ in units]
    columns = range(keys // width)
    step = pl.program_id(0)
    deep = 2 * LANES

    def gradient_copy():
        return pltpu.make_async_copy(pg_hbm, pg_scr, sems.at[0])

    def weight_copy(group):
        first = pl.multiple_of((offset_ref[0] * step_units + group) * deep, deep)
        return pltpu.make_async_copy(w_hbm.at[pl.ds(first, deep), :], w_scr.at[group], sems.at[1 + group])

    @pl.when(step == 0)
    def _():
        gradient_copy().start()
        for group in range(steps * step_units):
            weight_copy(group).start()

    if base:

        @pl.when(step == 0)
        def _():
            out_ref[:, :base] = before_ref[...]

    def prepare(i):
        g, t = units[i]
        if t == 0:
            for b, (k_ref, v_ref) in enumerate(((k0, v0), (k1, v1), (k2, v2))):
                span = slice(b * rows, (b + 1) * rows)
                ke[g % 2, span, :LANES] = k_ref[:, g * LANES : (g + 1) * LANES]
                ve[g % 2, span, :LANES] = v_ref[:, g * LANES : (g + 1) * LANES]
                ke[g % 2, span, LANES:] = ext_ref[span, :]
                ve[g % 2, span, LANES:] = ext_ref[span, :]
        s = state[i]
        r0 = t * tile
        c0 = 2 * LANES * g
        s["q"] = jnp.concatenate(
            [q_ref[r0 : r0 + tile, c0 : c0 + LANES], q_ref[r0 : r0 + tile, c0 + LANES : c0 + 2 * LANES]], 0
        )
        start = st_ref[r0 : r0 + tile, :]
        s["start"] = jnp.concatenate([start, start], 0)
        s["peak"] = None

    def cotangent(i):
        g, t = units[i]
        if t == 0:
            own = dotf(pg_scr[...], w_scr[step * step_units + g], NT)
            got = recv_ref[:, deep * g : deep * (g + 1)].astype(jnp.float32)
            do_scr[g % 2] = (own + got).astype(jnp.bfloat16)

    def score(i, j):
        g, t = units[i]
        s = state[i]
        at = t * tile + j * width
        raw = dotf(s["q"], ke[g % 2, at : at + width, :LANES], NT)
        for h in range(width // LANES):
            value = raw[:, h * LANES : (h + 1) * LANES]
            pos = lax.broadcasted_iota(jnp.int32, value.shape, 1) + (at + h * LANES)
            ok = pos >= s["start"]
            if j == len(columns) - 1:
                row = lax.broadcasted_iota(jnp.int32, value.shape, 0)
                row = jnp.where(row >= tile, row - tile, row)
                ok = ok & (pos <= row + (2 * rows + t * tile))
            value = jnp.where(ok, value, -1e30)
            s_scr[i % 2, :, j * width + h * LANES : j * width + (h + 1) * LANES] = value
            s["peak"] = value if s["peak"] is None else jnp.maximum(s["peak"], value)

    def weigh(i, j):
        g, t = units[i]
        s = state[i]
        at = t * tile + j * width
        cols = slice(j * width, (j + 1) * width)
        e = jnp.exp2((s_scr[i % 2, :, cols] - s["top"]) * factor).astype(jnp.bfloat16)
        e_scr[i % 2, :, cols] = e
        part = dotf(e, ve[g % 2, at : at + width, :], NN)
        s["acc"] = part if j == 0 else s["acc"] + part

    def weighed(i):
        g, t = units[i]
        s = state[i]
        acc = s["acc"]
        do = do_scr[g % 2, t * tile : (t + 1) * tile, :]
        s["do"] = jnp.concatenate([do[:, :LANES], do[:, LANES:]], 0)
        s["inverse"] = 1.0 / acc[:, LANES + ROW_ONE : LANES + ROW_ONE + 1]
        s["delta"] = (
            jnp.sum(s["do"].astype(jnp.float32) * acc[:, :LANES], axis=1, keepdims=True) * s["inverse"]
        )
        s["uv"] = (acc[:, LANES:] * s["inverse"]).astype(jnp.bfloat16)

    def back(i, j):
        g, t = units[i]
        s = state[i]
        at = t * tile + j * width
        dp = dotf(s["do"], ve[g % 2, at : at + width, :LANES], NT)
        e = e_scr[i % 2, :, j * width : (j + 1) * width].astype(jnp.float32)
        ds = (e * (dp - s["delta"])).astype(jnp.bfloat16)
        part = dotf(ds, ke[g % 2, at : at + width, :], NN)
        s["back"] = part if j == 0 else s["back"] + part

    def backed(i):
        g, t = units[i]
        s = state[i]
        fin = (s["back"] * (s["inverse"] * SCALE)).astype(jnp.bfloat16)
        dq = jnp.concatenate([fin[:tile, :LANES], fin[tile:, :LANES]], 1)
        low_q = lq_ref[2 * ADAPTER_RANK :, t * tile : (t + 1) * tile]
        out = (dotf(low_q, dq, NN), dotf(fin[:, LANES:], s["q"], TN), dotf(s["uv"], s["do"], TN))
        if t > 0:
            out = tuple(a + b for a, b in zip(out, state[i - 1]["out"]))
            state[i - 1].clear()
        s["out"] = out
        if t == parts - 1:
            for unit_step in range(steps):

                @pl.when(step == unit_step)
                def _():
                    at = base + 4 * LANES * (unit_step * step_units + g)
                    out_ref[:, at : at + 2 * LANES] = out[0][ADAPTER_RANK:].astype(out_ref.dtype)
                    out_ref[:, at + 2 * LANES : at + 3 * LANES] = out[1][ROW_K : ROW_K + ADAPTER_RANK].astype(out_ref.dtype)
                    out_ref[:, at + 3 * LANES : at + 4 * LANES] = out[2][ROW_V : ROW_V + ADAPTER_RANK].astype(out_ref.dtype)

    prepare(0)
    for j in columns:
        score(0, j)

    @pl.when(step == 0)
    def _():
        gradient_copy().wait()

    for g in range(step_units):
        weight_copy(step * step_units + g).wait()
    cotangent(0)
    for i in range(len(units) + 1):
        if i < len(units):
            state[i]["top"] = jnp.max(state[i]["peak"], axis=1, keepdims=True)
        if i + 1 < len(units):
            prepare(i + 1)
            cotangent(i + 1)
        for j in columns:
            if i < len(units):
                weigh(i, j)
            if i + 1 < len(units):
                score(i + 1, j)
            if i > 0:
                back(i - 1, j)
        if i < len(units):
            weighed(i)
        if i > 0:
            backed(i - 1)


def attend(queries, gradient, weight, recv, packs, ext, table, starts, first, skip, steps, units, before):
    rows, depth = gradient.shape
    tile = rows // 2
    keys = LOOKBACK_SPAN + tile
    base = 0 if before is None else before.shape[1]
    groups = steps * units
    col = lambda width, fn: pl.BlockSpec((rows, width), fn)
    total = base + 4 * LANES * groups
    wide = units * LANES
    operands = [queries, gradient, weight, recv, *packs, *packs, ext, table, starts]
    in_specs = (
        [
            col(2 * wide, lambda g, off: (0, g + skip)),
            pl.BlockSpec(memory_space=pl.ANY),
            pl.BlockSpec(memory_space=pl.ANY),
            col(2 * wide, lambda g, off: (0, g)),
        ]
        + [col(wide, lambda g, off: (0, 2 * g))] * 3
        + [col(wide, lambda g, off: (0, 2 * g + 1))] * 3
        + [
            pl.BlockSpec((3 * rows, LANES), lambda g, off: (0, 0)),
            pl.BlockSpec((TABLE, rows), lambda g, off: (0, 0)),
            pl.BlockSpec((rows, LANES), lambda g, off: (0, 0)),
        ]
    )
    if base:
        operands.append(before)
        in_specs.append(pl.BlockSpec((ADAPTER_RANK, base), lambda g, off: (0, 0)))
    pushes = rows * groups * 2 * keys // 256 * 4
    return pl.pallas_call(
        functools.partial(attend_body, steps, units, base),
        grid_spec=pltpu.PrefetchScalarGridSpec(
            num_scalar_prefetch=1,
            grid=(steps,),
            in_specs=in_specs,
            out_specs=pl.BlockSpec((ADAPTER_RANK, total), lambda g, off: (0, 0)),
            scratch_shapes=[
                pltpu.VMEM((2, 2 * tile, keys), jnp.float32),
                pltpu.VMEM((2, 2 * tile, keys), jnp.bfloat16),
                pltpu.VMEM((2, 3 * rows, 2 * LANES), jnp.bfloat16),
                pltpu.VMEM((2, 3 * rows, 2 * LANES), jnp.bfloat16),
                pltpu.VMEM((2, rows, 2 * LANES), jnp.bfloat16),
                pltpu.VMEM((rows, depth), jnp.bfloat16),
                pltpu.VMEM((groups, 2 * LANES, depth), jnp.bfloat16),
                pltpu.SemaphoreType.DMA((1 + groups,)),
            ],
        ),
        out_shape=jax.ShapeDtypeStruct((ADAPTER_RANK, total), jnp.bfloat16),
        cost_estimate=pl.CostEstimate(
            flops=pushes * 256 * 256 * 2 + 2 * rows * depth * 2 * LANES * groups,
            bytes_accessed=groups * rows * LANES * 20 + 4 * LANES * groups * depth,
            transcendentals=rows * groups * 2 * keys,
        ),
        compiler_params=pltpu.CompilerParams(vmem_limit_bytes=GRANT),
    )(first, *operands)


def finish_body(*refs):
    q_ref, k_ref, v_ref = refs[-3:]
    mine = refs[0][...].astype(jnp.float32) + refs[1][...].astype(jnp.float32)
    total = refs[2][0:1, 0:1]
    count = float(ADAPTER_RANK * (QUERY_HEADS + 2 * KEY_VALUE_HEADS) * HEAD_SIZE)
    mine = mine * jnp.sqrt(count / (total + 1e-06))
    for g in range(k_ref.shape[1] // LANES):
        at = 4 * LANES * g
        q_ref[:, 2 * LANES * g : 2 * LANES * (g + 1)] = mine[:, at : at + 2 * LANES]
        k_ref[:, LANES * g : LANES * (g + 1)] = mine[:, at + 2 * LANES : at + 3 * LANES]
        v_ref[:, LANES * g : LANES * (g + 1)] = mine[:, at + 3 * LANES : at + 4 * LANES]


def local(
    layer_input,
    norm_weight,
    document_index,
    stored_queries,
    stored_keys,
    stored_values,
    output_weight,
    projection_gradient,
    adapter_down_maps,
):
    rows = stored_queries.shape[0]
    heads_width = stored_queries.shape[1]
    groups = stored_keys.shape[1] // HEAD_SIZE
    tp, ctx = lax.axis_size("tp"), lax.axis_size("ctx")
    tp_at, ctx_at = lax.axis_index("tp"), lax.axis_index("ctx")
    chunks = 2 if groups % 4 == 0 else 1
    units = chunks
    steps = groups // (chunks * units)
    width = 2 * LANES
    half = heads_width // width
    per = half // chunks
    scalar = lambda value: jnp.asarray(value, jnp.int32).reshape(1)

    packs = [pack_call(stored_keys, stored_values, units * LANES, steps)]
    fars = [shifted(packs[0], "ctx", 2)]

    received = []
    for c in range(chunks):
        got = []
        for d in range(1, tp):
            first = scalar(((tp_at + d) % tp) * half + c * per)
            if c == 0 and d == 1:
                part, low, *more = open_call(
                    projection_gradient,
                    output_weight,
                    first,
                    per,
                    width,
                    layer_input,
                    norm_weight[None, :],
                    adapter_down_maps.T,
                    stored_keys,
                    stored_values,
                    chunks,
                )
            else:
                part = project(projection_gradient, output_weight, first, per, width)
            got.append(lax.ppermute(part, "tp", [(at, (at + d) % tp) for at in range(tp)]))
        total = got[0]
        if len(got) > 1:
            total = sum(one.astype(jnp.float32) for one in got)
        received.append(total)

    move = 1
    while 2 * move < tp:
        low = low + xor_move(low, "tp", move)
        move *= 2
    other = xor_move(low, "tp", move)
    table = pl.pallas_call(
        table_body, out_shape=jax.ShapeDtypeStruct((TABLE, rows), jnp.bfloat16), compiler_params=SMALL
    )(
        low, other, document_index[None, :]
    )
    table2 = shifted(table, "ctx", 2)
    table1 = shifted(table, "ctx", 1)
    prepare = pl.pallas_call(
        prep_body,
        grid_spec=pltpu.PrefetchScalarGridSpec(
            num_scalar_prefetch=1,
            grid=(1,),
            in_specs=[pl.BlockSpec((TABLE, rows), lambda i, off: (0, 0))] * 3,
            out_specs=[
                pl.BlockSpec((3 * rows, LANES), lambda i, off: (0, 0)),
                pl.BlockSpec((rows, LANES), lambda i, off: (0, 0)),
            ],
        ),
        out_shape=[
            jax.ShapeDtypeStruct((3 * rows, LANES), jnp.bfloat16),
            jax.ShapeDtypeStruct((rows, LANES), jnp.int32),
        ],
        compiler_params=SMALL,
    )
    ext, starts = prepare(scalar(2 * rows - ctx_at * rows), table2, table1, table)

    second = (ctx_at % 2) == 1
    sums = None
    for c in range(chunks):
        if c > 0:
            packs.append(more[c - 1])
            fars.append(shifted(packs[c], "ctx", 2))
        picked = jnp.where(second, fars[c], packs[c])
        near = xor_move(picked, "ctx", 1)
        first = scalar((tp_at * half + c * per) // units)
        sums = attend(
            stored_queries,
            projection_gradient,
            output_weight,
            received[c],
            (fars[c], near, packs[c]),
            ext,
            table,
            starts,
            first,
            c * steps,
            steps,
            units,
            sums,
        )

    order = [1] + [1 << at for at in range(2, ctx.bit_length() - 1)]
    for move in order:
        sums = (sums.astype(jnp.float32) + xor_move(sums, "ctx", move).astype(jnp.float32)).astype(jnp.bfloat16)
    last = [sums, xor_move(sums, "ctx", 2)]
    squared = jnp.sum(jnp.square(last[0].astype(jnp.float32) + last[1].astype(jnp.float32))).reshape(1, 1)
    move = 1
    while move < tp:
        squared = squared + xor_move(squared, "tp", move)
        move *= 2
    last.append(squared)
    sizes = (heads_width, groups * HEAD_SIZE, groups * HEAD_SIZE)
    return pl.pallas_call(
        finish_body,
        out_shape=[jax.ShapeDtypeStruct((ADAPTER_RANK, size), jnp.float32) for size in sizes],
        compiler_params=SMALL,
    )(*last)


def solution(mesh):
    placed = (
        P("ctx", "tp"),
        P("tp"),
        P("ctx"),
        P("ctx", "tp"),
        P("ctx", "tp"),
        P("ctx", "tp"),
        P(None, "tp"),
        P("ctx", "tp"),
        P("tp", None),
    )
    return jax.shard_map(
        local,
        mesh=mesh,
        in_specs=placed,
        out_specs=(P(None, "tp"), P(None, "tp"), P(None, "tp")),
        check_vma=False,
    )
```

```python
import functools

import jax
import jax.numpy as jnp
from jax import lax
from jax.experimental import pallas as pl
from jax.experimental.pallas import tpu as pltpu
from jax.sharding import PartitionSpec as P


MODEL_WIDTH = 5376
QUERY_HEADS = 32
KEY_VALUE_HEADS = 16
HEAD_SIZE = 128
LOOKBACK_SPAN = 1024
ADAPTER_RANK = 8
LOG2E = 1.4426950408889634
SCALE = float(MODEL_WIDTH // QUERY_HEADS) ** (-0.5)
LANES = 128
GRANT = 52 << 20
SMALL = pltpu.CompilerParams(vmem_limit_bytes=8 << 20)
ROW_K, ROW_V, ROW_ONE, ROW_DOC = 0, ADAPTER_RANK, 2 * ADAPTER_RANK, 2 * ADAPTER_RANK + 1
TABLE = 4 * ADAPTER_RANK

NT = (((1,), (1,)), ((), ()))
NN = (((1,), (0,)), ((), ()))
TN = (((0,), (0,)), ((), ()))


def dotf(left, right, dims):
    return lax.dot_general(left, right, dims, preferred_element_type=jnp.float32)


def shifted(value, axis, steps):
    count = lax.axis_size(axis)
    first, last = (max(0, -steps), min(count, count - steps))
    return lax.ppermute(value, axis, [(source, source + steps) for source in range(first, last)])


def xor_move(value, axis, step):
    return lax.ppermute(value, axis, [(at, at ^ step) for at in range(lax.axis_size(axis))])


def project_body(offset_ref, gradient_ref, weight_ref, out_ref):
    out_ref[...] = dotf(gradient_ref[...], weight_ref[...], NT).astype(out_ref.dtype)


def project(gradient, weight, first_block, blocks, width, dtype=jnp.bfloat16):
    rows, depth = gradient.shape
    return pl.pallas_call(
        project_body,
        grid_spec=pltpu.PrefetchScalarGridSpec(
            num_scalar_prefetch=1,
            grid=(blocks,),
            in_specs=[
                pl.BlockSpec((rows, depth), lambda i, off: (0, 0)),
                pl.BlockSpec((width, depth), lambda i, off: (off[0] + i, 0)),
            ],
            out_specs=pl.BlockSpec((rows, width), lambda i, off: (0, i)),
        ),
        out_shape=jax.ShapeDtypeStruct((rows, blocks * width), dtype),
        cost_estimate=pl.CostEstimate(
            flops=2 * rows * depth * width * blocks,
            bytes_accessed=2 * (rows * depth + width * blocks * depth + rows * width * blocks),
            transcendentals=0,
        ),
        compiler_params=pltpu.CompilerParams(vmem_limit_bytes=GRANT),
    )(first_block, gradient, weight)


def open_body(each, offset_ref, gradient_ref, weight_ref, x_ref, norm_ref, down_ref, *rest):
    k_ref, v_ref, out_ref, low_ref, *packs = rest
    step = pl.program_id(0)
    out_ref[...] = dotf(gradient_ref[...], weight_ref[...], NT).astype(out_ref.dtype)
    hidden = x_ref[...].astype(jnp.float32)
    weighted = (hidden * norm_ref[...].astype(jnp.float32)).astype(jnp.bfloat16)
    low_ref[0 : 3 * ADAPTER_RANK, :] = dotf(down_ref[...], weighted, NT)
    ones = jnp.ones((ADAPTER_RANK, hidden.shape[1]), jnp.bfloat16)
    low_ref[3 * ADAPTER_RANK :, :] = dotf(ones, (hidden * hidden).astype(jnp.bfloat16), NT)
    wide = k_ref.shape[1]
    for c, pack_ref in enumerate(packs):

        @pl.when(step // each == c)
        def _(pack_ref=pack_ref):
            pack_ref[:, :wide] = k_ref[...]
            pack_ref[:, wide:] = v_ref[...]


def open_call(gradient, weight, first_block, blocks, width, x, norm, down, keys, values, chunks):
    rows, depth = gradient.shape
    slab = rows // blocks
    wide = keys.shape[1] // blocks
    each = blocks // chunks
    pack_specs = [
        pl.BlockSpec((rows, 2 * wide), lambda i, off, c=c: (0, jnp.clip(i - c * each, 0, each - 1)))
        for c in range(chunks)
    ]
    pack_shape = jax.ShapeDtypeStruct((rows, 2 * wide * each), keys.dtype)
    return pl.pallas_call(
        functools.partial(open_body, each),
        grid_spec=pltpu.PrefetchScalarGridSpec(
            num_scalar_prefetch=1,
            grid=(blocks,),
            in_specs=[
                pl.BlockSpec((rows, depth), lambda i, off: (0, 0)),
                pl.BlockSpec((width, depth), lambda i, off: (off[0] + i, 0)),
                pl.BlockSpec((slab, depth), lambda i, off: (i, 0)),
                pl.BlockSpec((1, depth), lambda i, off: (0, 0)),
                pl.BlockSpec((3 * ADAPTER_RANK, depth), lambda i, off: (0, 0)),
                pl.BlockSpec((rows, wide), lambda i, off: (0, i)),
                pl.BlockSpec((rows, wide), lambda i, off: (0, i)),
            ],
            out_specs=[
                pl.BlockSpec((rows, width), lambda i, off: (0, i)),
                pl.BlockSpec((TABLE, slab), lambda i, off: (0, i)),
            ]
            + pack_specs,
        ),
        out_shape=[
            jax.ShapeDtypeStruct((rows, blocks * width), jnp.bfloat16),
            jax.ShapeDtypeStruct((TABLE, rows), jnp.float32),
        ]
        + [pack_shape] * chunks,
        cost_estimate=pl.CostEstimate(
            flops=2 * rows * depth * width * blocks,
            bytes_accessed=2 * (2 * rows * depth + width * blocks * depth + rows * width * blocks),
            transcendentals=0,
        ),
        compiler_params=pltpu.CompilerParams(vmem_limit_bytes=GRANT),
    )(first_block, gradient, weight, x, norm, down, keys, values)


def table_body(mine_ref, theirs_ref, doc_ref, out_ref):
    joined = mine_ref[...] + theirs_ref[...]
    inverse = lax.rsqrt(joined[3 * ADAPTER_RANK : 3 * ADAPTER_RANK + 1] / float(MODEL_WIDTH) + 1e-06)
    low = joined * inverse
    rank = ADAPTER_RANK
    row = lax.broadcasted_iota(jnp.int32, (rank, low.shape[1]), 0)
    extra = jnp.where(row == 0, 1.0, jnp.where(row == 1, doc_ref[...].astype(jnp.float32), 0.0))
    out_ref[...] = jnp.concatenate([low[rank : 3 * rank], extra, low[:rank]], 0).astype(out_ref.dtype)


def prep_body(first_ref, t2_ref, t1_ref, t0_ref, ext_ref, st_ref):
    rows = t0_ref.shape[1]
    tables = [ref[...].astype(jnp.float32) for ref in (t2_ref, t1_ref, t0_ref)]
    blank = jnp.zeros((LANES - TABLE, rows), jnp.float32)
    for at, table in enumerate(tables):
        turned = jnp.concatenate([table, blank], 0).T
        ext_ref[at * rows : (at + 1) * rows, :] = turned.astype(ext_ref.dtype)
    ids = [table[ROW_DOC : ROW_DOC + 1] for table in tables]
    column = turned[:, ROW_DOC : ROW_DOC + 1]
    leading = column[0:1]
    before = sum(jnp.sum((one < leading).astype(jnp.float32), axis=1, keepdims=True) for one in ids[:2])
    inside = jnp.sum((ids[2] < column).astype(jnp.float32), axis=1, keepdims=True)
    begin = jnp.where(column > leading, inside + float(2 * rows), before).astype(jnp.int32)
    begin = jnp.broadcast_to(begin, st_ref.shape)
    band = lax.broadcasted_iota(jnp.int32, st_ref.shape, 0) + (2 * rows + 1 - LOOKBACK_SPAN)
    st_ref[...] = jnp.maximum(jnp.maximum(begin, band), first_ref[0])


def attend_body(steps, step_units, base, alone, offset_ref, q_ref, *rest):
    if alone:
        pg_hbm, w_hbm, *rest = rest
    else:
        own_ref, *rest = rest
    recv_ref, k0, k1, k2, v0, v1, v2, ext_ref, lq_ref, st_ref, *rest = rest
    if base:
        before_ref, *rest = rest
    out_ref, s_scr, e_scr, ve, ke, do_scr, *rest = rest
    if alone:
        pg_scr, w_scr, sems = rest
    rows = q_ref.shape[0]
    tile = s_scr.shape[1] // 2
    keys = s_scr.shape[2]
    width = tile
    factor = SCALE * LOG2E
    parts = rows // tile
    units = [(g, t) for g in range(step_units) for t in range(parts)]
    state = [{} for _ in units]
    columns = range(keys // width)
    step = pl.program_id(0)
    deep = 2 * LANES

    def gradient_copy():
        return pltpu.make_async_copy(pg_hbm, pg_scr, sems.at[0])

    def weight_copy(group):
        first = pl.multiple_of((offset_ref[0] * step_units + group) * deep, deep)
        return pltpu.make_async_copy(w_hbm.at[pl.ds(first, deep), :], w_scr.at[group], sems.at[1 + group])

    if alone:

        @pl.when(step == 0)
        def _():
            gradient_copy().start()
            for group in range(steps * step_units):
                weight_copy(group).start()

    if base:

        @pl.when(step == 0)
        def _():
            out_ref[:, :base] = before_ref[...]

    def prepare(i):
        g, t = units[i]
        if t == 0:
            for b, (k_ref, v_ref) in enumerate(((k0, v0), (k1, v1), (k2, v2))):
                span = slice(b * rows, (b + 1) * rows)
                ke[g % 2, span, :LANES] = k_ref[:, g * LANES : (g + 1) * LANES]
                ve[g % 2, span, :LANES] = v_ref[:, g * LANES : (g + 1) * LANES]
                ke[g % 2, span, LANES:] = ext_ref[span, :]
                ve[g % 2, span, LANES:] = ext_ref[span, :]
        s = state[i]
        r0 = t * tile
        c0 = 2 * LANES * g
        s["q"] = jnp.concatenate(
            [q_ref[r0 : r0 + tile, c0 : c0 + LANES], q_ref[r0 : r0 + tile, c0 + LANES : c0 + 2 * LANES]], 0
        )
        start = st_ref[r0 : r0 + tile, :]
        s["start"] = jnp.concatenate([start, start], 0)
        s["peak"] = None

    def cotangent(i):
        g, t = units[i]
        if t == 0:
            if alone:
                own = dotf(pg_scr[...], w_scr[step * step_units + g], NT)
            else:
                own = own_ref[:, deep * g : deep * (g + 1)]
            got = recv_ref[:, deep * g : deep * (g + 1)].astype(jnp.float32)
            do_scr[g % 2] = (own + got).astype(jnp.bfloat16)

    def score(i, j):
        g, t = units[i]
        s = state[i]
        at = t * tile + j * width
        raw = dotf(s["q"], ke[g % 2, at : at + width, :LANES], NT)
        for h in range(width // LANES):
            value = raw[:, h * LANES : (h + 1) * LANES]
            pos = lax.broadcasted_iota(jnp.int32, value.shape, 1) + (at + h * LANES)
            ok = pos >= s["start"]
            if j == len(columns) - 1:
                row = lax.broadcasted_iota(jnp.int32, value.shape, 0)
                row = jnp.where(row >= tile, row - tile, row)
                ok = ok & (pos <= row + (2 * rows + t * tile))
            value = jnp.where(ok, value, -1e30)
            s_scr[i % 2, :, j * width + h * LANES : j * width + (h + 1) * LANES] = value
            s["peak"] = value if s["peak"] is None else jnp.maximum(s["peak"], value)

    def weigh(i, j):
        g, t = units[i]
        s = state[i]
        at = t * tile + j * width
        cols = slice(j * width, (j + 1) * width)
        e = jnp.exp2((s_scr[i % 2, :, cols] - s["top"]) * factor).astype(jnp.bfloat16)
        e_scr[i % 2, :, cols] = e
        part = dotf(e, ve[g % 2, at : at + width, :], NN)
        s["acc"] = part if j == 0 else s["acc"] + part

    def weighed(i):
        g, t = units[i]
        s = state[i]
        acc = s["acc"]
        do = do_scr[g % 2, t * tile : (t + 1) * tile, :]
        s["do"] = jnp.concatenate([do[:, :LANES], do[:, LANES:]], 0)
        s["inverse"] = 1.0 / acc[:, LANES + ROW_ONE : LANES + ROW_ONE + 1]
        s["delta"] = (
            jnp.sum(s["do"].astype(jnp.float32) * acc[:, :LANES], axis=1, keepdims=True) * s["inverse"]
        )
        s["uv"] = (acc[:, LANES:] * s["inverse"]).astype(jnp.bfloat16)

    def back(i, j):
        g, t = units[i]
        s = state[i]
        at = t * tile + j * width
        dp = dotf(s["do"], ve[g % 2, at : at + width, :LANES], NT)
        e = e_scr[i % 2, :, j * width : (j + 1) * width].astype(jnp.float32)
        ds = (e * (dp - s["delta"])).astype(jnp.bfloat16)
        part = dotf(ds, ke[g % 2, at : at + width, :], NN)
        s["back"] = part if j == 0 else s["back"] + part

    def backed(i):
        g, t = units[i]
        s = state[i]
        fin = (s["back"] * (s["inverse"] * SCALE)).astype(jnp.bfloat16)
        dq = jnp.concatenate([fin[:tile, :LANES], fin[tile:, :LANES]], 1)
        low_q = lq_ref[2 * ADAPTER_RANK :, t * tile : (t + 1) * tile]
        out = (dotf(low_q, dq, NN), dotf(fin[:, LANES:], s["q"], TN), dotf(s["uv"], s["do"], TN))
        if t > 0:
            out = tuple(a + b for a, b in zip(out, state[i - 1]["out"]))
            state[i - 1].clear()
        s["out"] = out
        if t == parts - 1:
            for unit_step in range(steps):

                @pl.when(step == unit_step)
                def _():
                    at = base + 4 * LANES * (unit_step * step_units + g)
                    out_ref[:, at : at + 2 * LANES] = out[0][ADAPTER_RANK:].astype(out_ref.dtype)
                    out_ref[:, at + 2 * LANES : at + 3 * LANES] = out[1][ROW_K : ROW_K + ADAPTER_RANK].astype(out_ref.dtype)
                    out_ref[:, at + 3 * LANES : at + 4 * LANES] = out[2][ROW_V : ROW_V + ADAPTER_RANK].astype(out_ref.dtype)

    prepare(0)
    for j in columns:
        score(0, j)

    if alone:

        @pl.when(step == 0)
        def _():
            gradient_copy().wait()

        for g in range(step_units):
            weight_copy(step * step_units + g).wait()
    cotangent(0)
    for i in range(len(units) + 1):
        if i < len(units):
            state[i]["top"] = jnp.max(state[i]["peak"], axis=1, keepdims=True)
        if i + 1 < len(units):
            prepare(i + 1)
            cotangent(i + 1)
        for j in columns:
            if i < len(units):
                weigh(i, j)
            if i + 1 < len(units):
                score(i + 1, j)
            if i > 0:
                back(i - 1, j)
        if i < len(units):
            weighed(i)
        if i > 0:
            backed(i - 1)


def attend(queries, gradient, weight, recv, own, packs, ext, table, starts, first, skip, steps, units, before):
    rows, depth = gradient.shape
    tile = rows // 2
    keys = LOOKBACK_SPAN + tile
    base = 0 if before is None else before.shape[1]
    groups = steps * units
    col = lambda width, fn: pl.BlockSpec((rows, width), fn)
    total = base + 4 * LANES * groups
    wide = units * LANES
    alone = own is None
    source = [gradient, weight] if alone else [own]
    operands = [queries, *source, recv, *packs, *packs, ext, table, starts]
    in_specs = (
        [
            col(2 * wide, lambda g, off: (0, g + skip)),
            *([pl.BlockSpec(memory_space=pl.ANY)] * 2 if alone else [col(2 * wide, lambda g, off: (0, g))]),
            col(2 * wide, lambda g, off: (0, g)),
        ]
        + [col(wide, lambda g, off: (0, 2 * g))] * 3
        + [col(wide, lambda g, off: (0, 2 * g + 1))] * 3
        + [
            pl.BlockSpec((3 * rows, LANES), lambda g, off: (0, 0)),
            pl.BlockSpec((TABLE, rows), lambda g, off: (0, 0)),
            pl.BlockSpec((rows, LANES), lambda g, off: (0, 0)),
        ]
    )
    if base:
        operands.append(before)
        in_specs.append(pl.BlockSpec((ADAPTER_RANK, base), lambda g, off: (0, 0)))
    pushes = rows * groups * 2 * keys // 256 * 4
    return pl.pallas_call(
        functools.partial(attend_body, steps, units, base, alone),
        grid_spec=pltpu.PrefetchScalarGridSpec(
            num_scalar_prefetch=1,
            grid=(steps,),
            in_specs=in_specs,
            out_specs=pl.BlockSpec((ADAPTER_RANK, total), lambda g, off: (0, 0)),
            scratch_shapes=[
                pltpu.VMEM((2, 2 * tile, keys), jnp.float32),
                pltpu.VMEM((2, 2 * tile, keys), jnp.bfloat16),
                pltpu.VMEM((2, 3 * rows, 2 * LANES), jnp.bfloat16),
                pltpu.VMEM((2, 3 * rows, 2 * LANES), jnp.bfloat16),
                pltpu.VMEM((2, rows, 2 * LANES), jnp.bfloat16),
            ]
            + alone
            * [
                pltpu.VMEM((rows, depth), jnp.bfloat16),
                pltpu.VMEM((groups, 2 * LANES, depth), jnp.bfloat16),
                pltpu.SemaphoreType.DMA((1 + groups,)),
            ],
        ),
        out_shape=jax.ShapeDtypeStruct((ADAPTER_RANK, total), jnp.bfloat16),
        cost_estimate=pl.CostEstimate(
            flops=pushes * 256 * 256 * 2 + alone * 2 * rows * depth * 2 * LANES * groups,
            bytes_accessed=groups * rows * LANES * 20 + 4 * LANES * groups * depth,
            transcendentals=rows * groups * 2 * keys,
        ),
        compiler_params=pltpu.CompilerParams(vmem_limit_bytes=GRANT),
    )(first, *operands)


def finish_body(*refs):
    q_ref, k_ref, v_ref = refs[-3:]
    mine = refs[0][...].astype(jnp.float32) + refs[1][...].astype(jnp.float32)
    total = refs[2][0:1, 0:1]
    count = float(ADAPTER_RANK * (QUERY_HEADS + 2 * KEY_VALUE_HEADS) * HEAD_SIZE)
    mine = mine * jnp.sqrt(count / (total + 1e-06))
    for g in range(k_ref.shape[1] // LANES):
        at = 4 * LANES * g
        q_ref[:, 2 * LANES * g : 2 * LANES * (g + 1)] = mine[:, at : at + 2 * LANES]
        k_ref[:, LANES * g : LANES * (g + 1)] = mine[:, at + 2 * LANES : at + 3 * LANES]
        v_ref[:, LANES * g : LANES * (g + 1)] = mine[:, at + 3 * LANES : at + 4 * LANES]


def local(
    layer_input,
    norm_weight,
    document_index,
    stored_queries,
    stored_keys,
    stored_values,
    output_weight,
    projection_gradient,
    adapter_down_maps,
):
    rows = stored_queries.shape[0]
    heads_width = stored_queries.shape[1]
    groups = stored_keys.shape[1] // HEAD_SIZE
    tp, ctx = lax.axis_size("tp"), lax.axis_size("ctx")
    tp_at, ctx_at = lax.axis_index("tp"), lax.axis_index("ctx")
    chunks = 2 if groups % 4 == 0 else 1
    units = chunks
    steps = groups // (chunks * units)
    width = 2 * LANES
    half = heads_width // width
    per = half // chunks
    scalar = lambda value: jnp.asarray(value, jnp.int32).reshape(1)

    received = []
    for c in range(chunks):
        got = []
        for d in range(1, tp):
            first = scalar(((tp_at + d) % tp) * half + c * per)
            if c == 0 and d == 1:
                part, low, *packs = open_call(
                    projection_gradient,
                    output_weight,
                    first,
                    per,
                    width,
                    layer_input,
                    norm_weight[None, :],
                    adapter_down_maps.T,
                    stored_keys,
                    stored_values,
                    chunks,
                )
            else:
                part = project(projection_gradient, output_weight, first, per, width)
            got.append(lax.ppermute(part, "tp", [(at, (at + d) % tp) for at in range(tp)]))
        total = got[0]
        if len(got) > 1:
            total = sum(one.astype(jnp.float32) for one in got)
        received.append(total)

    move = 1
    while 2 * move < tp:
        low = low + xor_move(low, "tp", move)
        move *= 2
    other = xor_move(low, "tp", move)
    table = pl.pallas_call(
        table_body, out_shape=jax.ShapeDtypeStruct((TABLE, rows), jnp.bfloat16), compiler_params=SMALL
    )(
        low, other, document_index[None, :]
    )
    table2 = shifted(table, "ctx", 2)
    table1 = shifted(table, "ctx", 1)
    prepare = pl.pallas_call(
        prep_body,
        grid_spec=pltpu.PrefetchScalarGridSpec(
            num_scalar_prefetch=1,
            grid=(1,),
            in_specs=[pl.BlockSpec((TABLE, rows), lambda i, off: (0, 0))] * 3,
            out_specs=[
                pl.BlockSpec((3 * rows, LANES), lambda i, off: (0, 0)),
                pl.BlockSpec((rows, LANES), lambda i, off: (0, 0)),
            ],
        ),
        out_shape=[
            jax.ShapeDtypeStruct((3 * rows, LANES), jnp.bfloat16),
            jax.ShapeDtypeStruct((rows, LANES), jnp.int32),
        ],
        compiler_params=SMALL,
    )
    ext, starts = prepare(scalar(2 * rows - ctx_at * rows), table2, table1, table)

    second = (ctx_at % 2) == 1
    sums = None
    for c in range(chunks):
        far = shifted(packs[c], "ctx", 2)
        picked = jnp.where(second, far, packs[c])
        near = xor_move(picked, "ctx", 1)
        first = scalar((tp_at * half + c * per) // units)
        own = None
        if c < chunks - 1:
            begin = scalar(tp_at * half + c * per)
            own = project(projection_gradient, output_weight, begin, per, width, jnp.float32)
        sums = attend(
            stored_queries,
            projection_gradient,
            output_weight,
            received[c],
            own,
            (far, near, packs[c]),
            ext,
            table,
            starts,
            first,
            c * steps,
            steps,
            units,
            sums,
        )

    order = [1] + [1 << at for at in range(2, ctx.bit_length() - 1)]
    for move in order:
        sums = (sums.astype(jnp.float32) + xor_move(sums, "ctx", move).astype(jnp.float32)).astype(jnp.bfloat16)
    last = [sums, xor_move(sums, "ctx", 2)]
    squared = jnp.sum(jnp.square(last[0].astype(jnp.float32) + last[1].astype(jnp.float32))).reshape(1, 1)
    move = 1
    while move < tp:
        squared = squared + xor_move(squared, "tp", move)
        move *= 2
    last.append(squared)
    sizes = (heads_width, groups * HEAD_SIZE, groups * HEAD_SIZE)
    return pl.pallas_call(
        finish_body,
        out_shape=[jax.ShapeDtypeStruct((ADAPTER_RANK, size), jnp.float32) for size in sizes],
        compiler_params=SMALL,
    )(*last)


def solution(mesh):
    placed = (
        P("ctx", "tp"),
        P("tp"),
        P("ctx"),
        P("ctx", "tp"),
        P("ctx", "tp"),
        P("ctx", "tp"),
        P(None, "tp"),
        P("ctx", "tp"),
        P("tp", None),
    )
    return jax.shard_map(
        local,
        mesh=mesh,
        in_specs=placed,
        out_specs=(P(None, "tp"), P(None, "tp"), P(None, "tp")),
        check_vma=False,
    )
```

```python
import functools

import jax
import jax.numpy as jnp
from jax import lax
from jax.experimental import pallas as pl
from jax.experimental.pallas import tpu as pltpu
from jax.sharding import PartitionSpec as P


MODEL_WIDTH = 5376
QUERY_HEADS = 32
KEY_VALUE_HEADS = 16
HEAD_SIZE = 128
LOOKBACK_SPAN = 1024
ADAPTER_RANK = 8
LOG2E = 1.4426950408889634
SCALE = float(MODEL_WIDTH // QUERY_HEADS) ** (-0.5)
LANES = 128
GRANT = 52 << 20
SMALL = pltpu.CompilerParams(vmem_limit_bytes=8 << 20)
ROW_K, ROW_V, ROW_ONE, ROW_DOC = 0, ADAPTER_RANK, 2 * ADAPTER_RANK, 2 * ADAPTER_RANK + 1
TABLE = 4 * ADAPTER_RANK

NT = (((1,), (1,)), ((), ()))
NN = (((1,), (0,)), ((), ()))
TN = (((0,), (0,)), ((), ()))


def dotf(left, right, dims):
    return lax.dot_general(left, right, dims, preferred_element_type=jnp.float32)


def shifted(value, axis, steps):
    count = lax.axis_size(axis)
    first, last = (max(0, -steps), min(count, count - steps))
    return lax.ppermute(value, axis, [(source, source + steps) for source in range(first, last)])


def xor_move(value, axis, step):
    return lax.ppermute(value, axis, [(at, at ^ step) for at in range(lax.axis_size(axis))])


def project_body(offset_ref, gradient_ref, weight_ref, *rest):
    if len(rest) > 1:
        k_ref, v_ref, out_ref, pack_ref = rest
        wide = k_ref.shape[1]
        pack_ref[:, :wide] = k_ref[...]
        pack_ref[:, wide:] = v_ref[...]
    else:
        (out_ref,) = rest
    out_ref[...] = dotf(gradient_ref[...], weight_ref[...], NT).astype(out_ref.dtype)


def pack_body(k_ref, v_ref, out_ref):
    wide = k_ref.shape[1]
    out_ref[:, :wide] = k_ref[...]
    out_ref[:, wide:] = v_ref[...]


def pack_call(keys, values, wide, blocks):
    rows = keys.shape[0]
    return pl.pallas_call(
        pack_body,
        grid=(blocks,),
        in_specs=[pl.BlockSpec((rows, wide), lambda i: (0, i))] * 2,
        out_specs=pl.BlockSpec((rows, 2 * wide), lambda i: (0, i)),
        out_shape=jax.ShapeDtypeStruct((rows, 2 * wide * blocks), keys.dtype),
        compiler_params=pltpu.CompilerParams(vmem_limit_bytes=62 << 20),
    )(keys, values)


def project(gradient, weight, first_block, blocks, width, keys=None, values=None, wide=0, skip=0):
    rows, depth = gradient.shape
    out_specs = [pl.BlockSpec((rows, width), lambda i, off: (0, i))]
    out_shape = [jax.ShapeDtypeStruct((rows, blocks * width), jnp.bfloat16)]
    in_specs = [
        pl.BlockSpec((rows, depth), lambda i, off: (0, 0)),
        pl.BlockSpec((width, depth), lambda i, off: (off[0] + i, 0)),
    ]
    operands = [gradient, weight]
    if keys is not None:
        operands += [keys, values]
        in_specs += [pl.BlockSpec((rows, wide), lambda i, off: (0, i // 2 + skip))] * 2
        out_specs.append(pl.BlockSpec((rows, 2 * wide), lambda i, off: (0, i // 2)))
        out_shape.append(jax.ShapeDtypeStruct((rows, blocks * wide), keys.dtype))
    return pl.pallas_call(
        project_body,
        grid_spec=pltpu.PrefetchScalarGridSpec(
            num_scalar_prefetch=1, grid=(blocks,), in_specs=in_specs, out_specs=out_specs
        ),
        out_shape=out_shape,
        cost_estimate=pl.CostEstimate(
            flops=2 * rows * depth * width * blocks,
            bytes_accessed=2 * (rows * depth + width * blocks * depth + rows * width * blocks),
            transcendentals=0,
        ),
        compiler_params=pltpu.CompilerParams(vmem_limit_bytes=GRANT),
    )(first_block, *operands)


def open_body(offset_ref, gradient_ref, weight_ref, x_ref, norm_ref, down_ref, out_ref, low_ref):
    out_ref[...] = dotf(gradient_ref[...], weight_ref[...], NT).astype(out_ref.dtype)
    hidden = x_ref[...].astype(jnp.float32)
    weighted = (hidden * norm_ref[...].astype(jnp.float32)).astype(jnp.bfloat16)
    low_ref[0 : 3 * ADAPTER_RANK, :] = dotf(down_ref[...], weighted, NT)
    ones = jnp.ones((ADAPTER_RANK, hidden.shape[1]), jnp.bfloat16)
    low_ref[3 * ADAPTER_RANK :, :] = dotf(ones, (hidden * hidden).astype(jnp.bfloat16), NT)


def open_call(gradient, weight, first_block, blocks, width, x, norm, down):
    rows, depth = gradient.shape
    slab = rows // blocks
    return pl.pallas_call(
        open_body,
        grid_spec=pltpu.PrefetchScalarGridSpec(
            num_scalar_prefetch=1,
            grid=(blocks,),
            in_specs=[
                pl.BlockSpec((rows, depth), lambda i, off: (0, 0)),
                pl.BlockSpec((width, depth), lambda i, off: (off[0] + i, 0)),
                pl.BlockSpec((slab, depth), lambda i, off: (i, 0)),
                pl.BlockSpec((1, depth), lambda i, off: (0, 0)),
                pl.BlockSpec((3 * ADAPTER_RANK, depth), lambda i, off: (0, 0)),
            ],
            out_specs=[
                pl.BlockSpec((rows, width), lambda i, off: (0, i)),
                pl.BlockSpec((TABLE, slab), lambda i, off: (0, i)),
            ],
        ),
        out_shape=[
            jax.ShapeDtypeStruct((rows, blocks * width), jnp.bfloat16),
            jax.ShapeDtypeStruct((TABLE, rows), jnp.float32),
        ],
        cost_estimate=pl.CostEstimate(
            flops=2 * rows * depth * width * blocks,
            bytes_accessed=2 * (2 * rows * depth + width * blocks * depth + rows * width * blocks),
            transcendentals=0,
        ),
        compiler_params=pltpu.CompilerParams(vmem_limit_bytes=GRANT),
    )(first_block, gradient, weight, x, norm, down)


def table_body(mine_ref, theirs_ref, doc_ref, out_ref):
    joined = mine_ref[...] + theirs_ref[...]
    inverse = lax.rsqrt(joined[3 * ADAPTER_RANK : 3 * ADAPTER_RANK + 1] / float(MODEL_WIDTH) + 1e-06)
    low = joined * inverse
    rank = ADAPTER_RANK
    row = lax.broadcasted_iota(jnp.int32, (rank, low.shape[1]), 0)
    extra = jnp.where(row == 0, 1.0, jnp.where(row == 1, doc_ref[...].astype(jnp.float32), 0.0))
    out_ref[...] = jnp.concatenate([low[rank : 3 * rank], extra, low[:rank]], 0).astype(out_ref.dtype)


def prep_body(first_ref, t2_ref, t1_ref, t0_ref, ext_ref, st_ref):
    rows = t0_ref.shape[1]
    tables = [ref[...].astype(jnp.float32) for ref in (t2_ref, t1_ref, t0_ref)]
    blank = jnp.zeros((LANES - TABLE, rows), jnp.float32)
    for at, table in enumerate(tables):
        turned = jnp.concatenate([table, blank], 0).T
        ext_ref[at * rows : (at + 1) * rows, :] = turned.astype(ext_ref.dtype)
    ids = [table[ROW_DOC : ROW_DOC + 1] for table in tables]
    column = turned[:, ROW_DOC : ROW_DOC + 1]
    leading = column[0:1]
    before = sum(jnp.sum((one < leading).astype(jnp.float32), axis=1, keepdims=True) for one in ids[:2])
    inside = jnp.sum((ids[2] < column).astype(jnp.float32), axis=1, keepdims=True)
    begin = jnp.where(column > leading, inside + float(2 * rows), before).astype(jnp.int32)
    begin = jnp.broadcast_to(begin, st_ref.shape)
    band = lax.broadcasted_iota(jnp.int32, st_ref.shape, 0) + (2 * rows + 1 - LOOKBACK_SPAN)
    st_ref[...] = jnp.maximum(jnp.maximum(begin, band), first_ref[0])


def attend_body(steps, step_units, base, alone, offset_ref, q_ref, *rest):
    if alone:
        pg_hbm, w_hbm, *rest = rest
    else:
        own_ref, *rest = rest
    recv_ref, k0, k1, k2, v0, v1, v2, ext_ref, lq_ref, st_ref, *rest = rest
    if base:
        before_ref, *rest = rest
    out_ref, s_scr, e_scr, ve, ke, do_scr, *rest = rest
    if alone:
        pg_scr, w_scr, sems = rest
    rows = q_ref.shape[0]
    tile = s_scr.shape[1] // 2
    keys = s_scr.shape[2]
    width = tile
    factor = SCALE * LOG2E
    parts = rows // tile
    units = [(g, t) for g in range(step_units) for t in range(parts)]
    state = [{} for _ in units]
    columns = range(keys // width)
    step = pl.program_id(0)
    deep = 2 * LANES

    def gradient_copy():
        return pltpu.make_async_copy(pg_hbm, pg_scr, sems.at[0])

    def weight_copy(group):
        first = pl.multiple_of((offset_ref[0] * step_units + group) * deep, deep)
        return pltpu.make_async_copy(w_hbm.at[pl.ds(first, deep), :], w_scr.at[group], sems.at[1 + group])

    if alone:

        @pl.when(step == 0)
        def _():
            gradient_copy().start()
            for group in range(steps * step_units):
                weight_copy(group).start()

    if base:

        @pl.when(step == 0)
        def _():
            out_ref[:, :base] = before_ref[...]

    def prepare(i):
        g, t = units[i]
        if t == 0:
            for b, (k_ref, v_ref) in enumerate(((k0, v0), (k1, v1), (k2, v2))):
                span = slice(b * rows, (b + 1) * rows)
                ke[g % 2, span, :LANES] = k_ref[:, g * LANES : (g + 1) * LANES]
                ve[g % 2, span, :LANES] = v_ref[:, g * LANES : (g + 1) * LANES]
                ke[g % 2, span, LANES:] = ext_ref[span, :]
                ve[g % 2, span, LANES:] = ext_ref[span, :]
        s = state[i]
        r0 = t * tile
        c0 = 2 * LANES * g
        s["q"] = jnp.concatenate(
            [q_ref[r0 : r0 + tile, c0 : c0 + LANES], q_ref[r0 : r0 + tile, c0 + LANES : c0 + 2 * LANES]], 0
        )
        start = st_ref[r0 : r0 + tile, :]
        s["start"] = jnp.concatenate([start, start], 0)
        s["peak"] = None

    def cotangent(i):
        g, t = units[i]
        if t == 0:
            if alone:
                own = dotf(pg_scr[...], w_scr[step * step_units + g], NT)
            else:
                own = own_ref[:, deep * g : deep * (g + 1)]
            got = recv_ref[:, deep * g : deep * (g + 1)].astype(jnp.float32)
            do_scr[g % 2] = (own + got).astype(jnp.bfloat16)

    def score(i, j):
        g, t = units[i]
        s = state[i]
        at = t * tile + j * width
        raw = dotf(s["q"], ke[g % 2, at : at + width, :LANES], NT)
        for h in range(width // LANES):
            value = raw[:, h * LANES : (h + 1) * LANES]
            pos = lax.broadcasted_iota(jnp.int32, value.shape, 1) + (at + h * LANES)
            ok = pos >= s["start"]
            if j == len(columns) - 1:
                row = lax.broadcasted_iota(jnp.int32, value.shape, 0)
                row = jnp.where(row >= tile, row - tile, row)
                ok = ok & (pos <= row + (2 * rows + t * tile))
            value = jnp.where(ok, value, -1e30)
            s_scr[i % 2, :, j * width + h * LANES : j * width + (h + 1) * LANES] = value
            s["peak"] = value if s["peak"] is None else jnp.maximum(s["peak"], value)

    def weigh(i, j):
        g, t = units[i]
        s = state[i]
        at = t * tile + j * width
        cols = slice(j * width, (j + 1) * width)
        e = jnp.exp2((s_scr[i % 2, :, cols] - s["top"]) * factor).astype(jnp.bfloat16)
        e_scr[i % 2, :, cols] = e
        part = dotf(e, ve[g % 2, at : at + width, :], NN)
        s["acc"] = part if j == 0 else s["acc"] + part

    def weighed(i):
        g, t = units[i]
        s = state[i]
        acc = s["acc"]
        do = do_scr[g % 2, t * tile : (t + 1) * tile, :]
        s["do"] = jnp.concatenate([do[:, :LANES], do[:, LANES:]], 0)
        s["inverse"] = 1.0 / acc[:, LANES + ROW_ONE : LANES + ROW_ONE + 1]
        s["delta"] = (
            jnp.sum(s["do"].astype(jnp.float32) * acc[:, :LANES], axis=1, keepdims=True) * s["inverse"]
        )
        s["uv"] = (acc[:, LANES:] * s["inverse"]).astype(jnp.bfloat16)

    def back(i, j):
        g, t = units[i]
        s = state[i]
        at = t * tile + j * width
        dp = dotf(s["do"], ve[g % 2, at : at + width, :LANES], NT)
        e = e_scr[i % 2, :, j * width : (j + 1) * width].astype(jnp.float32)
        ds = (e * (dp - s["delta"])).astype(jnp.bfloat16)
        part = dotf(ds, ke[g % 2, at : at + width, :], NN)
        s["back"] = part if j == 0 else s["back"] + part

    def backed(i):
        g, t = units[i]
        s = state[i]
        fin = (s["back"] * (s["inverse"] * SCALE)).astype(jnp.bfloat16)
        dq = jnp.concatenate([fin[:tile, :LANES], fin[tile:, :LANES]], 1)
        low_q = lq_ref[2 * ADAPTER_RANK :, t * tile : (t + 1) * tile]
        out = (dotf(low_q, dq, NN), dotf(fin[:, LANES:], s["q"], TN), dotf(s["uv"], s["do"], TN))
        if t > 0:
            out = tuple(a + b for a, b in zip(out, state[i - 1]["out"]))
            state[i - 1].clear()
        s["out"] = out
        if t == parts - 1:
            for unit_step in range(steps):

                @pl.when(step == unit_step)
                def _():
                    at = base + 4 * LANES * (unit_step * step_units + g)
                    out_ref[:, at : at + 2 * LANES] = out[0][ADAPTER_RANK:].astype(out_ref.dtype)
                    out_ref[:, at + 2 * LANES : at + 3 * LANES] = out[1][ROW_K : ROW_K + ADAPTER_RANK].astype(out_ref.dtype)
                    out_ref[:, at + 3 * LANES : at + 4 * LANES] = out[2][ROW_V : ROW_V + ADAPTER_RANK].astype(out_ref.dtype)

    prepare(0)
    for j in columns:
        score(0, j)

    if alone:

        @pl.when(step == 0)
        def _():
            gradient_copy().wait()

        for g in range(step_units):
            weight_copy(step * step_units + g).wait()
    cotangent(0)
    for i in range(len(units) + 1):
        if i < len(units):
            state[i]["top"] = jnp.max(state[i]["peak"], axis=1, keepdims=True)
        if i + 1 < len(units):
            prepare(i + 1)
            cotangent(i + 1)
        for j in columns:
            if i < len(units):
                weigh(i, j)
            if i + 1 < len(units):
                score(i + 1, j)
            if i > 0:
                back(i - 1, j)
        if i < len(units):
            weighed(i)
        if i > 0:
            backed(i - 1)


def attend(queries, gradient, weight, recv, own, packs, ext, table, starts, first, skip, steps, units, before):
    rows, depth = gradient.shape
    tile = rows // 2
    keys = LOOKBACK_SPAN + tile
    base = 0 if before is None else before.shape[1]
    groups = steps * units
    col = lambda width, fn: pl.BlockSpec((rows, width), fn)
    total = base + 4 * LANES * groups
    wide = units * LANES
    alone = own is None
    source = [gradient, weight] if alone else [own]
    operands = [queries, *source, recv, *packs, *packs, ext, table, starts]
    in_specs = (
        [
            col(2 * wide, lambda g, off: (0, g + skip)),
            *([pl.BlockSpec(memory_space=pl.ANY)] * 2 if alone else [col(2 * wide, lambda g, off: (0, g))]),
            col(2 * wide, lambda g, off: (0, g)),
        ]
        + [col(wide, lambda g, off: (0, 2 * g))] * 3
        + [col(wide, lambda g, off: (0, 2 * g + 1))] * 3
        + [
            pl.BlockSpec((3 * rows, LANES), lambda g, off: (0, 0)),
            pl.BlockSpec((TABLE, rows), lambda g, off: (0, 0)),
            pl.BlockSpec((rows, LANES), lambda g, off: (0, 0)),
        ]
    )
    if base:
        operands.append(before)
        in_specs.append(pl.BlockSpec((ADAPTER_RANK, base), lambda g, off: (0, 0)))
    pushes = rows * groups * 2 * keys // 256 * 4
    return pl.pallas_call(
        functools.partial(attend_body, steps, units, base, alone),
        grid_spec=pltpu.PrefetchScalarGridSpec(
            num_scalar_prefetch=1,
            grid=(steps,),
            in_specs=in_specs,
            out_specs=pl.BlockSpec((ADAPTER_RANK, total), lambda g, off: (0, 0)),
            scratch_shapes=[
                pltpu.VMEM((2, 2 * tile, keys), jnp.float32),
                pltpu.VMEM((2, 2 * tile, keys), jnp.bfloat16),
                pltpu.VMEM((2, 3 * rows, 2 * LANES), jnp.bfloat16),
                pltpu.VMEM((2, 3 * rows, 2 * LANES), jnp.bfloat16),
                pltpu.VMEM((2, rows, 2 * LANES), jnp.bfloat16),
            ]
            + alone
            * [
                pltpu.VMEM((rows, depth), jnp.bfloat16),
                pltpu.VMEM((groups, 2 * LANES, depth), jnp.bfloat16),
                pltpu.SemaphoreType.DMA((1 + groups,)),
            ],
        ),
        out_shape=jax.ShapeDtypeStruct((ADAPTER_RANK, total), jnp.bfloat16),
        cost_estimate=pl.CostEstimate(
            flops=pushes * 256 * 256 * 2 + alone * 2 * rows * depth * 2 * LANES * groups,
            bytes_accessed=groups * rows * LANES * 20 + 4 * LANES * groups * depth,
            transcendentals=rows * groups * 2 * keys,
        ),
        compiler_params=pltpu.CompilerParams(vmem_limit_bytes=GRANT),
    )(first, *operands)


def finish_body(*refs):
    q_ref, k_ref, v_ref = refs[-3:]
    mine = refs[0][...].astype(jnp.float32) + refs[1][...].astype(jnp.float32)
    total = refs[2][0:1, 0:1] + refs[3][0:1, 0:1]
    count = float(ADAPTER_RANK * (QUERY_HEADS + 2 * KEY_VALUE_HEADS) * HEAD_SIZE)
    mine = mine * jnp.sqrt(count / (total + 1e-06))
    for g in range(k_ref.shape[1] // LANES):
        at = 4 * LANES * g
        q_ref[:, 2 * LANES * g : 2 * LANES * (g + 1)] = mine[:, at : at + 2 * LANES]
        k_ref[:, LANES * g : LANES * (g + 1)] = mine[:, at + 2 * LANES : at + 3 * LANES]
        v_ref[:, LANES * g : LANES * (g + 1)] = mine[:, at + 3 * LANES : at + 4 * LANES]


def local(
    layer_input,
    norm_weight,
    document_index,
    stored_queries,
    stored_keys,
    stored_values,
    output_weight,
    projection_gradient,
    adapter_down_maps,
):
    rows = stored_queries.shape[0]
    heads_width = stored_queries.shape[1]
    groups = stored_keys.shape[1] // HEAD_SIZE
    tp, ctx = lax.axis_size("tp"), lax.axis_size("ctx")
    tp_at, ctx_at = lax.axis_index("tp"), lax.axis_index("ctx")
    chunks = 2 if groups % 4 == 0 else 1
    units = chunks
    steps = groups // (chunks * units)
    width = 2 * LANES
    half = heads_width // width
    per = half // chunks
    scalar = lambda value: jnp.asarray(value, jnp.int32).reshape(1)

    packs = [pack_call(stored_keys, stored_values, units * LANES, steps)]

    received = []
    for c in range(chunks):
        got = []
        for d in range(1, tp):
            first = scalar(((tp_at + d) % tp) * half + c * per)
            if c == 0 and d == 1:
                part, low = open_call(
                    projection_gradient,
                    output_weight,
                    first,
                    per,
                    width,
                    layer_input,
                    norm_weight[None, :],
                    adapter_down_maps.T,
                )
            else:
                if d == 1:
                    part, pack = project(
                        projection_gradient,
                        output_weight,
                        first,
                        per,
                        width,
                        stored_keys,
                        stored_values,
                        units * LANES,
                        c * steps,
                    )
                    packs.append(pack)
                else:
                    (part,) = project(projection_gradient, output_weight, first, per, width)
            got.append(lax.ppermute(part, "tp", [(at, (at + d) % tp) for at in range(tp)]))
        total = got[0]
        if len(got) > 1:
            total = sum(one.astype(jnp.float32) for one in got)
        received.append(total)

    move = 1
    while 2 * move < tp:
        low = low + xor_move(low, "tp", move)
        move *= 2
    other = xor_move(low, "tp", move)
    table = pl.pallas_call(
        table_body, out_shape=jax.ShapeDtypeStruct((TABLE, rows), jnp.bfloat16), compiler_params=SMALL
    )(
        low, other, document_index[None, :]
    )
    table2 = shifted(table, "ctx", 2)
    table1 = shifted(table, "ctx", 1)
    prepare = pl.pallas_call(
        prep_body,
        grid_spec=pltpu.PrefetchScalarGridSpec(
            num_scalar_prefetch=1,
            grid=(1,),
            in_specs=[pl.BlockSpec((TABLE, rows), lambda i, off: (0, 0))] * 3,
            out_specs=[
                pl.BlockSpec((3 * rows, LANES), lambda i, off: (0, 0)),
                pl.BlockSpec((rows, LANES), lambda i, off: (0, 0)),
            ],
        ),
        out_shape=[
            jax.ShapeDtypeStruct((3 * rows, LANES), jnp.bfloat16),
            jax.ShapeDtypeStruct((rows, LANES), jnp.int32),
        ],
        compiler_params=SMALL,
    )
    ext, starts = prepare(scalar(2 * rows - ctx_at * rows), table2, table1, table)

    second = (ctx_at % 2) == 1
    sums = None
    for c in range(chunks):
        far = shifted(packs[c], "ctx", 2)
        if c == 0:
            picked = jnp.where(second, far, packs[c])
            near = xor_move(picked, "ctx", 1)
        else:
            near = shifted(packs[c], "ctx", 1)
        first = scalar((tp_at * half + c * per) // units)
        sums = attend(
            stored_queries,
            projection_gradient,
            output_weight,
            received[c],
            None,
            (far, near, packs[c]),
            ext,
            table,
            starts,
            first,
            c * steps,
            steps,
            units,
            sums,
        )

    def joined(*parts):
        wide = [part.astype(jnp.float32) for part in parts]
        total = wide[0] + wide[1]
        return total if len(parts) == 2 else total + (wide[2] + wide[3])

    sums = joined(sums, xor_move(sums, "ctx", 1)).astype(jnp.bfloat16)
    sums = joined(sums, *[xor_move(sums, "ctx", move) for move in (2, 4, 6)]).astype(jnp.bfloat16)
    move = 8
    while 2 * move < ctx:
        sums = joined(sums, xor_move(sums, "ctx", move)).astype(jnp.bfloat16)
        move *= 2
    last = [sums, xor_move(sums, "ctx", move)]
    squared = jnp.sum(jnp.square(joined(*last))).reshape(1, 1)
    move = 1
    while 2 * move < tp:
        squared = squared + xor_move(squared, "tp", move)
        move *= 2
    last += [squared, xor_move(squared, "tp", move)]
    sizes = (heads_width, groups * HEAD_SIZE, groups * HEAD_SIZE)
    return pl.pallas_call(
        finish_body,
        out_shape=[jax.ShapeDtypeStruct((ADAPTER_RANK, size), jnp.float32) for size in sizes],
        compiler_params=SMALL,
    )(*last)


def solution(mesh):
    placed = (
        P("ctx", "tp"),
        P("tp"),
        P("ctx"),
        P("ctx", "tp"),
        P("ctx", "tp"),
        P("ctx", "tp"),
        P(None, "tp"),
        P("ctx", "tp"),
        P("tp", None),
    )
    return jax.shard_map(
        local,
        mesh=mesh,
        in_specs=placed,
        out_specs=(P(None, "tp"), P(None, "tp"), P(None, "tp")),
        check_vma=False,
    )
```

```python
import functools

import jax
import jax.numpy as jnp
from jax import lax
from jax.experimental import pallas as pl
from jax.experimental.pallas import tpu as pltpu
from jax.sharding import PartitionSpec as P


MODEL_WIDTH = 5376
QUERY_HEADS = 32
KEY_VALUE_HEADS = 16
HEAD_SIZE = 128
LOOKBACK_SPAN = 1024
ADAPTER_RANK = 8
LOG2E = 1.4426950408889634
SCALE = float(MODEL_WIDTH // QUERY_HEADS) ** (-0.5)
LANES = 128
GRANT = 52 << 20
SMALL = pltpu.CompilerParams(vmem_limit_bytes=8 << 20)
ROW_K, ROW_V, ROW_ONE, ROW_DOC = 0, ADAPTER_RANK, 2 * ADAPTER_RANK, 2 * ADAPTER_RANK + 1
TABLE = 4 * ADAPTER_RANK

NT = (((1,), (1,)), ((), ()))
NN = (((1,), (0,)), ((), ()))
TN = (((0,), (0,)), ((), ()))


def dotf(left, right, dims):
    return lax.dot_general(left, right, dims, preferred_element_type=jnp.float32)


def shifted(value, axis, steps):
    count = lax.axis_size(axis)
    first, last = (max(0, -steps), min(count, count - steps))
    return lax.ppermute(value, axis, [(source, source + steps) for source in range(first, last)])


def xor_move(value, axis, step):
    return lax.ppermute(value, axis, [(at, at ^ step) for at in range(lax.axis_size(axis))])


def project_body(offset_ref, gradient_ref, weight_ref, *rest):
    if len(rest) > 1:
        k_ref, v_ref, out_ref, pack_ref = rest
        wide = k_ref.shape[1]
        pack_ref[:, :wide] = k_ref[...]
        pack_ref[:, wide:] = v_ref[...]
    else:
        (out_ref,) = rest
    out_ref[...] = dotf(gradient_ref[...], weight_ref[...], NT).astype(out_ref.dtype)


def pack_body(wide, k_ref, v_ref, out_ref):
    for at in range(0, k_ref.shape[1], wide):
        out_ref[:, 2 * at : 2 * at + wide] = k_ref[:, at : at + wide]
        out_ref[:, 2 * at + wide : 2 * at + 2 * wide] = v_ref[:, at : at + wide]


def pack_call(keys, values, wide, blocks):
    rows = keys.shape[0]
    return pl.pallas_call(
        functools.partial(pack_body, wide),
        grid=(1,),
        in_specs=[pl.BlockSpec((rows, wide * blocks), lambda i: (0, 0))] * 2,
        out_specs=pl.BlockSpec((rows, 2 * wide * blocks), lambda i: (0, 0)),
        out_shape=jax.ShapeDtypeStruct((rows, 2 * wide * blocks), keys.dtype),
        compiler_params=pltpu.CompilerParams(vmem_limit_bytes=62 << 20),
    )(keys, values)


def project(gradient, weight, first_block, blocks, width, keys=None, values=None, wide=0, skip=0):
    rows, depth = gradient.shape
    out_specs = [pl.BlockSpec((rows, width), lambda i, off: (0, i))]
    out_shape = [jax.ShapeDtypeStruct((rows, blocks * width), jnp.bfloat16)]
    in_specs = [
        pl.BlockSpec((rows, depth), lambda i, off: (0, 0)),
        pl.BlockSpec((width, depth), lambda i, off: (off[0] + i, 0)),
    ]
    operands = [gradient, weight]
    if keys is not None:
        operands += [keys, values]
        in_specs += [pl.BlockSpec((rows, wide), lambda i, off: (0, i // 2 + skip))] * 2
        out_specs.append(pl.BlockSpec((rows, 2 * wide), lambda i, off: (0, i // 2)))
        out_shape.append(jax.ShapeDtypeStruct((rows, blocks * wide), keys.dtype))
    return pl.pallas_call(
        project_body,
        grid_spec=pltpu.PrefetchScalarGridSpec(
            num_scalar_prefetch=1, grid=(blocks,), in_specs=in_specs, out_specs=out_specs
        ),
        out_shape=out_shape,
        cost_estimate=pl.CostEstimate(
            flops=2 * rows * depth * width * blocks,
            bytes_accessed=2 * (rows * depth + width * blocks * depth + rows * width * blocks),
            transcendentals=0,
        ),
        compiler_params=pltpu.CompilerParams(vmem_limit_bytes=GRANT),
    )(first_block, *operands)


def open_body(offset_ref, gradient_ref, weight_ref, x_ref, norm_ref, down_ref, out_ref, low_ref):
    out_ref[...] = dotf(gradient_ref[...], weight_ref[...], NT).astype(out_ref.dtype)
    hidden = x_ref[...].astype(jnp.float32)
    weighted = (hidden * norm_ref[...].astype(jnp.float32)).astype(jnp.bfloat16)
    reduced = dotf(weighted, down_ref[...], NT)
    squares = jnp.sum(hidden * hidden, axis=1, keepdims=True)
    squares = jnp.broadcast_to(squares, (squares.shape[0], LANES - 3 * ADAPTER_RANK))
    low_ref[...] = jnp.concatenate([reduced, squares], 1).T[:TABLE]


def open_call(gradient, weight, first_block, blocks, width, x, norm, down):
    rows, depth = gradient.shape
    slab = rows // blocks
    return pl.pallas_call(
        open_body,
        grid_spec=pltpu.PrefetchScalarGridSpec(
            num_scalar_prefetch=1,
            grid=(blocks,),
            in_specs=[
                pl.BlockSpec((rows, depth), lambda i, off: (0, 0)),
                pl.BlockSpec((width, depth), lambda i, off: (off[0] + i, 0)),
                pl.BlockSpec((slab, depth), lambda i, off: (i, 0)),
                pl.BlockSpec((1, depth), lambda i, off: (0, 0)),
                pl.BlockSpec((3 * ADAPTER_RANK, depth), lambda i, off: (0, 0)),
            ],
            out_specs=[
                pl.BlockSpec((rows, width), lambda i, off: (0, i)),
                pl.BlockSpec((TABLE, slab), lambda i, off: (0, i)),
            ],
        ),
        out_shape=[
            jax.ShapeDtypeStruct((rows, blocks * width), jnp.bfloat16),
            jax.ShapeDtypeStruct((TABLE, rows), jnp.float32),
        ],
        cost_estimate=pl.CostEstimate(
            flops=2 * rows * depth * width * blocks,
            bytes_accessed=2 * (2 * rows * depth + width * blocks * depth + rows * width * blocks),
            transcendentals=0,
        ),
        compiler_params=pltpu.CompilerParams(vmem_limit_bytes=GRANT),
    )(first_block, gradient, weight, x, norm, down)


def table_body(mine_ref, theirs_ref, doc_ref, out_ref):
    joined = mine_ref[...] + theirs_ref[...]
    inverse = lax.rsqrt(joined[3 * ADAPTER_RANK : 3 * ADAPTER_RANK + 1] / float(MODEL_WIDTH) + 1e-06)
    low = joined * inverse
    rank = ADAPTER_RANK
    row = lax.broadcasted_iota(jnp.int32, (rank, low.shape[1]), 0)
    extra = jnp.where(row == 0, 1.0, jnp.where(row == 1, doc_ref[...].astype(jnp.float32), 0.0))
    out_ref[...] = jnp.concatenate([low[rank : 3 * rank], extra, low[:rank]], 0).astype(out_ref.dtype)


def prep_body(first_ref, t2_ref, t1_ref, t0_ref, ext_ref, st_ref):
    rows = t0_ref.shape[1]
    tables = [ref[...].astype(jnp.float32) for ref in (t2_ref, t1_ref, t0_ref)]
    blank = jnp.zeros((LANES - TABLE, rows), jnp.float32)
    for at, table in enumerate(tables):
        turned = jnp.concatenate([table, blank], 0).T
        ext_ref[at * rows : (at + 1) * rows, :] = turned.astype(ext_ref.dtype)
    ids = [table[ROW_DOC : ROW_DOC + 1] for table in tables]
    column = turned[:, ROW_DOC : ROW_DOC + 1]
    leading = column[0:1]
    before = sum(jnp.sum((one < leading).astype(jnp.float32), axis=1, keepdims=True) for one in ids[:2])
    inside = jnp.sum((ids[2] < column).astype(jnp.float32), axis=1, keepdims=True)
    begin = jnp.where(column > leading, inside + float(2 * rows), before).astype(jnp.int32)
    begin = jnp.broadcast_to(begin, st_ref.shape)
    band = lax.broadcasted_iota(jnp.int32, st_ref.shape, 0) + (2 * rows + 1 - LOOKBACK_SPAN)
    st_ref[...] = jnp.maximum(jnp.maximum(begin, band), first_ref[0])


def attend_body(steps, step_units, base, alone, offset_ref, q_ref, *rest):
    if alone:
        pg_hbm, w_hbm, *rest = rest
    else:
        own_ref, *rest = rest
    recv_ref, k0, k1, k2, v0, v1, v2, ext_ref, lq_ref, st_ref, *rest = rest
    if base:
        before_ref, *rest = rest
    out_ref, s_scr, e_scr, ve, ke, do_scr, *rest = rest
    if alone:
        pg_scr, w_scr, sems = rest
    rows = q_ref.shape[0]
    tile = s_scr.shape[1] // 2
    keys = s_scr.shape[2]
    width = tile
    factor = SCALE * LOG2E
    parts = rows // tile
    units = [(g, t) for g in range(step_units) for t in range(parts)]
    state = [{} for _ in units]
    columns = range(keys // width)
    step = pl.program_id(0)
    deep = 2 * LANES

    def gradient_copy():
        return pltpu.make_async_copy(pg_hbm, pg_scr, sems.at[0])

    def weight_copy(group):
        first = pl.multiple_of((offset_ref[0] * step_units + group) * deep, deep)
        return pltpu.make_async_copy(w_hbm.at[pl.ds(first, deep), :], w_scr.at[group], sems.at[1 + group])

    if alone:

        @pl.when(step == 0)
        def _():
            gradient_copy().start()
            for group in range(steps * step_units):
                weight_copy(group).start()

    if base:

        @pl.when(step == 0)
        def _():
            out_ref[:, :base] = before_ref[...]

    def prepare(i):
        g, t = units[i]
        if t == 0:
            for b, (k_ref, v_ref) in enumerate(((k0, v0), (k1, v1), (k2, v2))):
                span = slice(b * rows, (b + 1) * rows)
                ke[g % 2, span, :LANES] = k_ref[:, g * LANES : (g + 1) * LANES]
                ve[g % 2, span, :LANES] = v_ref[:, g * LANES : (g + 1) * LANES]
                ke[g % 2, span, LANES:] = ext_ref[span, :]
                ve[g % 2, span, LANES:] = ext_ref[span, :]
        s = state[i]
        r0 = t * tile
        c0 = 2 * LANES * g
        s["q"] = jnp.concatenate(
            [q_ref[r0 : r0 + tile, c0 : c0 + LANES], q_ref[r0 : r0 + tile, c0 + LANES : c0 + 2 * LANES]], 0
        )
        start = st_ref[r0 : r0 + tile, :]
        s["start"] = jnp.concatenate([start, start], 0)
        s["peak"] = None

    def cotangent(i):
        g, t = units[i]
        if t == 0:
            if alone:
                own = dotf(pg_scr[...], w_scr[step * step_units + g], NT)
            else:
                own = own_ref[:, deep * g : deep * (g + 1)]
            got = recv_ref[:, deep * g : deep * (g + 1)].astype(jnp.float32)
            do_scr[g % 2] = (own + got).astype(jnp.bfloat16)

    def score(i, j):
        g, t = units[i]
        s = state[i]
        at = t * tile + j * width
        raw = dotf(s["q"], ke[g % 2, at : at + width, :LANES], NT)
        for h in range(width // LANES):
            value = raw[:, h * LANES : (h + 1) * LANES]
            pos = lax.broadcasted_iota(jnp.int32, value.shape, 1) + (at + h * LANES)
            ok = pos >= s["start"]
            if j == len(columns) - 1:
                row = lax.broadcasted_iota(jnp.int32, value.shape, 0)
                row = jnp.where(row >= tile, row - tile, row)
                ok = ok & (pos <= row + (2 * rows + t * tile))
            value = jnp.where(ok, value, -1e30)
            s_scr[i % 2, :, j * width + h * LANES : j * width + (h + 1) * LANES] = value
            s["peak"] = value if s["peak"] is None else jnp.maximum(s["peak"], value)

    def weigh(i, j):
        g, t = units[i]
        s = state[i]
        at = t * tile + j * width
        cols = slice(j * width, (j + 1) * width)
        e = jnp.exp2((s_scr[i % 2, :, cols] - s["top"]) * factor).astype(jnp.bfloat16)
        e_scr[i % 2, :, cols] = e
        part = dotf(e, ve[g % 2, at : at + width, :], NN)
        s["acc"] = part if j == 0 else s["acc"] + part

    def weighed(i):
        g, t = units[i]
        s = state[i]
        acc = s["acc"]
        do = do_scr[g % 2, t * tile : (t + 1) * tile, :]
        s["do"] = jnp.concatenate([do[:, :LANES], do[:, LANES:]], 0)
        s["inverse"] = 1.0 / acc[:, LANES + ROW_ONE : LANES + ROW_ONE + 1]
        s["delta"] = (
            jnp.sum(s["do"].astype(jnp.float32) * acc[:, :LANES], axis=1, keepdims=True) * s["inverse"]
        )
        s["uv"] = (acc[:, LANES : LANES + ROW_ONE] * s["inverse"]).astype(jnp.bfloat16)

    def back(i, j):
        g, t = units[i]
        s = state[i]
        at = t * tile + j * width
        dp = dotf(s["do"], ve[g % 2, at : at + width, :LANES], NT)
        e = e_scr[i % 2, :, j * width : (j + 1) * width].astype(jnp.float32)
        ds = (e * (dp - s["delta"])).astype(jnp.bfloat16)
        part = dotf(ds, ke[g % 2, at : at + width, :], NN)
        s["back"] = part if j == 0 else s["back"] + part

    def backed(i):
        g, t = units[i]
        s = state[i]
        fin = (s["back"] * (s["inverse"] * SCALE)).astype(jnp.bfloat16)
        dq = jnp.concatenate([fin[:tile, :LANES], fin[tile:, :LANES]], 1)
        low_q = lq_ref[2 * ADAPTER_RANK :, t * tile : (t + 1) * tile]
        out = (dotf(low_q, dq, NN), dotf(fin[:, LANES : LANES + ROW_ONE], s["q"], TN), dotf(s["uv"], s["do"], TN))
        if t > 0:
            out = tuple(a + b for a, b in zip(out, state[i - 1]["out"]))
            state[i - 1].clear()
        s["out"] = out
        if t == parts - 1:
            for unit_step in range(steps):

                @pl.when(step == unit_step)
                def _():
                    at = base + 4 * LANES * (unit_step * step_units + g)
                    out_ref[:, at : at + 2 * LANES] = out[0][ADAPTER_RANK:].astype(out_ref.dtype)
                    out_ref[:, at + 2 * LANES : at + 3 * LANES] = out[1][ROW_K : ROW_K + ADAPTER_RANK].astype(out_ref.dtype)
                    out_ref[:, at + 3 * LANES : at + 4 * LANES] = out[2][ROW_V : ROW_V + ADAPTER_RANK].astype(out_ref.dtype)

    prepare(0)
    for j in columns:
        score(0, j)

    if alone:

        @pl.when(step == 0)
        def _():
            gradient_copy().wait()

        for g in range(step_units):
            weight_copy(step * step_units + g).wait()
    cotangent(0)
    for i in range(len(units) + 1):
        if i < len(units):
            state[i]["top"] = jnp.max(state[i]["peak"], axis=1, keepdims=True)
        if i + 1 < len(units):
            prepare(i + 1)
            cotangent(i + 1)
        for j in columns:
            if i < len(units):
                weigh(i, j)
            if i + 1 < len(units):
                score(i + 1, j)
            if i > 0:
                back(i - 1, j)
        if i < len(units):
            weighed(i)
        if i > 0:
            backed(i - 1)


def attend(queries, gradient, weight, recv, own, packs, ext, table, starts, first, skip, steps, units, before):
    rows, depth = gradient.shape
    tile = rows // 2
    keys = LOOKBACK_SPAN + tile
    base = 0 if before is None else before.shape[1]
    groups = steps * units
    col = lambda width, fn: pl.BlockSpec((rows, width), fn)
    total = base + 4 * LANES * groups
    wide = units * LANES
    alone = own is None
    source = [gradient, weight] if alone else [own]
    operands = [queries, *source, recv, *packs, *packs, ext, table, starts]
    in_specs = (
        [
            col(2 * wide, lambda g, off: (0, g + skip)),
            *([pl.BlockSpec(memory_space=pl.ANY)] * 2 if alone else [col(2 * wide, lambda g, off: (0, g))]),
            col(2 * wide, lambda g, off: (0, g)),
        ]
        + [col(wide, lambda g, off: (0, 2 * g))] * 3
        + [col(wide, lambda g, off: (0, 2 * g + 1))] * 3
        + [
            pl.BlockSpec((3 * rows, LANES), lambda g, off: (0, 0)),
            pl.BlockSpec((TABLE, rows), lambda g, off: (0, 0)),
            pl.BlockSpec((rows, LANES), lambda g, off: (0, 0)),
        ]
    )
    if base:
        operands.append(before)
        in_specs.append(pl.BlockSpec((ADAPTER_RANK, base), lambda g, off: (0, 0)))
    pushes = rows * groups * 2 * keys // 256 * 4
    return pl.pallas_call(
        functools.partial(attend_body, steps, units, base, alone),
        grid_spec=pltpu.PrefetchScalarGridSpec(
            num_scalar_prefetch=1,
            grid=(steps,),
            in_specs=in_specs,
            out_specs=pl.BlockSpec((ADAPTER_RANK, total), lambda g, off: (0, 0)),
            scratch_shapes=[
                pltpu.VMEM((2, 2 * tile, keys), jnp.float32),
                pltpu.VMEM((2, 2 * tile, keys), jnp.bfloat16),
                pltpu.VMEM((2, 3 * rows, 2 * LANES), jnp.bfloat16),
                pltpu.VMEM((2, 3 * rows, 2 * LANES), jnp.bfloat16),
                pltpu.VMEM((2, rows, 2 * LANES), jnp.bfloat16),
            ]
            + alone
            * [
                pltpu.VMEM((rows, depth), jnp.bfloat16),
                pltpu.VMEM((groups, 2 * LANES, depth), jnp.bfloat16),
                pltpu.SemaphoreType.DMA((1 + groups,)),
            ],
        ),
        out_shape=jax.ShapeDtypeStruct((ADAPTER_RANK, total), jnp.bfloat16),
        cost_estimate=pl.CostEstimate(
            flops=pushes * 256 * 256 * 2 + alone * 2 * rows * depth * 2 * LANES * groups,
            bytes_accessed=groups * rows * LANES * 20 + 4 * LANES * groups * depth,
            transcendentals=rows * groups * 2 * keys,
        ),
        compiler_params=pltpu.CompilerParams(vmem_limit_bytes=GRANT),
    )(first, *operands)


def square_body(mine_ref, theirs_ref, out_ref):
    mine = mine_ref[...].astype(jnp.float32) + theirs_ref[...].astype(jnp.float32)
    out_ref[...] = sum(jnp.square(mine[:, at : at + LANES]) for at in range(0, mine.shape[1], LANES))


def finish_body(*refs):
    q_ref, k_ref, v_ref = refs[-3:]
    mine = refs[0][...].astype(jnp.float32) + refs[1][...].astype(jnp.float32)
    total = jnp.sum(refs[2][...] + refs[3][...], keepdims=True)
    count = float(ADAPTER_RANK * (QUERY_HEADS + 2 * KEY_VALUE_HEADS) * HEAD_SIZE)
    mine = mine * jnp.sqrt(count / (total + 1e-06))
    for g in range(k_ref.shape[1] // LANES):
        at = 4 * LANES * g
        q_ref[:, 2 * LANES * g : 2 * LANES * (g + 1)] = mine[:, at : at + 2 * LANES]
        k_ref[:, LANES * g : LANES * (g + 1)] = mine[:, at + 2 * LANES : at + 3 * LANES]
        v_ref[:, LANES * g : LANES * (g + 1)] = mine[:, at + 3 * LANES : at + 4 * LANES]


def local(
    layer_input,
    norm_weight,
    document_index,
    stored_queries,
    stored_keys,
    stored_values,
    output_weight,
    projection_gradient,
    adapter_down_maps,
):
    rows = stored_queries.shape[0]
    heads_width = stored_queries.shape[1]
    groups = stored_keys.shape[1] // HEAD_SIZE
    tp, ctx = lax.axis_size("tp"), lax.axis_size("ctx")
    tp_at, ctx_at = lax.axis_index("tp"), lax.axis_index("ctx")
    chunks = 2 if groups % 4 == 0 else 1
    units = chunks
    steps = groups // (chunks * units)
    width = 2 * LANES
    half = heads_width // width
    per = half // chunks
    scalar = lambda value: jnp.asarray(value, jnp.int32).reshape(1)

    packs = [pack_call(stored_keys, stored_values, units * LANES, steps)]

    received = []
    for c in range(chunks):
        got = []
        for d in range(1, tp):
            first = scalar(((tp_at + d) % tp) * half + c * per)
            if c == 0 and d == 1:
                part, low = open_call(
                    projection_gradient,
                    output_weight,
                    first,
                    per,
                    width,
                    layer_input,
                    norm_weight[None, :],
                    adapter_down_maps.T,
                )
            else:
                if d == 1:
                    part, pack = project(
                        projection_gradient,
                        output_weight,
                        first,
                        per,
                        width,
                        stored_keys,
                        stored_values,
                        units * LANES,
                        c * steps,
                    )
                    packs.append(pack)
                else:
                    (part,) = project(projection_gradient, output_weight, first, per, width)
            got.append(lax.ppermute(part, "tp", [(at, (at + d) % tp) for at in range(tp)]))
        total = got[0]
        if len(got) > 1:
            total = sum(one.astype(jnp.float32) for one in got)
        received.append(total)

    move = 1
    while 2 * move < tp:
        low = low + xor_move(low, "tp", move)
        move *= 2
    other = xor_move(low, "tp", move)
    table = pl.pallas_call(
        table_body, out_shape=jax.ShapeDtypeStruct((TABLE, rows), jnp.bfloat16), compiler_params=SMALL
    )(
        low, other, document_index[None, :]
    )
    table2 = shifted(table, "ctx", 2)
    table1 = shifted(table, "ctx", 1)
    prepare = pl.pallas_call(
        prep_body,
        grid_spec=pltpu.PrefetchScalarGridSpec(
            num_scalar_prefetch=1,
            grid=(1,),
            in_specs=[pl.BlockSpec((TABLE, rows), lambda i, off: (0, 0))] * 3,
            out_specs=[
                pl.BlockSpec((3 * rows, LANES), lambda i, off: (0, 0)),
                pl.BlockSpec((rows, LANES), lambda i, off: (0, 0)),
            ],
        ),
        out_shape=[
            jax.ShapeDtypeStruct((3 * rows, LANES), jnp.bfloat16),
            jax.ShapeDtypeStruct((rows, LANES), jnp.int32),
        ],
        compiler_params=SMALL,
    )
    ext, starts = prepare(scalar(2 * rows - ctx_at * rows), table2, table1, table)

    second = (ctx_at % 2) == 1
    sums = None
    for c in range(chunks):
        far = shifted(packs[c], "ctx", 2)
        if c == 0:
            picked = jnp.where(second, far, packs[c])
            near = xor_move(picked, "ctx", 1)
        else:
            near = shifted(packs[c], "ctx", 1)
        first = scalar((tp_at * half + c * per) // units)
        sums = attend(
            stored_queries,
            projection_gradient,
            output_weight,
            received[c],
            None,
            (far, near, packs[c]),
            ext,
            table,
            starts,
            first,
            c * steps,
            steps,
            units,
            sums,
        )

    def joined(*parts):
        wide = [part.astype(jnp.float32) for part in parts]
        total = wide[0] + wide[1]
        return total if len(parts) == 2 else total + (wide[2] + wide[3])

    sums = joined(sums, xor_move(sums, "ctx", 1)).astype(jnp.bfloat16)
    sums = joined(sums, *[xor_move(sums, "ctx", move) for move in (2, 4, 6)]).astype(jnp.bfloat16)
    move = 8
    while 2 * move < ctx:
        sums = joined(sums, xor_move(sums, "ctx", move)).astype(jnp.bfloat16)
        move *= 2
    last = [sums, xor_move(sums, "ctx", move)]
    squared = pl.pallas_call(
        square_body, out_shape=jax.ShapeDtypeStruct((ADAPTER_RANK, LANES), jnp.float32), compiler_params=SMALL
    )(*last)
    move = 1
    while 2 * move < tp:
        squared = squared + xor_move(squared, "tp", move)
        move *= 2
    last += [squared, xor_move(squared, "tp", move)]
    sizes = (heads_width, groups * HEAD_SIZE, groups * HEAD_SIZE)
    return pl.pallas_call(
        finish_body,
        out_shape=[jax.ShapeDtypeStruct((ADAPTER_RANK, size), jnp.float32) for size in sizes],
        compiler_params=SMALL,
    )(*last)


def solution(mesh):
    placed = (
        P("ctx", "tp"),
        P("tp"),
        P("ctx"),
        P("ctx", "tp"),
        P("ctx", "tp"),
        P("ctx", "tp"),
        P(None, "tp"),
        P("ctx", "tp"),
        P("tp", None),
    )
    return jax.shard_map(
        local,
        mesh=mesh,
        in_specs=placed,
        out_specs=(P(None, "tp"), P(None, "tp"), P(None, "tp")),
        check_vma=False,
    )
```

```python
import functools

import jax
import jax.numpy as jnp
from jax import lax
from jax.experimental import pallas as pl
from jax.experimental.pallas import tpu as pltpu
from jax.sharding import PartitionSpec as P


MODEL_WIDTH = 5376
QUERY_HEADS = 32
KEY_VALUE_HEADS = 16
HEAD_SIZE = 128
LOOKBACK_SPAN = 1024
ADAPTER_RANK = 8
LOG2E = 1.4426950408889634
SCALE = float(MODEL_WIDTH // QUERY_HEADS) ** (-0.5)
LANES = 128
GRANT = 52 << 20
SMALL = pltpu.CompilerParams(vmem_limit_bytes=8 << 20)
ROW_K, ROW_V, ROW_ONE, ROW_DOC = 0, ADAPTER_RANK, 2 * ADAPTER_RANK, 2 * ADAPTER_RANK + 1
TABLE = 4 * ADAPTER_RANK

NT = (((1,), (1,)), ((), ()))
NN = (((1,), (0,)), ((), ()))
TN = (((0,), (0,)), ((), ()))


def dotf(left, right, dims):
    return lax.dot_general(left, right, dims, preferred_element_type=jnp.float32)


def shifted(value, axis, steps):
    count = lax.axis_size(axis)
    first, last = (max(0, -steps), min(count, count - steps))
    return lax.ppermute(value, axis, [(source, source + steps) for source in range(first, last)])


def xor_move(value, axis, step):
    return lax.ppermute(value, axis, [(at, at ^ step) for at in range(lax.axis_size(axis))])


def project_body(offset_ref, gradient_ref, weight_ref, *rest):
    if len(rest) > 1:
        k_ref, v_ref, out_ref, pack_ref = rest
        wide = k_ref.shape[1]
        pack_ref[:, :wide] = k_ref[...]
        pack_ref[:, wide:] = v_ref[...]
    else:
        (out_ref,) = rest
    out_ref[...] = dotf(gradient_ref[...], weight_ref[...], NT).astype(out_ref.dtype)


def pack_body(wide, k_ref, v_ref, out_ref):
    for at in range(0, k_ref.shape[1], wide):
        out_ref[:, 2 * at : 2 * at + wide] = k_ref[:, at : at + wide]
        out_ref[:, 2 * at + wide : 2 * at + 2 * wide] = v_ref[:, at : at + wide]


def pack_call(keys, values, wide, blocks):
    rows = keys.shape[0]
    return pl.pallas_call(
        functools.partial(pack_body, wide),
        grid=(blocks,),
        in_specs=[pl.BlockSpec((rows, wide), lambda i: (0, i))] * 2,
        out_specs=pl.BlockSpec((rows, 2 * wide), lambda i: (0, i)),
        out_shape=jax.ShapeDtypeStruct((rows, 2 * wide * blocks), keys.dtype),
        compiler_params=pltpu.CompilerParams(vmem_limit_bytes=62 << 20),
    )(keys, values)


def project(gradient, weight, first_block, blocks, width, keys=None, values=None, wide=0, skip=0):
    rows, depth = gradient.shape
    out_specs = [pl.BlockSpec((rows, width), lambda i, off: (0, i))]
    out_shape = [jax.ShapeDtypeStruct((rows, blocks * width), jnp.bfloat16)]
    in_specs = [
        pl.BlockSpec((rows, depth), lambda i, off: (0, 0)),
        pl.BlockSpec((width, depth), lambda i, off: (off[0] + i, 0)),
    ]
    operands = [gradient, weight]
    if keys is not None:
        operands += [keys, values]
        in_specs += [pl.BlockSpec((rows, wide), lambda i, off: (0, i // 2 + skip))] * 2
        out_specs.append(pl.BlockSpec((rows, 2 * wide), lambda i, off: (0, i // 2)))
        out_shape.append(jax.ShapeDtypeStruct((rows, blocks * wide), keys.dtype))
    return pl.pallas_call(
        project_body,
        grid_spec=pltpu.PrefetchScalarGridSpec(
            num_scalar_prefetch=1, grid=(blocks,), in_specs=in_specs, out_specs=out_specs
        ),
        out_shape=out_shape,
        cost_estimate=pl.CostEstimate(
            flops=2 * rows * depth * width * blocks,
            bytes_accessed=2 * (rows * depth + width * blocks * depth + rows * width * blocks),
            transcendentals=0,
        ),
        compiler_params=pltpu.CompilerParams(vmem_limit_bytes=GRANT),
    )(first_block, *operands)


def open_body(offset_ref, gradient_ref, weight_ref, x_ref, norm_ref, down_ref, out_ref, low_ref):
    out_ref[...] = dotf(gradient_ref[...], weight_ref[...], NT).astype(out_ref.dtype)
    hidden = x_ref[...].astype(jnp.float32)
    weighted = (hidden * norm_ref[...].astype(jnp.float32)).astype(jnp.bfloat16)
    reduced = dotf(weighted, down_ref[...], NT)
    squares = jnp.sum(hidden * hidden, axis=1, keepdims=True)
    squares = jnp.broadcast_to(squares, (squares.shape[0], LANES - 3 * ADAPTER_RANK))
    low_ref[...] = jnp.concatenate([reduced, squares], 1).T[:TABLE]


def open_call(gradient, weight, first_block, blocks, width, x, norm, down):
    rows, depth = gradient.shape
    slab = rows // blocks
    return pl.pallas_call(
        open_body,
        grid_spec=pltpu.PrefetchScalarGridSpec(
            num_scalar_prefetch=1,
            grid=(blocks,),
            in_specs=[
                pl.BlockSpec((rows, depth), lambda i, off: (0, 0)),
                pl.BlockSpec((width, depth), lambda i, off: (off[0] + i, 0)),
                pl.BlockSpec((slab, depth), lambda i, off: (i, 0)),
                pl.BlockSpec((1, depth), lambda i, off: (0, 0)),
                pl.BlockSpec((3 * ADAPTER_RANK, depth), lambda i, off: (0, 0)),
            ],
            out_specs=[
                pl.BlockSpec((rows, width), lambda i, off: (0, i)),
                pl.BlockSpec((TABLE, slab), lambda i, off: (0, i)),
            ],
        ),
        out_shape=[
            jax.ShapeDtypeStruct((rows, blocks * width), jnp.bfloat16),
            jax.ShapeDtypeStruct((TABLE, rows), jnp.float32),
        ],
        cost_estimate=pl.CostEstimate(
            flops=2 * rows * depth * width * blocks,
            bytes_accessed=2 * (2 * rows * depth + width * blocks * depth + rows * width * blocks),
            transcendentals=0,
        ),
        compiler_params=pltpu.CompilerParams(vmem_limit_bytes=GRANT),
    )(first_block, gradient, weight, x, norm, down)


def table_body(mine_ref, theirs_ref, doc_ref, out_ref):
    joined = mine_ref[...] + theirs_ref[...]
    inverse = lax.rsqrt(joined[3 * ADAPTER_RANK : 3 * ADAPTER_RANK + 1] / float(MODEL_WIDTH) + 1e-06)
    low = joined * inverse
    rank = ADAPTER_RANK
    row = lax.broadcasted_iota(jnp.int32, (rank, low.shape[1]), 0)
    extra = jnp.where(row == 0, 1.0, jnp.where(row == 1, doc_ref[...].astype(jnp.float32), 0.0))
    out_ref[...] = jnp.concatenate([low[rank : 3 * rank], extra, low[:rank]], 0).astype(out_ref.dtype)


def pick_body(second_ref, far_ref, own_ref, there_ref, here_ref, out_ref):
    rows = far_ref.shape[0]

    @pl.when(second_ref[0] == 1)
    def _():
        out_ref[:rows, :] = far_ref[...]
        out_ref[rows:, :] = there_ref[...]

    @pl.when(second_ref[0] != 1)
    def _():
        out_ref[:rows, :] = own_ref[...]
        out_ref[rows:, :] = here_ref[...]


def pick_call(second, far, own, there, here):
    rows, span = own.shape
    width = 2 * LANES
    last = here.shape[1] // width - 1
    side = pl.BlockSpec((TABLE, width), lambda i, sec: (0, jnp.minimum(i, last)))
    return pl.pallas_call(
        pick_body,
        grid_spec=pltpu.PrefetchScalarGridSpec(
            num_scalar_prefetch=1,
            grid=(span // width,),
            in_specs=[
                pl.BlockSpec((rows, width), lambda i, sec: (0, i * sec[0])),
                pl.BlockSpec((rows, width), lambda i, sec: (0, i * (1 - sec[0]))),
                side,
                side,
            ],
            out_specs=pl.BlockSpec((rows + TABLE, width), lambda i, sec: (0, i)),
        ),
        out_shape=jax.ShapeDtypeStruct((rows + TABLE, span), own.dtype),
        compiler_params=pltpu.CompilerParams(vmem_limit_bytes=GRANT),
    )(second, far, own, there, here)


def prep_body(first_ref, t2_ref, t1_ref, t0_ref, ext_ref, st_ref):
    rows = t0_ref.shape[1]
    tables = [ref[...].astype(jnp.float32) for ref in (t2_ref, t1_ref, t0_ref)]
    blank = jnp.zeros((LANES - TABLE, rows), jnp.float32)
    for at, table in enumerate(tables):
        turned = jnp.concatenate([table, blank], 0).T
        ext_ref[at * rows : (at + 1) * rows, :] = turned.astype(ext_ref.dtype)
    ids = [table[ROW_DOC : ROW_DOC + 1] for table in tables]
    column = turned[:, ROW_DOC : ROW_DOC + 1]
    leading = column[0:1]
    before = sum(jnp.sum((one < leading).astype(jnp.float32), axis=1, keepdims=True) for one in ids[:2])
    inside = jnp.sum((ids[2] < column).astype(jnp.float32), axis=1, keepdims=True)
    begin = jnp.where(column > leading, inside + float(2 * rows), before).astype(jnp.int32)
    begin = jnp.broadcast_to(begin, st_ref.shape)
    band = lax.broadcasted_iota(jnp.int32, st_ref.shape, 0) + (2 * rows + 1 - LOOKBACK_SPAN)
    st_ref[...] = jnp.maximum(jnp.maximum(begin, band), first_ref[0])


def attend_body(steps, step_units, base, alone, offset_ref, q_ref, *rest):
    if alone:
        pg_hbm, w_hbm, *rest = rest
    else:
        own_ref, *rest = rest
    recv_ref, k0, k1, k2, v0, v1, v2, ext_ref, lq_ref, st_ref, *rest = rest
    if base:
        before_ref, *rest = rest
    out_ref, s_scr, e_scr, ve, ke, do_scr, *rest = rest
    if alone:
        pg_scr, w_scr, sems = rest
    rows = q_ref.shape[0]
    tile = s_scr.shape[1] // 2
    keys = s_scr.shape[2]
    width = tile
    factor = SCALE * LOG2E
    parts = rows // tile
    units = [(g, t) for g in range(step_units) for t in range(parts)]
    state = [{} for _ in units]
    columns = range(keys // width)
    step = pl.program_id(0)
    deep = 2 * LANES

    def gradient_copy():
        return pltpu.make_async_copy(pg_hbm, pg_scr, sems.at[0])

    def weight_copy(group):
        first = pl.multiple_of((offset_ref[0] * step_units + group) * deep, deep)
        return pltpu.make_async_copy(w_hbm.at[pl.ds(first, deep), :], w_scr.at[group], sems.at[1 + group])

    if alone:

        @pl.when(step == 0)
        def _():
            gradient_copy().start()
            for group in range(steps * step_units):
                weight_copy(group).start()

    if base:

        @pl.when(step == 0)
        def _():
            out_ref[:, :base] = before_ref[...]

    def prepare(i):
        g, t = units[i]
        if t == 0:
            for b, (k_ref, v_ref) in enumerate(((k0, v0), (k1, v1), (k2, v2))):
                span = slice(b * rows, (b + 1) * rows)
                ke[g % 2, span, :LANES] = k_ref[:, g * LANES : (g + 1) * LANES]
                ve[g % 2, span, :LANES] = v_ref[:, g * LANES : (g + 1) * LANES]
                ke[g % 2, span, LANES:] = ext_ref[span, :]
                ve[g % 2, span, LANES:] = ext_ref[span, :]
        s = state[i]
        r0 = t * tile
        c0 = 2 * LANES * g
        s["q"] = jnp.concatenate(
            [q_ref[r0 : r0 + tile, c0 : c0 + LANES], q_ref[r0 : r0 + tile, c0 + LANES : c0 + 2 * LANES]], 0
        )
        start = st_ref[r0 : r0 + tile, :]
        s["start"] = jnp.concatenate([start, start], 0)
        s["peak"] = None

    def cotangent(i):
        g, t = units[i]
        if t == 0:
            if alone:
                own = dotf(pg_scr[...], w_scr[step * step_units + g], NT)
            else:
                own = own_ref[:, deep * g : deep * (g + 1)]
            got = recv_ref[:, deep * g : deep * (g + 1)].astype(jnp.float32)
            do_scr[g % 2] = (own + got).astype(jnp.bfloat16)

    def score(i, j):
        g, t = units[i]
        s = state[i]
        at = t * tile + j * width
        raw = dotf(s["q"], ke[g % 2, at : at + width, :LANES], NT)
        for h in range(width // LANES):
            value = raw[:, h * LANES : (h + 1) * LANES]
            pos = lax.broadcasted_iota(jnp.int32, value.shape, 1) + (at + h * LANES)
            ok = pos >= s["start"]
            if j == len(columns) - 1:
                row = lax.broadcasted_iota(jnp.int32, value.shape, 0)
                row = jnp.where(row >= tile, row - tile, row)
                ok = ok & (pos <= row + (2 * rows + t * tile))
            value = jnp.where(ok, value, -1e30)
            s_scr[i % 2, :, j * width + h * LANES : j * width + (h + 1) * LANES] = value
            s["peak"] = value if s["peak"] is None else jnp.maximum(s["peak"], value)

    def weigh(i, j):
        g, t = units[i]
        s = state[i]
        at = t * tile + j * width
        cols = slice(j * width, (j + 1) * width)
        e = jnp.exp2((s_scr[i % 2, :, cols] - s["top"]) * factor).astype(jnp.bfloat16)
        e_scr[i % 2, :, cols] = e
        part = dotf(e, ve[g % 2, at : at + width, :], NN)
        s["acc"] = part if j == 0 else s["acc"] + part

    def weighed(i):
        g, t = units[i]
        s = state[i]
        acc = s["acc"]
        do = do_scr[g % 2, t * tile : (t + 1) * tile, :]
        s["do"] = jnp.concatenate([do[:, :LANES], do[:, LANES:]], 0)
        s["inverse"] = 1.0 / acc[:, LANES + ROW_ONE : LANES + ROW_ONE + 1]
        s["delta"] = (
            jnp.sum(s["do"].astype(jnp.float32) * acc[:, :LANES], axis=1, keepdims=True) * s["inverse"]
        )
        s["uv"] = (acc[:, LANES : LANES + ROW_ONE] * s["inverse"]).astype(jnp.bfloat16)

    def back(i, j):
        g, t = units[i]
        s = state[i]
        at = t * tile + j * width
        dp = dotf(s["do"], ve[g % 2, at : at + width, :LANES], NT)
        e = e_scr[i % 2, :, j * width : (j + 1) * width].astype(jnp.float32)
        ds = (e * (dp - s["delta"])).astype(jnp.bfloat16)
        part = dotf(ds, ke[g % 2, at : at + width, :], NN)
        s["back"] = part if j == 0 else s["back"] + part

    def backed(i):
        g, t = units[i]
        s = state[i]
        fin = (s["back"] * (s["inverse"] * SCALE)).astype(jnp.bfloat16)
        dq = jnp.concatenate([fin[:tile, :LANES], fin[tile:, :LANES]], 1)
        low_q = lq_ref[2 * ADAPTER_RANK :, t * tile : (t + 1) * tile]
        out = (dotf(low_q, dq, NN), dotf(fin[:, LANES : LANES + ROW_ONE], s["q"], TN), dotf(s["uv"], s["do"], TN))
        if t > 0:
            out = tuple(a + b for a, b in zip(out, state[i - 1]["out"]))
            state[i - 1].clear()
        s["out"] = out
        if t == parts - 1:
            for unit_step in range(steps):

                @pl.when(step == unit_step)
                def _():
                    at = base + 4 * LANES * (unit_step * step_units + g)
                    out_ref[:, at : at + 2 * LANES] = out[0][ADAPTER_RANK:].astype(out_ref.dtype)
                    out_ref[:, at + 2 * LANES : at + 3 * LANES] = out[1][ROW_K : ROW_K + ADAPTER_RANK].astype(out_ref.dtype)
                    out_ref[:, at + 3 * LANES : at + 4 * LANES] = out[2][ROW_V : ROW_V + ADAPTER_RANK].astype(out_ref.dtype)

    prepare(0)
    for j in columns:
        score(0, j)

    if alone:

        @pl.when(step == 0)
        def _():
            gradient_copy().wait()

        for g in range(step_units):
            weight_copy(step * step_units + g).wait()
    cotangent(0)
    for i in range(len(units) + 1):
        if i < len(units):
            state[i]["top"] = jnp.max(state[i]["peak"], axis=1, keepdims=True)
        if i + 1 < len(units):
            prepare(i + 1)
            cotangent(i + 1)
        for j in columns:
            if i < len(units):
                weigh(i, j)
            if i + 1 < len(units):
                score(i + 1, j)
            if i > 0:
                back(i - 1, j)
        if i < len(units):
            weighed(i)
        if i > 0:
            backed(i - 1)


def attend(queries, gradient, weight, recv, own, packs, ext, table, starts, first, skip, steps, units, before):
    rows, depth = gradient.shape
    tile = rows // 2
    keys = LOOKBACK_SPAN + tile
    base = 0 if before is None else before.shape[1]
    groups = steps * units
    col = lambda width, fn: pl.BlockSpec((rows, width), fn)
    total = base + 4 * LANES * groups
    wide = units * LANES
    alone = own is None
    source = [gradient, weight] if alone else [own]
    operands = [queries, *source, recv, *packs, *packs, ext, table, starts]
    in_specs = (
        [
            col(2 * wide, lambda g, off: (0, g + skip)),
            *([pl.BlockSpec(memory_space=pl.ANY)] * 2 if alone else [col(2 * wide, lambda g, off: (0, g))]),
            col(2 * wide, lambda g, off: (0, g)),
        ]
        + [col(wide, lambda g, off: (0, 2 * g))] * 3
        + [col(wide, lambda g, off: (0, 2 * g + 1))] * 3
        + [
            pl.BlockSpec((3 * rows, LANES), lambda g, off: (0, 0)),
            pl.BlockSpec((TABLE, rows), lambda g, off: (0, 0)),
            pl.BlockSpec((rows, LANES), lambda g, off: (0, 0)),
        ]
    )
    if base:
        operands.append(before)
        in_specs.append(pl.BlockSpec((ADAPTER_RANK, base), lambda g, off: (0, 0)))
    pushes = rows * groups * 2 * keys // 256 * 4
    return pl.pallas_call(
        functools.partial(attend_body, steps, units, base, alone),
        grid_spec=pltpu.PrefetchScalarGridSpec(
            num_scalar_prefetch=1,
            grid=(steps,),
            in_specs=in_specs,
            out_specs=pl.BlockSpec((ADAPTER_RANK, total), lambda g, off: (0, 0)),
            scratch_shapes=[
                pltpu.VMEM((2, 2 * tile, keys), jnp.float32),
                pltpu.VMEM((2, 2 * tile, keys), jnp.bfloat16),
                pltpu.VMEM((2, 3 * rows, 2 * LANES), jnp.bfloat16),
                pltpu.VMEM((2, 3 * rows, 2 * LANES), jnp.bfloat16),
                pltpu.VMEM((2, rows, 2 * LANES), jnp.bfloat16),
            ]
            + alone
            * [
                pltpu.VMEM((rows, depth), jnp.bfloat16),
                pltpu.VMEM((groups, 2 * LANES, depth), jnp.bfloat16),
                pltpu.SemaphoreType.DMA((1 + groups,)),
            ],
        ),
        out_shape=jax.ShapeDtypeStruct((ADAPTER_RANK, total), jnp.bfloat16),
        cost_estimate=pl.CostEstimate(
            flops=pushes * 256 * 256 * 2 + alone * 2 * rows * depth * 2 * LANES * groups,
            bytes_accessed=groups * rows * LANES * 20 + 4 * LANES * groups * depth,
            transcendentals=rows * groups * 2 * keys,
        ),
        compiler_params=pltpu.CompilerParams(vmem_limit_bytes=GRANT),
    )(first, *operands)


def square_body(mine_ref, theirs_ref, out_ref):
    mine = mine_ref[...].astype(jnp.float32) + theirs_ref[...].astype(jnp.float32)
    out_ref[...] = sum(jnp.square(mine[:, at : at + LANES]) for at in range(0, mine.shape[1], LANES))


def finish_body(*refs):
    q_ref, k_ref, v_ref = refs[-3:]
    mine = refs[0][...].astype(jnp.float32) + refs[1][...].astype(jnp.float32)
    total = jnp.sum(refs[2][...] + refs[3][...], keepdims=True)
    count = float(ADAPTER_RANK * (QUERY_HEADS + 2 * KEY_VALUE_HEADS) * HEAD_SIZE)
    mine = mine * jnp.sqrt(count / (total + 1e-06))
    for g in range(k_ref.shape[1] // LANES):
        at = 4 * LANES * g
        q_ref[:, 2 * LANES * g : 2 * LANES * (g + 1)] = mine[:, at : at + 2 * LANES]
        k_ref[:, LANES * g : LANES * (g + 1)] = mine[:, at + 2 * LANES : at + 3 * LANES]
        v_ref[:, LANES * g : LANES * (g + 1)] = mine[:, at + 3 * LANES : at + 4 * LANES]


def local(
    layer_input,
    norm_weight,
    document_index,
    stored_queries,
    stored_keys,
    stored_values,
    output_weight,
    projection_gradient,
    adapter_down_maps,
):
    rows = stored_queries.shape[0]
    heads_width = stored_queries.shape[1]
    groups = stored_keys.shape[1] // HEAD_SIZE
    tp, ctx = lax.axis_size("tp"), lax.axis_size("ctx")
    tp_at, ctx_at = lax.axis_index("tp"), lax.axis_index("ctx")
    chunks = 2 if groups % 4 == 0 else 1
    units = chunks
    steps = groups // (chunks * units)
    width = 2 * LANES
    half = heads_width // width
    per = half // chunks
    scalar = lambda value: jnp.asarray(value, jnp.int32).reshape(1)

    packs = [pack_call(stored_keys, stored_values, units * LANES, steps)]

    received = []
    for c in range(chunks):
        got = []
        for d in range(1, tp):
            first = scalar(((tp_at + d) % tp) * half + c * per)
            if c == 0 and d == 1:
                part, low = open_call(
                    projection_gradient,
                    output_weight,
                    first,
                    per,
                    width,
                    layer_input,
                    norm_weight[None, :],
                    adapter_down_maps.T,
                )
            else:
                if d == 1:
                    part, pack = project(
                        projection_gradient,
                        output_weight,
                        first,
                        per,
                        width,
                        stored_keys,
                        stored_values,
                        units * LANES,
                        c * steps,
                    )
                    packs.append(pack)
                else:
                    (part,) = project(projection_gradient, output_weight, first, per, width)
            got.append(lax.ppermute(part, "tp", [(at, (at + d) % tp) for at in range(tp)]))
        total = got[0]
        if len(got) > 1:
            total = sum(one.astype(jnp.float32) for one in got)
        received.append(total)

    move = 1
    while 2 * move < tp:
        low = low + xor_move(low, "tp", move)
        move *= 2
    other = xor_move(low, "tp", move)
    table = pl.pallas_call(
        table_body, out_shape=jax.ShapeDtypeStruct((TABLE, rows), jnp.bfloat16), compiler_params=SMALL
    )(
        low, other, document_index[None, :]
    )
    table2 = shifted(table, "ctx", 2)
    prepare = pl.pallas_call(
        prep_body,
        grid_spec=pltpu.PrefetchScalarGridSpec(
            num_scalar_prefetch=1,
            grid=(1,),
            in_specs=[
                pl.BlockSpec((TABLE, rows), lambda i, off: (0, 0)),
                pl.BlockSpec((TABLE, rows), lambda i, off: (rows // TABLE, 0)),
                pl.BlockSpec((TABLE, rows), lambda i, off: (0, 0)),
            ],
            out_specs=[
                pl.BlockSpec((3 * rows, LANES), lambda i, off: (0, 0)),
                pl.BlockSpec((rows, LANES), lambda i, off: (0, 0)),
            ],
        ),
        out_shape=[
            jax.ShapeDtypeStruct((3 * rows, LANES), jnp.bfloat16),
            jax.ShapeDtypeStruct((rows, LANES), jnp.int32),
        ],
        compiler_params=SMALL,
    )

    second = scalar(ctx_at % 2)
    sums = None
    for c in range(chunks):
        far = shifted(packs[c], "ctx", 2)
        if c == 0:
            picked = pick_call(second, far, packs[c], table2, table)
            near = xor_move(picked, "ctx", 1)
            ext, starts = prepare(scalar(2 * rows - ctx_at * rows), table2, near, table)
        else:
            near = shifted(packs[c], "ctx", 1)
        first = scalar((tp_at * half + c * per) // units)
        sums = attend(
            stored_queries,
            projection_gradient,
            output_weight,
            received[c],
            None,
            (far, near, packs[c]),
            ext,
            table,
            starts,
            first,
            c * steps,
            steps,
            units,
            sums,
        )

    def joined(*parts):
        wide = [part.astype(jnp.float32) for part in parts]
        total = wide[0] + wide[1]
        return total if len(parts) == 2 else total + (wide[2] + wide[3])

    sums = joined(sums, xor_move(sums, "ctx", 1)).astype(jnp.bfloat16)
    sums = joined(sums, *[xor_move(sums, "ctx", move) for move in (2, 4, 6)]).astype(jnp.bfloat16)
    move = 8
    while 2 * move < ctx:
        sums = joined(sums, xor_move(sums, "ctx", move)).astype(jnp.bfloat16)
        move *= 2
    last = [sums, xor_move(sums, "ctx", move)]
    squared = pl.pallas_call(
        square_body, out_shape=jax.ShapeDtypeStruct((ADAPTER_RANK, LANES), jnp.float32), compiler_params=SMALL
    )(*last)
    move = 1
    while 2 * move < tp:
        squared = squared + xor_move(squared, "tp", move)
        move *= 2
    last += [squared, xor_move(squared, "tp", move)]
    sizes = (heads_width, groups * HEAD_SIZE, groups * HEAD_SIZE)
    return pl.pallas_call(
        finish_body,
        out_shape=[jax.ShapeDtypeStruct((ADAPTER_RANK, size), jnp.float32) for size in sizes],
        compiler_params=SMALL,
    )(*last)


def solution(mesh):
    placed = (
        P("ctx", "tp"),
        P("tp"),
        P("ctx"),
        P("ctx", "tp"),
        P("ctx", "tp"),
        P("ctx", "tp"),
        P(None, "tp"),
        P("ctx", "tp"),
        P("tp", None),
    )
    return jax.shard_map(
        local,
        mesh=mesh,
        in_specs=placed,
        out_specs=(P(None, "tp"), P(None, "tp"), P(None, "tp")),
        check_vma=False,
    )
```

```python
import functools

import jax
import jax.numpy as jnp
from jax import lax
from jax.experimental import pallas as pl
from jax.experimental.pallas import tpu as pltpu
from jax.sharding import PartitionSpec as P


MODEL_WIDTH = 5376
QUERY_HEADS = 32
KEY_VALUE_HEADS = 16
HEAD_SIZE = 128
LOOKBACK_SPAN = 1024
ADAPTER_RANK = 8
LOG2E = 1.4426950408889634
SCALE = float(MODEL_WIDTH // QUERY_HEADS) ** (-0.5)
LANES = 128
GRANT = 52 << 20
SMALL = pltpu.CompilerParams(vmem_limit_bytes=8 << 20)
ROW_K, ROW_V, ROW_ONE, ROW_DOC = 0, ADAPTER_RANK, 2 * ADAPTER_RANK, 2 * ADAPTER_RANK + 1
TABLE = 4 * ADAPTER_RANK

NT = (((1,), (1,)), ((), ()))
NN = (((1,), (0,)), ((), ()))
TN = (((0,), (0,)), ((), ()))


def dotf(left, right, dims):
    return lax.dot_general(left, right, dims, preferred_element_type=jnp.float32)


def shifted(value, axis, steps):
    count = lax.axis_size(axis)
    first, last = (max(0, -steps), min(count, count - steps))
    return lax.ppermute(value, axis, [(source, source + steps) for source in range(first, last)])


def xor_move(value, axis, step):
    return lax.ppermute(value, axis, [(at, at ^ step) for at in range(lax.axis_size(axis))])


def project_body(offset_ref, gradient_ref, weight_ref, *rest):
    if len(rest) > 1:
        k_ref, v_ref, out_ref, pack_ref = rest
        wide = k_ref.shape[1]
        pack_ref[:, :wide] = k_ref[...]
        pack_ref[:, wide:] = v_ref[...]
    else:
        (out_ref,) = rest
    out_ref[...] = dotf(gradient_ref[...], weight_ref[...], NT).astype(out_ref.dtype)


def pack_body(wide, k_ref, v_ref, out_ref):
    for at in range(0, k_ref.shape[1], wide):
        out_ref[:, 2 * at : 2 * at + wide] = k_ref[:, at : at + wide]
        out_ref[:, 2 * at + wide : 2 * at + 2 * wide] = v_ref[:, at : at + wide]


def pack_call(keys, values, wide, blocks):
    rows = keys.shape[0]
    return pl.pallas_call(
        functools.partial(pack_body, wide),
        grid=(blocks,),
        in_specs=[pl.BlockSpec((rows, wide), lambda i: (0, i))] * 2,
        out_specs=pl.BlockSpec((rows, 2 * wide), lambda i: (0, i)),
        out_shape=jax.ShapeDtypeStruct((rows, 2 * wide * blocks), keys.dtype),
        compiler_params=pltpu.CompilerParams(vmem_limit_bytes=62 << 20),
    )(keys, values)


def project(gradient, weight, first_block, blocks, width, keys=None, values=None, wide=0, skip=0):
    rows, depth = gradient.shape
    out_specs = [pl.BlockSpec((rows, width), lambda i, off: (0, i))]
    out_shape = [jax.ShapeDtypeStruct((rows, blocks * width), jnp.bfloat16)]
    in_specs = [
        pl.BlockSpec((rows, depth), lambda i, off: (0, 0)),
        pl.BlockSpec((width, depth), lambda i, off: (off[0] + i, 0)),
    ]
    operands = [gradient, weight]
    if keys is not None:
        operands += [keys, values]
        in_specs += [pl.BlockSpec((rows, wide), lambda i, off: (0, i // 2 + skip))] * 2
        out_specs.append(pl.BlockSpec((rows, 2 * wide), lambda i, off: (0, i // 2)))
        out_shape.append(jax.ShapeDtypeStruct((rows, blocks * wide), keys.dtype))
    return pl.pallas_call(
        project_body,
        grid_spec=pltpu.PrefetchScalarGridSpec(
            num_scalar_prefetch=1, grid=(blocks,), in_specs=in_specs, out_specs=out_specs
        ),
        out_shape=out_shape,
        cost_estimate=pl.CostEstimate(
            flops=2 * rows * depth * width * blocks,
            bytes_accessed=2 * (rows * depth + width * blocks * depth + rows * width * blocks),
            transcendentals=0,
        ),
        compiler_params=pltpu.CompilerParams(vmem_limit_bytes=GRANT),
    )(first_block, *operands)


def open_body(offset_ref, gradient_ref, weight_ref, x_ref, norm_ref, down_ref, out_ref, low_ref):
    out_ref[...] = dotf(gradient_ref[...], weight_ref[...], NT).astype(out_ref.dtype)
    hidden = x_ref[...].astype(jnp.float32)
    weighted = (hidden * norm_ref[...].astype(jnp.float32)).astype(jnp.bfloat16)
    reduced = dotf(weighted, down_ref[...], NT)
    squares = jnp.sum(hidden * hidden, axis=1, keepdims=True)
    squares = jnp.broadcast_to(squares, (squares.shape[0], LANES - 3 * ADAPTER_RANK))
    low_ref[...] = jnp.concatenate([reduced, squares], 1).T[:TABLE]


def open_call(gradient, weight, first_block, blocks, width, x, norm, down):
    rows, depth = gradient.shape
    slab = rows // blocks
    return pl.pallas_call(
        open_body,
        grid_spec=pltpu.PrefetchScalarGridSpec(
            num_scalar_prefetch=1,
            grid=(blocks,),
            in_specs=[
                pl.BlockSpec((rows, depth), lambda i, off: (0, 0)),
                pl.BlockSpec((width, depth), lambda i, off: (off[0] + i, 0)),
                pl.BlockSpec((slab, depth), lambda i, off: (i, 0)),
                pl.BlockSpec((1, depth), lambda i, off: (0, 0)),
                pl.BlockSpec((3 * ADAPTER_RANK, depth), lambda i, off: (0, 0)),
            ],
            out_specs=[
                pl.BlockSpec((rows, width), lambda i, off: (0, i)),
                pl.BlockSpec((TABLE, slab), lambda i, off: (0, i)),
            ],
        ),
        out_shape=[
            jax.ShapeDtypeStruct((rows, blocks * width), jnp.bfloat16),
            jax.ShapeDtypeStruct((TABLE, rows), jnp.float32),
        ],
        cost_estimate=pl.CostEstimate(
            flops=2 * rows * depth * width * blocks,
            bytes_accessed=2 * (2 * rows * depth + width * blocks * depth + rows * width * blocks),
            transcendentals=0,
        ),
        compiler_params=pltpu.CompilerParams(vmem_limit_bytes=GRANT),
    )(first_block, gradient, weight, x, norm, down)


def table_body(mine_ref, theirs_ref, doc_ref, out_ref):
    joined = mine_ref[...] + theirs_ref[...]
    inverse = lax.rsqrt(joined[3 * ADAPTER_RANK : 3 * ADAPTER_RANK + 1] / float(MODEL_WIDTH) + 1e-06)
    low = joined * inverse
    rank = ADAPTER_RANK
    row = lax.broadcasted_iota(jnp.int32, (rank, low.shape[1]), 0)
    extra = jnp.where(row == 0, 1.0, jnp.where(row == 1, doc_ref[...].astype(jnp.float32), 0.0))
    out_ref[...] = jnp.concatenate([low[rank : 3 * rank], extra, low[:rank]], 0).astype(out_ref.dtype)


def pick_body(second_ref, far_ref, own_ref, there_ref, here_ref, out_ref):
    rows = far_ref.shape[0]

    @pl.when(second_ref[0] == 1)
    def _():
        out_ref[:rows, :] = far_ref[...]
        out_ref[rows:, :] = there_ref[...]

    @pl.when(second_ref[0] != 1)
    def _():
        out_ref[:rows, :] = own_ref[...]
        out_ref[rows:, :] = here_ref[...]


def pick_call(second, far, own, there, here):
    rows, span = own.shape
    width = 2 * LANES
    last = here.shape[1] // width - 1
    side = pl.BlockSpec((TABLE, width), lambda i, sec: (0, jnp.minimum(i, last)))
    return pl.pallas_call(
        pick_body,
        grid_spec=pltpu.PrefetchScalarGridSpec(
            num_scalar_prefetch=1,
            grid=(span // width,),
            in_specs=[
                pl.BlockSpec((rows, width), lambda i, sec: (0, i * sec[0])),
                pl.BlockSpec((rows, width), lambda i, sec: (0, i * (1 - sec[0]))),
                side,
                side,
            ],
            out_specs=pl.BlockSpec((rows + TABLE, width), lambda i, sec: (0, i)),
        ),
        out_shape=jax.ShapeDtypeStruct((rows + TABLE, span), own.dtype),
        compiler_params=pltpu.CompilerParams(vmem_limit_bytes=GRANT),
    )(second, far, own, there, here)


def prep_body(first_ref, t2_ref, t1_ref, t0_ref, ext_ref, st_ref):
    rows = t0_ref.shape[1]
    tables = [ref[...].astype(jnp.float32) for ref in (t2_ref, t1_ref, t0_ref)]
    blank = jnp.zeros((LANES - TABLE, rows), jnp.float32)
    for at, table in enumerate(tables):
        turned = jnp.concatenate([table, blank], 0).T
        ext_ref[at * rows : (at + 1) * rows, :] = turned.astype(ext_ref.dtype)
    ids = [table[ROW_DOC : ROW_DOC + 1] for table in tables]
    column = turned[:, ROW_DOC : ROW_DOC + 1]
    leading = column[0:1]
    before = sum(jnp.sum((one < leading).astype(jnp.float32), axis=1, keepdims=True) for one in ids[:2])
    inside = jnp.sum((ids[2] < column).astype(jnp.float32), axis=1, keepdims=True)
    begin = jnp.where(column > leading, inside + float(2 * rows), before).astype(jnp.int32)
    begin = jnp.broadcast_to(begin, st_ref.shape)
    band = lax.broadcasted_iota(jnp.int32, st_ref.shape, 0) + (2 * rows + 1 - LOOKBACK_SPAN)
    st_ref[...] = jnp.maximum(jnp.maximum(begin, band), first_ref[0])


def attend_body(steps, step_units, base, alone, offset_ref, q_ref, *rest):
    if alone:
        pg_hbm, w_hbm, *rest = rest
    else:
        own_ref, *rest = rest
    recv_ref, k0, k1, k2, v0, v1, v2, ext_ref, lq_ref, st_ref, *rest = rest
    if base:
        before_ref, *rest = rest
    out_ref, s_scr, e_scr, ve, ke, do_scr, *rest = rest
    if alone:
        pg_scr, w_scr, sems = rest
    rows = q_ref.shape[0]
    tile = s_scr.shape[1] // 2
    keys = s_scr.shape[2]
    width = tile
    factor = SCALE * LOG2E
    parts = rows // tile
    units = [(g, t) for g in range(step_units) for t in range(parts)]
    state = [{} for _ in units]
    columns = range(keys // width)
    step = pl.program_id(0)
    deep = 2 * LANES

    def gradient_copy():
        return pltpu.make_async_copy(pg_hbm, pg_scr, sems.at[0])

    def weight_copy(group):
        first = pl.multiple_of((offset_ref[0] * step_units + group) * deep, deep)
        return pltpu.make_async_copy(w_hbm.at[pl.ds(first, deep), :], w_scr.at[group], sems.at[1 + group])

    if alone:

        @pl.when(step == 0)
        def _():
            gradient_copy().start()
            for group in range(steps * step_units):
                weight_copy(group).start()

    if base:

        @pl.when(step == 0)
        def _():
            out_ref[:, :base] = before_ref[...]

    def prepare(i):
        g, t = units[i]
        if t == 0:
            for b, (k_ref, v_ref) in enumerate(((k0, v0), (k1, v1), (k2, v2))):
                span = slice(b * rows, (b + 1) * rows)
                ke[g % 2, span, :LANES] = k_ref[:, g * LANES : (g + 1) * LANES]
                ve[g % 2, span, :LANES] = v_ref[:, g * LANES : (g + 1) * LANES]
                ke[g % 2, span, LANES:] = ext_ref[span, :]
                ve[g % 2, span, LANES:] = ext_ref[span, :]
        s = state[i]
        r0 = t * tile
        c0 = 2 * LANES * g
        s["q"] = jnp.concatenate(
            [q_ref[r0 : r0 + tile, c0 : c0 + LANES], q_ref[r0 : r0 + tile, c0 + LANES : c0 + 2 * LANES]], 0
        )
        start = st_ref[r0 : r0 + tile, :]
        s["start"] = jnp.concatenate([start, start], 0)
        s["peak"] = None

    def cotangent(i):
        g, t = units[i]
        if t == 0:
            if alone:
                own = dotf(pg_scr[...], w_scr[step * step_units + g], NT)
            else:
                own = own_ref[:, deep * g : deep * (g + 1)]
            got = recv_ref[:, deep * g : deep * (g + 1)].astype(jnp.float32)
            do_scr[g % 2] = (own + got).astype(jnp.bfloat16)

    def score(i, j):
        g, t = units[i]
        s = state[i]
        at = t * tile + j * width
        raw = dotf(s["q"], ke[g % 2, at : at + width, :LANES], NT)
        for h in range(width // LANES):
            value = raw[:, h * LANES : (h + 1) * LANES]
            pos = lax.broadcasted_iota(jnp.int32, value.shape, 1) + (at + h * LANES)
            ok = pos >= s["start"]
            if j == len(columns) - 1:
                row = lax.broadcasted_iota(jnp.int32, value.shape, 0)
                row = jnp.where(row >= tile, row - tile, row)
                ok = ok & (pos <= row + (2 * rows + t * tile))
            value = jnp.where(ok, value, -1e30)
            s_scr[i % 2, :, j * width + h * LANES : j * width + (h + 1) * LANES] = value
            s["peak"] = value if s["peak"] is None else jnp.maximum(s["peak"], value)

    def weigh(i, j):
        g, t = units[i]
        s = state[i]
        at = t * tile + j * width
        cols = slice(j * width, (j + 1) * width)
        e = jnp.exp2((s_scr[i % 2, :, cols] - s["top"]) * factor).astype(jnp.bfloat16)
        e_scr[i % 2, :, cols] = e
        part = dotf(e, ve[g % 2, at : at + width, :], NN)
        s["acc"] = part if j == 0 else s["acc"] + part

    def weighed(i):
        g, t = units[i]
        s = state[i]
        acc = s["acc"]
        do = do_scr[g % 2, t * tile : (t + 1) * tile, :]
        s["do"] = jnp.concatenate([do[:, :LANES], do[:, LANES:]], 0)
        s["inverse"] = 1.0 / acc[:, LANES + ROW_ONE : LANES + ROW_ONE + 1]
        s["delta"] = (
            jnp.sum(s["do"].astype(jnp.float32) * acc[:, :LANES], axis=1, keepdims=True) * s["inverse"]
        )
        s["uv"] = (acc[:, LANES : LANES + ROW_ONE] * s["inverse"]).astype(jnp.bfloat16)

    def back(i, j):
        g, t = units[i]
        s = state[i]
        at = t * tile + j * width
        dp = dotf(s["do"], ve[g % 2, at : at + width, :LANES], NT)
        e = e_scr[i % 2, :, j * width : (j + 1) * width].astype(jnp.float32)
        ds = (e * (dp - s["delta"])).astype(jnp.bfloat16)
        part = dotf(ds, ke[g % 2, at : at + width, :], NN)
        s["back"] = part if j == 0 else s["back"] + part

    def backed(i):
        g, t = units[i]
        s = state[i]
        fin = (s["back"] * (s["inverse"] * SCALE)).astype(jnp.bfloat16)
        dq = jnp.concatenate([fin[:tile, :LANES], fin[tile:, :LANES]], 1)
        low_q = lq_ref[2 * ADAPTER_RANK :, t * tile : (t + 1) * tile]
        out = (dotf(low_q, dq, NN), dotf(fin[:, LANES : LANES + ROW_ONE], s["q"], TN), dotf(s["uv"], s["do"], TN))
        if t > 0:
            out = tuple(a + b for a, b in zip(out, state[i - 1]["out"]))
            state[i - 1].clear()
        s["out"] = out
        if t == parts - 1:
            for unit_step in range(steps):

                @pl.when(step == unit_step)
                def _():
                    at = base + 4 * LANES * (unit_step * step_units + g)
                    out_ref[:, at : at + 2 * LANES] = out[0][ADAPTER_RANK:].astype(out_ref.dtype)
                    out_ref[:, at + 2 * LANES : at + 3 * LANES] = out[1][ROW_K : ROW_K + ADAPTER_RANK].astype(out_ref.dtype)
                    out_ref[:, at + 3 * LANES : at + 4 * LANES] = out[2][ROW_V : ROW_V + ADAPTER_RANK].astype(out_ref.dtype)

    prepare(0)
    for j in columns:
        score(0, j)

    if alone:

        @pl.when(step == 0)
        def _():
            gradient_copy().wait()

        for g in range(step_units):
            weight_copy(step * step_units + g).wait()
    cotangent(0)
    for i in range(len(units) + 1):
        if i < len(units):
            state[i]["top"] = jnp.max(state[i]["peak"], axis=1, keepdims=True)
        if i + 1 < len(units):
            prepare(i + 1)
            cotangent(i + 1)
        for j in columns:
            if i < len(units):
                weigh(i, j)
            if i + 1 < len(units):
                score(i + 1, j)
            if i > 0:
                back(i - 1, j)
        if i < len(units):
            weighed(i)
        if i > 0:
            backed(i - 1)


def attend(queries, gradient, weight, recv, own, packs, ext, table, starts, first, skip, steps, units, before):
    rows, depth = gradient.shape
    tile = rows // 2
    keys = LOOKBACK_SPAN + tile
    base = 0 if before is None else before.shape[1]
    groups = steps * units
    col = lambda width, fn: pl.BlockSpec((rows, width), fn)
    total = base + 4 * LANES * groups
    wide = units * LANES
    alone = own is None
    source = [gradient, weight] if alone else [own]
    operands = [queries, *source, recv, *packs, *packs, ext, table, starts]
    in_specs = (
        [
            col(2 * wide, lambda g, off: (0, g + skip)),
            *([pl.BlockSpec(memory_space=pl.ANY)] * 2 if alone else [col(2 * wide, lambda g, off: (0, g))]),
            col(2 * wide, lambda g, off: (0, g)),
        ]
        + [col(wide, lambda g, off: (0, 2 * g))] * 3
        + [col(wide, lambda g, off: (0, 2 * g + 1))] * 3
        + [
            pl.BlockSpec((3 * rows, LANES), lambda g, off: (0, 0)),
            pl.BlockSpec((TABLE, rows), lambda g, off: (0, 0)),
            pl.BlockSpec((rows, LANES), lambda g, off: (0, 0)),
        ]
    )
    if base:
        operands.append(before)
        in_specs.append(pl.BlockSpec((ADAPTER_RANK, base), lambda g, off: (0, 0)))
    pushes = rows * groups * 2 * keys // 256 * 4
    return pl.pallas_call(
        functools.partial(attend_body, steps, units, base, alone),
        grid_spec=pltpu.PrefetchScalarGridSpec(
            num_scalar_prefetch=1,
            grid=(steps,),
            in_specs=in_specs,
            out_specs=pl.BlockSpec((ADAPTER_RANK, total), lambda g, off: (0, 0)),
            scratch_shapes=[
                pltpu.VMEM((2, 2 * tile, keys), jnp.float32),
                pltpu.VMEM((2, 2 * tile, keys), jnp.bfloat16),
                pltpu.VMEM((2, 3 * rows, 2 * LANES), jnp.bfloat16),
                pltpu.VMEM((2, 3 * rows, 2 * LANES), jnp.bfloat16),
                pltpu.VMEM((2, rows, 2 * LANES), jnp.bfloat16),
            ]
            + alone
            * [
                pltpu.VMEM((rows, depth), jnp.bfloat16),
                pltpu.VMEM((groups, 2 * LANES, depth), jnp.bfloat16),
                pltpu.SemaphoreType.DMA((1 + groups,)),
            ],
        ),
        out_shape=jax.ShapeDtypeStruct((ADAPTER_RANK, total), jnp.bfloat16),
        cost_estimate=pl.CostEstimate(
            flops=pushes * 256 * 256 * 2 + alone * 2 * rows * depth * 2 * LANES * groups,
            bytes_accessed=groups * rows * LANES * 20 + 4 * LANES * groups * depth,
            transcendentals=rows * groups * 2 * keys,
        ),
        compiler_params=pltpu.CompilerParams(vmem_limit_bytes=GRANT),
    )(first, *operands)


def square_body(mine_ref, theirs_ref, out_ref):
    mine = mine_ref[...].astype(jnp.float32) + theirs_ref[...].astype(jnp.float32)
    out_ref[...] = sum(jnp.square(mine[:, at : at + LANES]) for at in range(0, mine.shape[1], LANES))


def union_body(mine_ref, other_ref, there_ref, beyond_ref, out_ref):
    mine = mine_ref[...].astype(jnp.float32) + other_ref[...].astype(jnp.float32)
    theirs = there_ref[...].astype(jnp.float32) + beyond_ref[...].astype(jnp.float32)
    span = mine.shape[1]
    tile = lambda value: sum(jnp.square(value[:, at : at + LANES]) for at in range(0, span, LANES))
    out_ref[:, :span] = mine
    out_ref[:, span:] = tile(mine) + tile(theirs)


def place(mine, total, q_ref, k_ref, v_ref, skip, groups):
    count = float(ADAPTER_RANK * (QUERY_HEADS + 2 * KEY_VALUE_HEADS) * HEAD_SIZE)
    mine = mine * jnp.sqrt(count / (total + 1e-06))
    for g in range(groups):
        at, to = 4 * LANES * g, g + skip
        q_ref[:, 2 * LANES * to : 2 * LANES * (to + 1)] = mine[:, at : at + 2 * LANES]
        k_ref[:, LANES * to : LANES * (to + 1)] = mine[:, at + 2 * LANES : at + 3 * LANES]
        v_ref[:, LANES * to : LANES * (to + 1)] = mine[:, at + 3 * LANES : at + 4 * LANES]


def halves_body(second_ref, mine_ref, other_ref, q_ref, k_ref, v_ref):
    span = mine_ref.shape[1] - LANES
    groups = span // (4 * LANES)
    total = jnp.sum(mine_ref[:, span:] + other_ref[:, span:], keepdims=True)
    second = second_ref[0] == 1
    mine, other = mine_ref[:, :span], other_ref[:, :span]
    place(jnp.where(second, other, mine), total, q_ref, k_ref, v_ref, 0, groups)
    place(jnp.where(second, mine, other), total, q_ref, k_ref, v_ref, groups, groups)


def finish_body(*refs):
    q_ref, k_ref, v_ref = refs[-3:]
    mine = refs[0][...].astype(jnp.float32) + refs[1][...].astype(jnp.float32)
    total = jnp.sum(refs[2][...] + refs[3][...], keepdims=True)
    place(mine, total, q_ref, k_ref, v_ref, 0, k_ref.shape[1] // LANES)


def local(
    layer_input,
    norm_weight,
    document_index,
    stored_queries,
    stored_keys,
    stored_values,
    output_weight,
    projection_gradient,
    adapter_down_maps,
):
    rows = stored_queries.shape[0]
    heads_width = stored_queries.shape[1]
    groups = stored_keys.shape[1] // HEAD_SIZE
    tp, ctx = lax.axis_size("tp"), lax.axis_size("ctx")
    tp_at, ctx_at = lax.axis_index("tp"), lax.axis_index("ctx")
    chunks = 2 if groups % 4 == 0 else 1
    units = chunks
    steps = groups // (chunks * units)
    width = 2 * LANES
    half = heads_width // width
    per = half // chunks
    scalar = lambda value: jnp.asarray(value, jnp.int32).reshape(1)

    packs = [pack_call(stored_keys, stored_values, units * LANES, steps)]

    received = []
    for c in range(chunks):
        got = []
        for d in range(1, tp):
            first = scalar(((tp_at + d) % tp) * half + c * per)
            if c == 0 and d == 1:
                part, low = open_call(
                    projection_gradient,
                    output_weight,
                    first,
                    per,
                    width,
                    layer_input,
                    norm_weight[None, :],
                    adapter_down_maps.T,
                )
            else:
                if d == 1:
                    part, pack = project(
                        projection_gradient,
                        output_weight,
                        first,
                        per,
                        width,
                        stored_keys,
                        stored_values,
                        units * LANES,
                        c * steps,
                    )
                    packs.append(pack)
                else:
                    (part,) = project(projection_gradient, output_weight, first, per, width)
            got.append(lax.ppermute(part, "tp", [(at, (at + d) % tp) for at in range(tp)]))
        total = got[0]
        if len(got) > 1:
            total = sum(one.astype(jnp.float32) for one in got)
        received.append(total)

    move = 1
    while 2 * move < tp:
        low = low + xor_move(low, "tp", move)
        move *= 2
    other = xor_move(low, "tp", move)
    table = pl.pallas_call(
        table_body, out_shape=jax.ShapeDtypeStruct((TABLE, rows), jnp.bfloat16), compiler_params=SMALL
    )(
        low, other, document_index[None, :]
    )
    table2 = shifted(table, "ctx", 2)
    prepare = pl.pallas_call(
        prep_body,
        grid_spec=pltpu.PrefetchScalarGridSpec(
            num_scalar_prefetch=1,
            grid=(1,),
            in_specs=[
                pl.BlockSpec((TABLE, rows), lambda i, off: (0, 0)),
                pl.BlockSpec((TABLE, rows), lambda i, off: (rows // TABLE, 0)),
                pl.BlockSpec((TABLE, rows), lambda i, off: (0, 0)),
            ],
            out_specs=[
                pl.BlockSpec((3 * rows, LANES), lambda i, off: (0, 0)),
                pl.BlockSpec((rows, LANES), lambda i, off: (0, 0)),
            ],
        ),
        out_shape=[
            jax.ShapeDtypeStruct((3 * rows, LANES), jnp.bfloat16),
            jax.ShapeDtypeStruct((rows, LANES), jnp.int32),
        ],
        compiler_params=SMALL,
    )

    second = scalar(ctx_at % 2)
    sums = None
    for c in range(chunks):
        far = shifted(packs[c], "ctx", 2)
        if c == 0:
            picked = pick_call(second, far, packs[c], table2, table)
            near = xor_move(picked, "ctx", 1)
            ext, starts = prepare(scalar(2 * rows - ctx_at * rows), table2, near, table)
        else:
            near = shifted(packs[c], "ctx", 1)
        first = scalar((tp_at * half + c * per) // units)
        sums = attend(
            stored_queries,
            projection_gradient,
            output_weight,
            received[c],
            None,
            (far, near, packs[c]),
            ext,
            table,
            starts,
            first,
            c * steps,
            steps,
            units,
            sums,
        )

    def joined(*parts):
        wide = [part.astype(jnp.float32) for part in parts]
        total = wide[0] + wide[1]
        return total if len(parts) == 2 else total + (wide[2] + wide[3])

    sizes = (heads_width, groups * HEAD_SIZE, groups * HEAD_SIZE)
    results = [jax.ShapeDtypeStruct((ADAPTER_RANK, size), jnp.float32) for size in sizes]
    if chunks == 2 and tp == 2:
        span = sums.shape[1] // 2
        flip = second[0] == 1
        lower, upper = sums[:, :span], sums[:, span:]
        kept = jnp.where(flip, upper, lower)
        mine = joined(kept, xor_move(jnp.where(flip, lower, upper), "ctx", 1)).astype(jnp.bfloat16)
        mine = joined(mine, *[xor_move(mine, "ctx", move) for move in (2, 4, 6)]).astype(jnp.bfloat16)
        move = 8
        while 2 * move < ctx:
            mine = joined(mine, xor_move(mine, "ctx", move)).astype(jnp.bfloat16)
            move *= 2
        both = [(at, at ^ (2 * move + 1)) for at in range(2 * ctx)]
        union = pl.pallas_call(
            union_body,
            out_shape=jax.ShapeDtypeStruct((ADAPTER_RANK, span + LANES), jnp.float32),
            compiler_params=SMALL,
        )(mine, xor_move(mine, "ctx", move), xor_move(mine, "tp", 1), lax.ppermute(mine, ("ctx", "tp"), both))
        return pl.pallas_call(
            halves_body,
            grid_spec=pltpu.PrefetchScalarGridSpec(
                num_scalar_prefetch=1,
                grid=(1,),
                in_specs=[pl.BlockSpec(union.shape, lambda i, sec: (0, 0))] * 2,
                out_specs=[pl.BlockSpec(one.shape, lambda i, sec: (0, 0)) for one in results],
            ),
            out_shape=results,
            compiler_params=SMALL,
        )(second, union, xor_move(union, "ctx", 1))
    sums = joined(sums, xor_move(sums, "ctx", 1)).astype(jnp.bfloat16)
    sums = joined(sums, *[xor_move(sums, "ctx", move) for move in (2, 4, 6)]).astype(jnp.bfloat16)
    move = 8
    while 2 * move < ctx:
        sums = joined(sums, xor_move(sums, "ctx", move)).astype(jnp.bfloat16)
        move *= 2
    last = [sums, xor_move(sums, "ctx", move)]
    squared = pl.pallas_call(
        square_body, out_shape=jax.ShapeDtypeStruct((ADAPTER_RANK, LANES), jnp.float32), compiler_params=SMALL
    )(*last)
    move = 1
    while 2 * move < tp:
        squared = squared + xor_move(squared, "tp", move)
        move *= 2
    last += [squared, xor_move(squared, "tp", move)]
    return pl.pallas_call(
        finish_body,
        out_shape=results,
        compiler_params=SMALL,
    )(*last)


def solution(mesh):
    placed = (
        P("ctx", "tp"),
        P("tp"),
        P("ctx"),
        P("ctx", "tp"),
        P("ctx", "tp"),
        P("ctx", "tp"),
        P(None, "tp"),
        P("ctx", "tp"),
        P("tp", None),
    )
    return jax.shard_map(
        local,
        mesh=mesh,
        in_specs=placed,
        out_specs=(P(None, "tp"), P(None, "tp"), P(None, "tp")),
        check_vma=False,
    )
```

```python
import functools

import jax
import jax.numpy as jnp
from jax import lax
from jax.experimental import pallas as pl
from jax.experimental.pallas import tpu as pltpu
from jax.sharding import PartitionSpec as P


MODEL_WIDTH = 5376
QUERY_HEADS = 32
KEY_VALUE_HEADS = 16
HEAD_SIZE = 128
LOOKBACK_SPAN = 1024
ADAPTER_RANK = 8
LOG2E = 1.4426950408889634
SCALE = float(MODEL_WIDTH // QUERY_HEADS) ** (-0.5)
LANES = 128
GRANT = 52 << 20
SMALL = pltpu.CompilerParams(vmem_limit_bytes=8 << 20)
ROW_K, ROW_V, ROW_ONE, ROW_DOC = 0, ADAPTER_RANK, 2 * ADAPTER_RANK, 2 * ADAPTER_RANK + 1
TABLE = 4 * ADAPTER_RANK

NT = (((1,), (1,)), ((), ()))
NN = (((1,), (0,)), ((), ()))
TN = (((0,), (0,)), ((), ()))


def dotf(left, right, dims):
    return lax.dot_general(left, right, dims, preferred_element_type=jnp.float32)


def shifted(value, axis, steps):
    count = lax.axis_size(axis)
    first, last = (max(0, -steps), min(count, count - steps))
    return lax.ppermute(value, axis, [(source, source + steps) for source in range(first, last)])


def xor_move(value, axis, step):
    return lax.ppermute(value, axis, [(at, at ^ step) for at in range(lax.axis_size(axis))])


def project_body(offset_ref, gradient_ref, weight_ref, *rest):
    if len(rest) > 1:
        k_ref, v_ref, out_ref, pack_ref = rest
        wide = k_ref.shape[1]
        pack_ref[:, :wide] = k_ref[...]
        pack_ref[:, wide:] = v_ref[...]
    else:
        (out_ref,) = rest
    out_ref[...] = dotf(gradient_ref[...], weight_ref[...], NT).astype(out_ref.dtype)


def pack_body(wide, k_ref, v_ref, out_ref):
    for at in range(0, k_ref.shape[1], wide):
        out_ref[:, 2 * at : 2 * at + wide] = k_ref[:, at : at + wide]
        out_ref[:, 2 * at + wide : 2 * at + 2 * wide] = v_ref[:, at : at + wide]


def pack_call(keys, values, wide, blocks):
    rows = keys.shape[0]
    return pl.pallas_call(
        functools.partial(pack_body, wide),
        grid=(blocks,),
        in_specs=[pl.BlockSpec((rows, wide), lambda i: (0, i))] * 2,
        out_specs=pl.BlockSpec((rows, 2 * wide), lambda i: (0, i)),
        out_shape=jax.ShapeDtypeStruct((rows, 2 * wide * blocks), keys.dtype),
        compiler_params=pltpu.CompilerParams(vmem_limit_bytes=62 << 20),
    )(keys, values)


def project(gradient, weight, first_block, blocks, width, keys=None, values=None, wide=0, skip=0):
    rows, depth = gradient.shape
    out_specs = [pl.BlockSpec((rows, width), lambda i, off: (0, i))]
    out_shape = [jax.ShapeDtypeStruct((rows, blocks * width), jnp.bfloat16)]
    in_specs = [
        pl.BlockSpec((rows, depth), lambda i, off: (0, 0)),
        pl.BlockSpec((width, depth), lambda i, off: (off[0] + i, 0)),
    ]
    operands = [gradient, weight]
    if keys is not None:
        operands += [keys, values]
        in_specs += [pl.BlockSpec((rows, wide), lambda i, off: (0, i // 2 + skip))] * 2
        out_specs.append(pl.BlockSpec((rows, 2 * wide), lambda i, off: (0, i // 2)))
        out_shape.append(jax.ShapeDtypeStruct((rows, blocks * wide), keys.dtype))
    return pl.pallas_call(
        project_body,
        grid_spec=pltpu.PrefetchScalarGridSpec(
            num_scalar_prefetch=1, grid=(blocks,), in_specs=in_specs, out_specs=out_specs
        ),
        out_shape=out_shape,
        cost_estimate=pl.CostEstimate(
            flops=2 * rows * depth * width * blocks,
            bytes_accessed=2 * (rows * depth + width * blocks * depth + rows * width * blocks),
            transcendentals=0,
        ),
        compiler_params=pltpu.CompilerParams(vmem_limit_bytes=GRANT),
    )(first_block, *operands)


def open_body(offset_ref, gradient_ref, weight_ref, x_ref, norm_ref, down_ref, out_ref, low_ref, sent_ref):
    out_ref[...] = dotf(gradient_ref[...], weight_ref[...], NT).astype(out_ref.dtype)
    hidden = x_ref[...].astype(jnp.float32)
    weighted = (hidden * norm_ref[...].astype(jnp.float32)).astype(jnp.bfloat16)
    reduced = dotf(weighted, down_ref[...], NT)
    squares = jnp.sum(hidden * hidden, axis=1, keepdims=True)
    squares = jnp.broadcast_to(squares, (squares.shape[0], LANES - 3 * ADAPTER_RANK))
    low = jnp.concatenate([reduced, squares], 1).T[:TABLE]
    low_ref[...] = low
    sent_ref[...] = low.astype(sent_ref.dtype)


def open_call(gradient, weight, first_block, blocks, width, x, norm, down):
    rows, depth = gradient.shape
    slab = rows // blocks
    return pl.pallas_call(
        open_body,
        grid_spec=pltpu.PrefetchScalarGridSpec(
            num_scalar_prefetch=1,
            grid=(blocks,),
            in_specs=[
                pl.BlockSpec((rows, depth), lambda i, off: (0, 0)),
                pl.BlockSpec((width, depth), lambda i, off: (off[0] + i, 0)),
                pl.BlockSpec((slab, depth), lambda i, off: (i, 0)),
                pl.BlockSpec((1, depth), lambda i, off: (0, 0)),
                pl.BlockSpec((3 * ADAPTER_RANK, depth), lambda i, off: (0, 0)),
            ],
            out_specs=[
                pl.BlockSpec((rows, width), lambda i, off: (0, i)),
                pl.BlockSpec((TABLE, slab), lambda i, off: (0, i)),
                pl.BlockSpec((TABLE, slab), lambda i, off: (0, i)),
            ],
        ),
        out_shape=[
            jax.ShapeDtypeStruct((rows, blocks * width), jnp.bfloat16),
            jax.ShapeDtypeStruct((TABLE, rows), jnp.float32),
            jax.ShapeDtypeStruct((TABLE, rows), jnp.bfloat16),
        ],
        cost_estimate=pl.CostEstimate(
            flops=2 * rows * depth * width * blocks,
            bytes_accessed=2 * (2 * rows * depth + width * blocks * depth + rows * width * blocks),
            transcendentals=0,
        ),
        compiler_params=pltpu.CompilerParams(vmem_limit_bytes=GRANT),
    )(first_block, gradient, weight, x, norm, down)


def table_body(mine_ref, theirs_ref, doc_ref, out_ref):
    joined = mine_ref[...] + theirs_ref[...].astype(jnp.float32)
    inverse = lax.rsqrt(joined[3 * ADAPTER_RANK : 3 * ADAPTER_RANK + 1] / float(MODEL_WIDTH) + 1e-06)
    low = joined * inverse
    rank = ADAPTER_RANK
    row = lax.broadcasted_iota(jnp.int32, (rank, low.shape[1]), 0)
    extra = jnp.where(row == 0, 1.0, jnp.where(row == 1, doc_ref[...].astype(jnp.float32), 0.0))
    out_ref[...] = jnp.concatenate([low[rank : 3 * rank], extra, low[:rank]], 0).astype(out_ref.dtype)


def pick_body(second_ref, far_ref, own_ref, there_ref, here_ref, out_ref):
    rows = far_ref.shape[0]

    @pl.when(second_ref[0] == 1)
    def _():
        out_ref[:rows, :] = far_ref[...]
        out_ref[rows:, :] = there_ref[...]

    @pl.when(second_ref[0] != 1)
    def _():
        out_ref[:rows, :] = own_ref[...]
        out_ref[rows:, :] = here_ref[...]


def pick_call(second, far, own, there, here):
    rows, span = own.shape
    width = 2 * LANES
    last = here.shape[1] // width - 1
    side = pl.BlockSpec((TABLE, width), lambda i, sec: (0, jnp.minimum(i, last)))
    return pl.pallas_call(
        pick_body,
        grid_spec=pltpu.PrefetchScalarGridSpec(
            num_scalar_prefetch=1,
            grid=(span // width,),
            in_specs=[
                pl.BlockSpec((rows, width), lambda i, sec: (0, i * sec[0])),
                pl.BlockSpec((rows, width), lambda i, sec: (0, i * (1 - sec[0]))),
                side,
                side,
            ],
            out_specs=pl.BlockSpec((rows + TABLE, width), lambda i, sec: (0, i)),
        ),
        out_shape=jax.ShapeDtypeStruct((rows + TABLE, span), own.dtype),
        compiler_params=pltpu.CompilerParams(vmem_limit_bytes=GRANT),
    )(second, far, own, there, here)


def prep_body(first_ref, t2_ref, t1_ref, t0_ref, ext_ref, st_ref):
    rows = t0_ref.shape[1]
    tables = [ref[...].astype(jnp.float32) for ref in (t2_ref, t1_ref, t0_ref)]
    blank = jnp.zeros((LANES - TABLE, rows), jnp.float32)
    for at, table in enumerate(tables):
        turned = jnp.concatenate([table, blank], 0).T
        ext_ref[at * rows : (at + 1) * rows, :] = turned.astype(ext_ref.dtype)
    ids = [table[ROW_DOC : ROW_DOC + 1] for table in tables]
    column = turned[:, ROW_DOC : ROW_DOC + 1]
    leading = column[0:1]
    before = sum(jnp.sum((one < leading).astype(jnp.float32), axis=1, keepdims=True) for one in ids[:2])
    inside = jnp.sum((ids[2] < column).astype(jnp.float32), axis=1, keepdims=True)
    begin = jnp.where(column > leading, inside + float(2 * rows), before).astype(jnp.int32)
    begin = jnp.broadcast_to(begin, st_ref.shape)
    band = lax.broadcasted_iota(jnp.int32, st_ref.shape, 0) + (2 * rows + 1 - LOOKBACK_SPAN)
    st_ref[...] = jnp.maximum(jnp.maximum(begin, band), first_ref[0])


def attend_body(steps, step_units, base, alone, offset_ref, q_ref, *rest):
    if alone:
        pg_hbm, w_hbm, *rest = rest
    else:
        own_ref, *rest = rest
    recv_ref, k0, k1, k2, v0, v1, v2, ext_ref, lq_ref, st_ref, *rest = rest
    if base:
        before_ref, *rest = rest
    out_ref, s_scr, e_scr, ve, ke, do_scr, *rest = rest
    if alone:
        pg_scr, w_scr, sems = rest
    rows = q_ref.shape[0]
    tile = s_scr.shape[1] // 2
    keys = s_scr.shape[2]
    width = tile
    factor = SCALE * LOG2E
    parts = rows // tile
    units = [(g, t) for g in range(step_units) for t in range(parts)]
    state = [{} for _ in units]
    columns = range(keys // width)
    step = pl.program_id(0)
    deep = 2 * LANES

    def gradient_copy():
        return pltpu.make_async_copy(pg_hbm, pg_scr, sems.at[0])

    def weight_copy(group):
        first = pl.multiple_of((offset_ref[0] * step_units + group) * deep, deep)
        return pltpu.make_async_copy(w_hbm.at[pl.ds(first, deep), :], w_scr.at[group], sems.at[1 + group])

    if alone:

        @pl.when(step == 0)
        def _():
            gradient_copy().start()
            for group in range(steps * step_units):
                weight_copy(group).start()

    if base:

        @pl.when(step == 0)
        def _():
            out_ref[:, :base] = before_ref[...]

    def prepare(i):
        g, t = units[i]
        if t == 0:
            for b, (k_ref, v_ref) in enumerate(((k0, v0), (k1, v1), (k2, v2))):
                span = slice(b * rows, (b + 1) * rows)
                ke[g % 2, span, :LANES] = k_ref[:, g * LANES : (g + 1) * LANES]
                ve[g % 2, span, :LANES] = v_ref[:, g * LANES : (g + 1) * LANES]
                ke[g % 2, span, LANES:] = ext_ref[span, :]
                ve[g % 2, span, LANES:] = ext_ref[span, :]
        s = state[i]
        r0 = t * tile
        c0 = 2 * LANES * g
        s["q"] = jnp.concatenate(
            [q_ref[r0 : r0 + tile, c0 : c0 + LANES], q_ref[r0 : r0 + tile, c0 + LANES : c0 + 2 * LANES]], 0
        )
        start = st_ref[r0 : r0 + tile, :]
        s["start"] = jnp.concatenate([start, start], 0)
        s["peak"] = None

    def cotangent(i):
        g, t = units[i]
        if t == 0:
            if alone:
                own = dotf(pg_scr[...], w_scr[step * step_units + g], NT)
            else:
                own = own_ref[:, deep * g : deep * (g + 1)]
            got = recv_ref[:, deep * g : deep * (g + 1)].astype(jnp.float32)
            do_scr[g % 2] = (own + got).astype(jnp.bfloat16)

    def score(i, j):
        g, t = units[i]
        s = state[i]
        at = t * tile + j * width
        raw = dotf(s["q"], ke[g % 2, at : at + width, :LANES], NT)
        for h in range(width // LANES):
            value = raw[:, h * LANES : (h + 1) * LANES]
            pos = lax.broadcasted_iota(jnp.int32, value.shape, 1) + (at + h * LANES)
            ok = pos >= s["start"]
            if j == len(columns) - 1:
                row = lax.broadcasted_iota(jnp.int32, value.shape, 0)
                row = jnp.where(row >= tile, row - tile, row)
                ok = ok & (pos <= row + (2 * rows + t * tile))
            value = jnp.where(ok, value, -1e30)
            s_scr[i % 2, :, j * width + h * LANES : j * width + (h + 1) * LANES] = value
            s["peak"] = value if s["peak"] is None else jnp.maximum(s["peak"], value)

    def weigh(i, j):
        g, t = units[i]
        s = state[i]
        at = t * tile + j * width
        cols = slice(j * width, (j + 1) * width)
        e = jnp.exp2((s_scr[i % 2, :, cols] - s["top"]) * factor).astype(jnp.bfloat16)
        e_scr[i % 2, :, cols] = e
        part = dotf(e, ve[g % 2, at : at + width, :], NN)
        s["acc"] = part if j == 0 else s["acc"] + part

    def weighed(i):
        g, t = units[i]
        s = state[i]
        acc = s["acc"]
        do = do_scr[g % 2, t * tile : (t + 1) * tile, :]
        s["do"] = jnp.concatenate([do[:, :LANES], do[:, LANES:]], 0)
        s["inverse"] = 1.0 / acc[:, LANES + ROW_ONE : LANES + ROW_ONE + 1]
        s["delta"] = (
            jnp.sum(s["do"].astype(jnp.float32) * acc[:, :LANES], axis=1, keepdims=True) * s["inverse"]
        )
        s["uv"] = (acc[:, LANES : LANES + ROW_ONE] * s["inverse"]).astype(jnp.bfloat16)

    def back(i, j):
        g, t = units[i]
        s = state[i]
        at = t * tile + j * width
        dp = dotf(s["do"], ve[g % 2, at : at + width, :LANES], NT)
        e = e_scr[i % 2, :, j * width : (j + 1) * width].astype(jnp.float32)
        ds = (e * (dp - s["delta"])).astype(jnp.bfloat16)
        part = dotf(ds, ke[g % 2, at : at + width, :], NN)
        s["back"] = part if j == 0 else s["back"] + part

    def backed(i):
        g, t = units[i]
        s = state[i]
        fin = (s["back"] * (s["inverse"] * SCALE)).astype(jnp.bfloat16)
        dq = jnp.concatenate([fin[:tile, :LANES], fin[tile:, :LANES]], 1)
        low_q = lq_ref[2 * ADAPTER_RANK :, t * tile : (t + 1) * tile]
        out = (dotf(low_q, dq, NN), dotf(fin[:, LANES : LANES + ROW_ONE], s["q"], TN), dotf(s["uv"], s["do"], TN))
        if t > 0:
            out = tuple(a + b for a, b in zip(out, state[i - 1]["out"]))
            state[i - 1].clear()
        s["out"] = out
        if t == parts - 1:
            for unit_step in range(steps):

                @pl.when(step == unit_step)
                def _():
                    at = base + 4 * LANES * (unit_step * step_units + g)
                    out_ref[:, at : at + 2 * LANES] = out[0][ADAPTER_RANK:].astype(out_ref.dtype)
                    out_ref[:, at + 2 * LANES : at + 3 * LANES] = out[1][ROW_K : ROW_K + ADAPTER_RANK].astype(out_ref.dtype)
                    out_ref[:, at + 3 * LANES : at + 4 * LANES] = out[2][ROW_V : ROW_V + ADAPTER_RANK].astype(out_ref.dtype)

    prepare(0)
    for j in columns:
        score(0, j)

    if alone:

        @pl.when(step == 0)
        def _():
            gradient_copy().wait()

        for g in range(step_units):
            weight_copy(step * step_units + g).wait()
    cotangent(0)
    for i in range(len(units) + 1):
        if i < len(units):
            state[i]["top"] = jnp.max(state[i]["peak"], axis=1, keepdims=True)
        if i + 1 < len(units):
            prepare(i + 1)
            cotangent(i + 1)
        for j in columns:
            if i < len(units):
                weigh(i, j)
            if i + 1 < len(units):
                score(i + 1, j)
            if i > 0:
                back(i - 1, j)
        if i < len(units):
            weighed(i)
        if i > 0:
            backed(i - 1)


def attend(queries, gradient, weight, recv, own, packs, ext, table, starts, first, skip, steps, units, before):
    rows, depth = gradient.shape
    tile = rows // 2
    keys = LOOKBACK_SPAN + tile
    base = 0 if before is None else before.shape[1]
    groups = steps * units
    col = lambda width, fn: pl.BlockSpec((rows, width), fn)
    total = base + 4 * LANES * groups
    wide = units * LANES
    alone = own is None
    source = [gradient, weight] if alone else [own]
    operands = [queries, *source, recv, *packs, *packs, ext, table, starts]
    in_specs = (
        [
            col(2 * wide, lambda g, off: (0, g + skip)),
            *([pl.BlockSpec(memory_space=pl.ANY)] * 2 if alone else [col(2 * wide, lambda g, off: (0, g))]),
            col(2 * wide, lambda g, off: (0, g)),
        ]
        + [col(wide, lambda g, off: (0, 2 * g))] * 3
        + [col(wide, lambda g, off: (0, 2 * g + 1))] * 3
        + [
            pl.BlockSpec((3 * rows, LANES), lambda g, off: (0, 0)),
            pl.BlockSpec((TABLE, rows), lambda g, off: (0, 0)),
            pl.BlockSpec((rows, LANES), lambda g, off: (0, 0)),
        ]
    )
    if base:
        operands.append(before)
        in_specs.append(pl.BlockSpec((ADAPTER_RANK, base), lambda g, off: (0, 0)))
    pushes = rows * groups * 2 * keys // 256 * 4
    return pl.pallas_call(
        functools.partial(attend_body, steps, units, base, alone),
        grid_spec=pltpu.PrefetchScalarGridSpec(
            num_scalar_prefetch=1,
            grid=(steps,),
            in_specs=in_specs,
            out_specs=pl.BlockSpec((ADAPTER_RANK, total), lambda g, off: (0, 0)),
            scratch_shapes=[
                pltpu.VMEM((2, 2 * tile, keys), jnp.float32),
                pltpu.VMEM((2, 2 * tile, keys), jnp.bfloat16),
                pltpu.VMEM((2, 3 * rows, 2 * LANES), jnp.bfloat16),
                pltpu.VMEM((2, 3 * rows, 2 * LANES), jnp.bfloat16),
                pltpu.VMEM((2, rows, 2 * LANES), jnp.bfloat16),
            ]
            + alone
            * [
                pltpu.VMEM((rows, depth), jnp.bfloat16),
                pltpu.VMEM((groups, 2 * LANES, depth), jnp.bfloat16),
                pltpu.SemaphoreType.DMA((1 + groups,)),
            ],
        ),
        out_shape=jax.ShapeDtypeStruct((ADAPTER_RANK, total), jnp.bfloat16),
        cost_estimate=pl.CostEstimate(
            flops=pushes * 256 * 256 * 2 + alone * 2 * rows * depth * 2 * LANES * groups,
            bytes_accessed=groups * rows * LANES * 20 + 4 * LANES * groups * depth,
            transcendentals=rows * groups * 2 * keys,
        ),
        compiler_params=pltpu.CompilerParams(vmem_limit_bytes=GRANT),
    )(first, *operands)


def square_body(mine_ref, theirs_ref, out_ref):
    mine = mine_ref[...].astype(jnp.float32) + theirs_ref[...].astype(jnp.float32)
    out_ref[...] = sum(jnp.square(mine[:, at : at + LANES]) for at in range(0, mine.shape[1], LANES))


def finish_body(*refs):
    q_ref, k_ref, v_ref = refs[-3:]
    mine = refs[0][...].astype(jnp.float32) + refs[1][...].astype(jnp.float32)
    total = jnp.sum(refs[2][...] + refs[3][...], keepdims=True)
    count = float(ADAPTER_RANK * (QUERY_HEADS + 2 * KEY_VALUE_HEADS) * HEAD_SIZE)
    mine = mine * jnp.sqrt(count / (total + 1e-06))
    for g in range(k_ref.shape[1] // LANES):
        at = 4 * LANES * g
        q_ref[:, 2 * LANES * g : 2 * LANES * (g + 1)] = mine[:, at : at + 2 * LANES]
        k_ref[:, LANES * g : LANES * (g + 1)] = mine[:, at + 2 * LANES : at + 3 * LANES]
        v_ref[:, LANES * g : LANES * (g + 1)] = mine[:, at + 3 * LANES : at + 4 * LANES]


def local(
    layer_input,
    norm_weight,
    document_index,
    stored_queries,
    stored_keys,
    stored_values,
    output_weight,
    projection_gradient,
    adapter_down_maps,
):
    rows = stored_queries.shape[0]
    heads_width = stored_queries.shape[1]
    groups = stored_keys.shape[1] // HEAD_SIZE
    tp, ctx = lax.axis_size("tp"), lax.axis_size("ctx")
    tp_at, ctx_at = lax.axis_index("tp"), lax.axis_index("ctx")
    chunks = 2 if groups % 4 == 0 else 1
    units = chunks
    steps = groups // (chunks * units)
    width = 2 * LANES
    half = heads_width // width
    per = half // chunks
    scalar = lambda value: jnp.asarray(value, jnp.int32).reshape(1)

    packs = [pack_call(stored_keys, stored_values, units * LANES, steps)]

    received = []
    for c in range(chunks):
        got = []
        for d in range(1, tp):
            first = scalar(((tp_at + d) % tp) * half + c * per)
            if c == 0 and d == 1:
                part, low, sent = open_call(
                    projection_gradient,
                    output_weight,
                    first,
                    per,
                    width,
                    layer_input,
                    norm_weight[None, :],
                    adapter_down_maps.T,
                )
            else:
                if d == 1:
                    part, pack = project(
                        projection_gradient,
                        output_weight,
                        first,
                        per,
                        width,
                        stored_keys,
                        stored_values,
                        units * LANES,
                        c * steps,
                    )
                    packs.append(pack)
                else:
                    (part,) = project(projection_gradient, output_weight, first, per, width)
            got.append(lax.ppermute(part, "tp", [(at, (at + d) % tp) for at in range(tp)]))
        total = got[0]
        if len(got) > 1:
            total = sum(one.astype(jnp.float32) for one in got)
        received.append(total)

    move = 1
    while 2 * move < tp:
        low = low + xor_move(low, "tp", move)
        sent = low.astype(jnp.bfloat16)
        move *= 2
    other = xor_move(sent, "tp", move)
    table = pl.pallas_call(
        table_body, out_shape=jax.ShapeDtypeStruct((TABLE, rows), jnp.bfloat16), compiler_params=SMALL
    )(
        low, other, document_index[None, :]
    )
    table2 = shifted(table, "ctx", 2)
    prepare = pl.pallas_call(
        prep_body,
        grid_spec=pltpu.PrefetchScalarGridSpec(
            num_scalar_prefetch=1,
            grid=(1,),
            in_specs=[
                pl.BlockSpec((TABLE, rows), lambda i, off: (0, 0)),
                pl.BlockSpec((TABLE, rows), lambda i, off: (rows // TABLE, 0)),
                pl.BlockSpec((TABLE, rows), lambda i, off: (0, 0)),
            ],
            out_specs=[
                pl.BlockSpec((3 * rows, LANES), lambda i, off: (0, 0)),
                pl.BlockSpec((rows, LANES), lambda i, off: (0, 0)),
            ],
        ),
        out_shape=[
            jax.ShapeDtypeStruct((3 * rows, LANES), jnp.bfloat16),
            jax.ShapeDtypeStruct((rows, LANES), jnp.int32),
        ],
        compiler_params=SMALL,
    )

    second = scalar(ctx_at % 2)
    sums = None
    for c in range(chunks):
        far = shifted(packs[c], "ctx", 2)
        if c == 0:
            picked = pick_call(second, far, packs[c], table2, table)
            near = xor_move(picked, "ctx", 1)
            ext, starts = prepare(scalar(2 * rows - ctx_at * rows), table2, near, table)
        else:
            near = shifted(packs[c], "ctx", 1)
        first = scalar((tp_at * half + c * per) // units)
        sums = attend(
            stored_queries,
            projection_gradient,
            output_weight,
            received[c],
            None,
            (far, near, packs[c]),
            ext,
            table,
            starts,
            first,
            c * steps,
            steps,
            units,
            sums,
        )

    def joined(*parts):
        wide = [part.astype(jnp.float32) for part in parts]
        total = wide[0] + wide[1]
        return total if len(parts) == 2 else total + (wide[2] + wide[3])

    sums = joined(sums, xor_move(sums, "ctx", 1)).astype(jnp.bfloat16)
    sums = joined(sums, *[xor_move(sums, "ctx", move) for move in (2, 4, 6)]).astype(jnp.bfloat16)
    move = 8
    while 2 * move < ctx:
        sums = joined(sums, xor_move(sums, "ctx", move)).astype(jnp.bfloat16)
        move *= 2
    last = [sums, xor_move(sums, "ctx", move)]
    squared = pl.pallas_call(
        square_body, out_shape=jax.ShapeDtypeStruct((ADAPTER_RANK, LANES), jnp.float32), compiler_params=SMALL
    )(*last)
    move = 1
    while 2 * move < tp:
        squared = squared + xor_move(squared, "tp", move)
        move *= 2
    last += [squared, xor_move(squared, "tp", move)]
    sizes = (heads_width, groups * HEAD_SIZE, groups * HEAD_SIZE)
    return pl.pallas_call(
        finish_body,
        out_shape=[jax.ShapeDtypeStruct((ADAPTER_RANK, size), jnp.float32) for size in sizes],
        compiler_params=SMALL,
    )(*last)


def solution(mesh):
    placed = (
        P("ctx", "tp"),
        P("tp"),
        P("ctx"),
        P("ctx", "tp"),
        P("ctx", "tp"),
        P("ctx", "tp"),
        P(None, "tp"),
        P("ctx", "tp"),
        P("tp", None),
    )
    return jax.shard_map(
        local,
        mesh=mesh,
        in_specs=placed,
        out_specs=(P(None, "tp"), P(None, "tp"), P(None, "tp")),
        check_vma=False,
    )
```
